512 devices in a mesh: dp: 64 (over z, x, core), class: 8 (over y).
Axes of the slice: x: 4, y: 8, z: 8, core: 2. Of those that a mesh axis runs over, the one named last changes fastest.
Arguments:
- embeddings: bfloat16 [16384, 1024], P('dp', 'class'), may hold values from -28 to 28, as said below
- labels: bfloat16 [16384, 4096], P('dp', 'class'), may hold values from -55 to 55
- head_weight: bfloat16 [1024, 4096], P(None, 'class'), may hold values from -0.1875 to 0.1875
- send_blocks: int32 [64, 64], P('dp'), may hold values from 0 to 1
- nbr_source: int32 [16384, 32], P('dp'), may hold values from 0 to 63
- nbr_offset: int32 [16384, 32], P('dp'), may hold values from 0 to 127
- counts: int32 [16384], P('dp'), may hold values from 1 to 32
Outputs:
- target_logits: bfloat16 [16384, 4096], P('dp', 'class')
- head_grad: bfloat16 [1024, 4096], P(None, 'class')
The draws below stay inside these ranges and needn't reach their ends.
Inputs may be any that keep to these rules, and one draw needn't show every extreme that they name: Each image of the embeddings has entries within the range. `send_blocks`: entry [p, q] names which of dp index p's own 2 blocks dp index q receives from p. The neighbour lies in the block that this dp index receives from dp index nbr_source. Only the first counts[r] neighbours of image r are used.
All inputs are finite; a program needn't handle non-finite values.
Results may differ from the reference program's by a relative error of at most 0.0062.
Values may be sent and summed in bfloat16 or wider, within the bound.
A program may use at most 64 MiB of HBM per device.

```python
import math
import jax
import jax.numpy as jnp
from jax import lax

D = 1024
C = 4096
K = 32
BLOCK = 128
BLK_DEV = 2
ROWS_DEV = 256
ROWS_ALL = 16384
N_DP = 64


def draw_embeddings(key, part):
    first = jax.random.fold_in(key, 0)
    return jnp.clip(jax.random.normal(first, (ROWS_ALL, D), jnp.float32), -6.0, 6.0).astype(jnp.bfloat16)


def draw_labels(key, part):
    first = jax.random.fold_in(jax.random.fold_in(key, 7), 0)
    return jnp.clip(jax.random.normal(first, (ROWS_ALL, C), jnp.float32), -6.0, 6.0).astype(jnp.bfloat16)


def draw_head_weight(key, part):
    first = jax.random.fold_in(jax.random.fold_in(key, 11), 0)
    base = jnp.clip(jax.random.normal(first, (D, C), jnp.float32), -6.0, 6.0)
    return (base / math.sqrt(D)).astype(jnp.bfloat16)


def with_ends(values, rng, least, high):
    shape = values.shape
    spot = [jax.random.randint(jax.random.fold_in(rng, axis), (), 0, shape[axis]) for axis in range(len(shape))]
    values = values.at[tuple(spot)].set(least)
    longest = shape.index(max(shape))
    spot[longest] = (spot[longest] + 1) % shape[longest]
    return values.at[tuple(spot)].set(high)


def setup_inputs(seed: int = 0) -> dict:
    arg_keys = jax.random.split(jax.random.key(seed), 8)
    embeddings = draw_embeddings(jax.random.fold_in(arg_keys[7], 71), 0)
    labels = draw_labels(jax.random.fold_in(arg_keys[7], 71), 0)
    head_weight = draw_head_weight(jax.random.fold_in(arg_keys[7], 71), 0)
    send_blocks = with_ends(jax.random.randint(arg_keys[3], (N_DP, N_DP), 0, BLK_DEV), jax.random.fold_in(arg_keys[3], 1), 0, BLK_DEV - 1).astype(jnp.int32)
    nbr_source = with_ends(jax.random.randint(arg_keys[4], (ROWS_ALL, K), 0, N_DP), jax.random.fold_in(arg_keys[4], 1), 0, N_DP - 1).astype(jnp.int32)
    nbr_offset = with_ends(jax.random.randint(arg_keys[5], (ROWS_ALL, K), 0, BLOCK), jax.random.fold_in(arg_keys[5], 1), 0, BLOCK - 1).astype(jnp.int32)
    counts = with_ends(jax.random.randint(arg_keys[6], (ROWS_ALL,), 1, K + 1), jax.random.fold_in(arg_keys[6], 1), 1, K).astype(jnp.int32)
    return dict(embeddings=embeddings, labels=labels, head_weight=head_weight, send_blocks=send_blocks, nbr_source=nbr_source, nbr_offset=nbr_offset, counts=counts)


def reference(embeddings, labels, head_weight, send_blocks, nbr_source, nbr_offset, counts):
    rows_all = embeddings.shape[0]
    owner = jnp.arange(rows_all, dtype=jnp.int32) // ROWS_DEV
    chosen = send_blocks[nbr_source, owner[:, None]]
    glob = ((BLK_DEV * nbr_source + chosen) * BLOCK + nbr_offset).astype(jnp.int32)
    valid = jnp.arange(K, dtype=jnp.int32)[None, :] < counts[:, None]
    step_rows = min(256, ROWS_DEV)
    count_steps = rows_all // step_rows

    def one(total, args):
        emb_blk, lab_blk, glob_blk, valid_blk = args
        near = embeddings[glob_blk].astype(jnp.float32)
        dots = jnp.einsum('rd,rkd->rk', emb_blk.astype(jnp.float32), near, precision=lax.Precision.HIGHEST)
        logits = jnp.where(valid_blk, dots / math.sqrt(D), -1e+30)
        top = lax.optimization_barrier(jnp.max(logits, axis=1, keepdims=True))
        expd = jnp.where(valid_blk, jnp.exp(logits - top), 0.0)
        weights = (expd / lax.optimization_barrier(jnp.sum(expd, axis=1, keepdims=True))).astype(jnp.bfloat16)
        near_lab = labels[glob_blk].astype(jnp.float32)
        target = 4.0 * jnp.einsum('rk,rkc->rc', weights.astype(jnp.float32), near_lab, precision=lax.Precision.HIGHEST) + lab_blk.astype(jnp.float32)
        prob_target = jax.nn.softmax(target, axis=-1)
        head = jnp.dot(emb_blk, head_weight, preferred_element_type=jnp.float32)
        prob_head = jax.nn.softmax(head, axis=-1)
        diff = (C * (prob_head - prob_target)).astype(jnp.bfloat16)
        total = total + jnp.dot(emb_blk.T, diff, preferred_element_type=jnp.float32)
        return (total, target.astype(jnp.bfloat16))
    total, targets = lax.scan(one, jnp.zeros((D, C), jnp.float32), (embeddings.reshape(count_steps, step_rows, D), labels.reshape(count_steps, step_rows, C), glob.reshape(count_steps, step_rows, K), valid.reshape(count_steps, step_rows, K)))
    raw = total / math.sqrt(rows_all)
    norm = jnp.sqrt(jnp.sum(raw * raw))
    factor = jnp.minimum(1.0, 0.5 * math.sqrt(D * C) / norm)
    return (targets.reshape(rows_all, C), (raw * factor).astype(jnp.bfloat16))
```

```python
import math

import jax
import jax.numpy as jnp
from jax import lax
from jax.sharding import PartitionSpec as P

D = 1024
C = 4096
BLOCK = 128


def _combine_stats(local_max, local_sum):
    both = lax.all_gather(jnp.stack([local_max, local_sum], axis=0), "class", axis=0)
    maxes, sums = both[:, 0], both[:, 1]
    top = jnp.max(maxes, axis=0)
    total = jnp.sum(sums * jnp.exp(maxes - top[None, :]), axis=0)
    return top, total


def on_device(embeddings, labels, head_weight, send_blocks, nbr_source, nbr_offset, counts):
    rows = embeddings.shape[0]
    width_part = embeddings.shape[1]
    class_part = labels.shape[1]
    dp_count = lax.axis_size("dp")
    nbrs = nbr_source.shape[1]
    picks = send_blocks[0]
    out_emb = embeddings.reshape(rows // BLOCK, BLOCK, width_part)[picks]
    out_lab = labels.reshape(rows // BLOCK, BLOCK, class_part)[picks]
    pool_emb = lax.all_to_all(out_emb, "dp", split_axis=0, concat_axis=0, tiled=True)
    pool_lab = lax.all_to_all(out_lab, "dp", split_axis=0, concat_axis=0, tiled=True)
    pool_rows = dp_count * BLOCK
    pool_emb = pool_emb.reshape(pool_rows, width_part)
    pool_lab = pool_lab.reshape(pool_rows, class_part)
    located = nbr_source * BLOCK + nbr_offset

    full_emb = lax.all_gather(embeddings, "class", axis=1, tiled=True)
    head = jnp.dot(full_emb, head_weight, preferred_element_type=jnp.float32)
    h_top, h_total = _combine_stats(
        jnp.max(head, axis=1),
        jnp.sum(jnp.exp(head - jnp.max(head, axis=1, keepdims=True)), axis=1),
    )
    prob_head = jnp.exp(head - h_top[:, None]) / h_total[:, None]

    near = pool_emb[located]
    partial_value = jnp.einsum(
        "rd,rkd->rk", embeddings, near, preferred_element_type=jnp.float32
    )
    scores = lax.psum(partial_value, "class")
    valid = lax.broadcasted_iota(jnp.int32, (rows, nbrs), 1) < counts[:, None]
    logits = jnp.where(valid, scores / math.sqrt(D), -1e30)
    top = jnp.max(logits, axis=1, keepdims=True)
    expd = jnp.where(valid, jnp.exp(logits - top), 0.0)
    weights = (expd / jnp.sum(expd, axis=1, keepdims=True)).astype(jnp.bfloat16)

    row_ids = lax.broadcasted_iota(jnp.int32, (rows, nbrs), 0)
    dense = jnp.zeros((rows, pool_rows), jnp.float32).at[row_ids, located].add(
        weights.astype(jnp.float32)
    )
    dense_hi = dense.astype(jnp.bfloat16)
    dense_lo = (dense - dense_hi.astype(jnp.float32)).astype(jnp.bfloat16)
    spread = jnp.dot(dense_hi, pool_lab, preferred_element_type=jnp.float32) + jnp.dot(
        dense_lo, pool_lab, preferred_element_type=jnp.float32
    )
    target = 4.0 * spread + labels.astype(jnp.float32)
    z_local = jnp.max(target, axis=1)
    z_top, z_total = _combine_stats(
        z_local, jnp.sum(jnp.exp(target - z_local[:, None]), axis=1)
    )
    prob_target = jnp.exp(target - z_top[:, None]) / z_total[:, None]
    diff = (C * (prob_head - prob_target)).astype(jnp.bfloat16)
    part_grad = lax.dot_general(
        full_emb, diff, (((0,), (0,)), ((), ())), preferred_element_type=jnp.float32
    )
    scale = 1.0 / math.sqrt(rows * dp_count)
    limit = 0.5 * math.sqrt(D * C)
    summed = lax.psum_scatter(part_grad, "dp", scatter_dimension=0, tiled=True) * scale
    squared = lax.psum(jnp.sum(summed * summed), ("dp", "class"))
    factor = jnp.minimum(1.0, limit / jnp.sqrt(squared))
    head_grad = lax.all_gather((summed * factor).astype(jnp.bfloat16), "dp", axis=0, tiled=True)
    return (target.astype(jnp.bfloat16), head_grad)


def solution(mesh):
    return jax.shard_map(
        on_device,
        mesh=mesh,
        in_specs=(
            P("dp", "class"),
            P("dp", "class"),
            P(None, "class"),
            P("dp", None),
            P("dp", None),
            P("dp", None),
            P("dp"),
        ),
        out_specs=(P("dp", "class"), P(None, "class")),
        check_vma=False,
    )
```

```python
import math

import jax
import jax.numpy as jnp
from jax import lax
from jax.experimental import pallas as pl
from jax.experimental.pallas import tpu as pltpu
from jax.sharding import PartitionSpec as P
import functools

D = 1024
C = 4096
BLOCK = 128

MESH = pl.DeviceIdType.MESH

def _grad_kernel(n, ncls, scale, limit, part_ref, out_ref, recv, gath, nrm_dp, nrm_cls,
                 send_a, recv_a, send_b, recv_b, send_c, recv_c, send_d, recv_d):
    me = lax.axis_index("dp")
    cj = lax.axis_index("class")
    rows = part_ref.shape[0] // n

    def peer(d):
        return lax.rem(me + d, n)

    barrier = pltpu.get_barrier_semaphore()

    def greet(d, c):
        pl.semaphore_signal(barrier, 1, device_id=(peer(d), cj), device_id_type=MESH)
        return c
    lax.fori_loop(1, n, greet, 0)
    for e in range(1, ncls):
        pl.semaphore_signal(barrier, 1, device_id=(me, lax.rem(cj + e, ncls)), device_id_type=MESH)
    pl.semaphore_wait(barrier, n - 1 + ncls - 1)

    def slot(i):
        return pl.ds(pl.multiple_of(i * rows, rows), rows)

    def rs_desc(t, s):
        return pltpu.make_async_remote_copy(
            src_ref=part_ref.at[slot(t)], dst_ref=recv.at[slot(s)],
            send_sem=send_a.at[t], recv_sem=recv_a.at[s],
            device_id=(t, cj), device_id_type=MESH)

    def rs_start(d, c):
        rs_desc(peer(d), me).start()
        return c
    lax.fori_loop(1, n, rs_start, 0)

    def rs_wait(d, c):
        rs_desc(peer(d), me).wait_send()
        rs_desc(me, peer(d)).wait_recv()
        return c
    lax.fori_loop(1, n, rs_wait, 0)

    def add(d, acc):
        return acc + recv[slot(peer(d)), :]
    acc = lax.fori_loop(1, n, add, part_ref[slot(me), :])
    summed = acc * scale
    sq = jnp.sum(summed * summed, axis=(0, 1), keepdims=True)
    nrm_dp[me] = jnp.broadcast_to(sq, nrm_dp.shape[1:])

    def b_desc(t, s):
        return pltpu.make_async_remote_copy(
            src_ref=nrm_dp.at[s], dst_ref=nrm_dp.at[s],
            send_sem=send_b.at[t], recv_sem=recv_b.at[s],
            device_id=(t, cj), device_id_type=MESH)

    def b_start(d, c):
        b_desc(peer(d), me).start()
        return c
    lax.fori_loop(1, n, b_start, 0)

    def b_wait(d, c):
        b_desc(peer(d), me).wait_send()
        b_desc(me, peer(d)).wait_recv()
        return c
    lax.fori_loop(1, n, b_wait, 0)

    def b_add(d, acc):
        return acc + nrm_dp[peer(d)]
    col = lax.fori_loop(1, n, b_add, nrm_dp[me])
    nrm_cls[cj] = col

    def c_desc(t, s):
        return pltpu.make_async_remote_copy(
            src_ref=nrm_cls.at[s], dst_ref=nrm_cls.at[s],
            send_sem=send_c.at[t], recv_sem=recv_c.at[s],
            device_id=(me, t), device_id_type=MESH)

    for e in range(1, ncls):
        c_desc(lax.rem(cj + e, ncls), cj).start()
    for e in range(1, ncls):
        c_desc(lax.rem(cj + e, ncls), cj).wait_send()
        c_desc(cj, lax.rem(cj + e, ncls)).wait_recv()
    tot = col
    for e in range(1, ncls):
        tot = tot + nrm_cls[lax.rem(cj + e, ncls)]
    factor = jnp.minimum(1.0, limit / jnp.sqrt(tot))
    fac = jnp.broadcast_to(factor[0:1, 0:1], summed.shape)
    gath[slot(me), :] = (summed * fac).astype(gath.dtype)

    def d_desc(t, s):
        return pltpu.make_async_remote_copy(
            src_ref=gath.at[slot(s)], dst_ref=gath.at[slot(s)],
            send_sem=send_d.at[t], recv_sem=recv_d.at[s],
            device_id=(t, cj), device_id_type=MESH)

    def d_start(d, c):
        d_desc(peer(d), me).start()
        return c
    lax.fori_loop(1, n, d_start, 0)

    def d_wait(d, c):
        d_desc(peer(d), me).wait_send()
        d_desc(me, peer(d)).wait_recv()
        return c
    lax.fori_loop(1, n, d_wait, 0)
    out_ref[...] = gath[...]


def grad_reduce(part_grad, n, ncls, scale, limit):
    width = part_grad.shape[1]
    total_rows = part_grad.shape[0]
    return pl.pallas_call(
        functools.partial(_grad_kernel, n, ncls, scale, limit),
        out_shape=jax.ShapeDtypeStruct((total_rows, width), jnp.bfloat16),
        in_specs=[pl.BlockSpec(memory_space=pltpu.VMEM)],
        out_specs=pl.BlockSpec(memory_space=pltpu.VMEM),
        scratch_shapes=[
            pltpu.VMEM((total_rows, width), jnp.float32),
            pltpu.VMEM((total_rows, width), jnp.bfloat16),
            pltpu.VMEM((n, 8, 128), jnp.float32),
            pltpu.VMEM((ncls, 8, 128), jnp.float32),
            pltpu.SemaphoreType.DMA((n,)), pltpu.SemaphoreType.DMA((n,)),
            pltpu.SemaphoreType.DMA((n,)), pltpu.SemaphoreType.DMA((n,)),
            pltpu.SemaphoreType.DMA((ncls,)), pltpu.SemaphoreType.DMA((ncls,)),
            pltpu.SemaphoreType.DMA((n,)), pltpu.SemaphoreType.DMA((n,)),
        ],
        compiler_params=pltpu.CompilerParams(collective_id=0, has_side_effects=True),
    )(part_grad)


def _combine_stats(local_max, local_sum):
    both = lax.all_gather(jnp.stack([local_max, local_sum], axis=0), "class", axis=0)
    maxes, sums = both[:, 0], both[:, 1]
    top = jnp.max(maxes, axis=0)
    total = jnp.sum(sums * jnp.exp(maxes - top[None, :]), axis=0)
    return top, total


def on_device(embeddings, labels, head_weight, send_blocks, nbr_source, nbr_offset, counts):
    rows = embeddings.shape[0]
    width_part = embeddings.shape[1]
    class_part = labels.shape[1]
    dp_count = lax.axis_size("dp")
    nbrs = nbr_source.shape[1]
    picks = send_blocks[0]
    out_emb = embeddings.reshape(rows // BLOCK, BLOCK, width_part)[picks]
    out_lab = labels.reshape(rows // BLOCK, BLOCK, class_part)[picks]
    pool_emb = lax.all_to_all(out_emb, "dp", split_axis=0, concat_axis=0, tiled=True)
    pool_lab = lax.all_to_all(out_lab, "dp", split_axis=0, concat_axis=0, tiled=True)
    pool_rows = dp_count * BLOCK
    pool_emb = pool_emb.reshape(pool_rows, width_part)
    pool_lab = pool_lab.reshape(pool_rows, class_part)
    located = nbr_source * BLOCK + nbr_offset

    full_emb = lax.all_gather(embeddings, "class", axis=1, tiled=True)
    head = jnp.dot(full_emb, head_weight, preferred_element_type=jnp.float32)
    h_top, h_total = _combine_stats(
        jnp.max(head, axis=1),
        jnp.sum(jnp.exp(head - jnp.max(head, axis=1, keepdims=True)), axis=1),
    )
    prob_head = jnp.exp(head - h_top[:, None]) / h_total[:, None]

    near = pool_emb[located]
    partial_value = jnp.einsum(
        "rd,rkd->rk", embeddings, near, preferred_element_type=jnp.float32
    )
    scores = lax.psum(partial_value, "class")
    valid = lax.broadcasted_iota(jnp.int32, (rows, nbrs), 1) < counts[:, None]
    logits = jnp.where(valid, scores / math.sqrt(D), -1e30)
    top = jnp.max(logits, axis=1, keepdims=True)
    expd = jnp.where(valid, jnp.exp(logits - top), 0.0)
    weights = (expd / jnp.sum(expd, axis=1, keepdims=True)).astype(jnp.bfloat16)

    row_ids = lax.broadcasted_iota(jnp.int32, (rows, nbrs), 0)
    dense = jnp.zeros((rows, pool_rows), jnp.float32).at[row_ids, located].add(
        weights.astype(jnp.float32)
    )
    dense_hi = dense.astype(jnp.bfloat16)
    dense_lo = (dense - dense_hi.astype(jnp.float32)).astype(jnp.bfloat16)
    spread = jnp.dot(dense_hi, pool_lab, preferred_element_type=jnp.float32) + jnp.dot(
        dense_lo, pool_lab, preferred_element_type=jnp.float32
    )
    target = 4.0 * spread + labels.astype(jnp.float32)
    z_local = jnp.max(target, axis=1)
    z_top, z_total = _combine_stats(
        z_local, jnp.sum(jnp.exp(target - z_local[:, None]), axis=1)
    )
    prob_target = jnp.exp(target - z_top[:, None]) / z_total[:, None]
    diff = (C * (prob_head - prob_target)).astype(jnp.bfloat16)
    part_grad = lax.dot_general(
        full_emb, diff, (((0,), (0,)), ((), ())), preferred_element_type=jnp.float32
    )
    scale = 1.0 / math.sqrt(rows * dp_count)
    limit = 0.5 * math.sqrt(D * C)
    head_grad = grad_reduce(part_grad, dp_count, lax.axis_size("class"), scale, limit)
    return (target.astype(jnp.bfloat16), head_grad)


def solution(mesh):
    return jax.shard_map(
        on_device,
        mesh=mesh,
        in_specs=(
            P("dp", "class"),
            P("dp", "class"),
            P(None, "class"),
            P("dp", None),
            P("dp", None),
            P("dp", None),
            P("dp"),
        ),
        out_specs=(P("dp", "class"), P(None, "class")),
        check_vma=False,
    )
```

```python
import math

import jax
import jax.numpy as jnp
from jax import lax
from jax.experimental import pallas as pl
from jax.experimental.pallas import tpu as pltpu
from jax.sharding import PartitionSpec as P
import functools

D = 1024
C = 4096
BLOCK = 128

MESH = pl.DeviceIdType.MESH

def _grad_kernel(nk, nx, nz, ncls, scale, limit, part_ref, out_ref,
                 recv1, acc1, recv2, acc2, recv3, gath, nrm_dp, nrm_cls,
                 s1, r1, s2, r2, s3, r3, sb, rb, sc, rc, g3s, g3r, g2s, g2r, g1s, g1r):
    n = nk * nx * nz
    me = lax.axis_index("dp")
    cj = lax.axis_index("class")
    kc = lax.rem(me, nk)
    xc = lax.rem(me // nk, nx)
    zc = me // (nk * nx)
    total = part_ref.shape[0]
    half = total // nk
    quarter = half // nx
    piece = quarter // nz

    def dev(z, x, k):
        return ((z * nx + x) * nk + k, cj)

    def rows(start, size):
        return pl.ds(pl.multiple_of(start, size), size)

    barrier = pltpu.get_barrier_semaphore()

    def greet(d, c):
        pl.semaphore_signal(barrier, 1, device_id=(lax.rem(me + d, n), cj), device_id_type=MESH)
        return c
    lax.fori_loop(1, n, greet, 0)
    for e in range(1, ncls):
        pl.semaphore_signal(barrier, 1, device_id=(me, lax.rem(cj + e, ncls)), device_id_type=MESH)
    pl.semaphore_wait(barrier, n - 1 + ncls - 1)

    def exchange(peers, make):
        for p in peers:
            make(p, True).start()
        for p in peers:
            make(p, True).wait_send()
            make(p, False).wait_recv()

    k_peers = [lax.rem(kc + e, nk) for e in range(1, nk)]

    def m1(p, mine):
        if mine:
            return pltpu.make_async_remote_copy(
                src_ref=part_ref.at[rows(p * half, half)], dst_ref=recv1.at[kc],
                send_sem=s1.at[p], recv_sem=r1.at[kc], device_id=dev(zc, xc, p), device_id_type=MESH)
        return pltpu.make_async_remote_copy(
            src_ref=part_ref.at[rows(kc * half, half)], dst_ref=recv1.at[p],
            send_sem=s1.at[kc], recv_sem=r1.at[p], device_id=dev(zc, xc, p), device_id_type=MESH)
    exchange(k_peers, m1)
    a1 = part_ref[rows(kc * half, half), :]
    for p in k_peers:
        a1 = a1 + recv1[p]
    acc1[...] = a1

    x_peers = [lax.rem(xc + e, nx) for e in range(1, nx)]

    def m2(p, mine):
        if mine:
            return pltpu.make_async_remote_copy(
                src_ref=acc1.at[rows(p * quarter, quarter)], dst_ref=recv2.at[xc],
                send_sem=s2.at[p], recv_sem=r2.at[xc], device_id=dev(zc, p, kc), device_id_type=MESH)
        return pltpu.make_async_remote_copy(
            src_ref=acc1.at[rows(xc * quarter, quarter)], dst_ref=recv2.at[p],
            send_sem=s2.at[xc], recv_sem=r2.at[p], device_id=dev(zc, p, kc), device_id_type=MESH)
    exchange(x_peers, m2)
    a2 = acc1[rows(xc * quarter, quarter), :]
    for p in x_peers:
        a2 = a2 + recv2[p]
    acc2[...] = a2

    z_peers = [lax.rem(zc + e, nz) for e in range(1, nz)]

    def m3(p, mine):
        if mine:
            return pltpu.make_async_remote_copy(
                src_ref=acc2.at[rows(p * piece, piece)], dst_ref=recv3.at[zc],
                send_sem=s3.at[p], recv_sem=r3.at[zc], device_id=dev(p, xc, kc), device_id_type=MESH)
        return pltpu.make_async_remote_copy(
            src_ref=acc2.at[rows(zc * piece, piece)], dst_ref=recv3.at[p],
            send_sem=s3.at[zc], recv_sem=r3.at[p], device_id=dev(p, xc, kc), device_id_type=MESH)
    exchange(z_peers, m3)
    a3 = acc2[rows(zc * piece, piece), :]
    for p in z_peers:
        a3 = a3 + recv3[p]
    summed = a3 * scale

    sq = jnp.sum(summed * summed, axis=(0, 1), keepdims=True)
    nrm_dp[me] = jnp.broadcast_to(sq, nrm_dp.shape[1:])

    def b_desc(t, s):
        return pltpu.make_async_remote_copy(
            src_ref=nrm_dp.at[s], dst_ref=nrm_dp.at[s],
            send_sem=sb.at[t], recv_sem=rb.at[s],
            device_id=(t, cj), device_id_type=MESH)

    def b_start(d, c):
        b_desc(lax.rem(me + d, n), me).start()
        return c
    lax.fori_loop(1, n, b_start, 0)

    def b_wait(d, c):
        b_desc(lax.rem(me + d, n), me).wait_send()
        b_desc(me, lax.rem(me + d, n)).wait_recv()
        return c
    lax.fori_loop(1, n, b_wait, 0)

    def b_add(d, acc):
        return acc + nrm_dp[lax.rem(me + d, n)]
    col = lax.fori_loop(1, n, b_add, nrm_dp[me])
    nrm_cls[cj] = col

    def c_desc(t, s):
        return pltpu.make_async_remote_copy(
            src_ref=nrm_cls.at[s], dst_ref=nrm_cls.at[s],
            send_sem=sc.at[t], recv_sem=rc.at[s],
            device_id=(me, t), device_id_type=MESH)

    c_peers = [lax.rem(cj + e, ncls) for e in range(1, ncls)]
    for t in c_peers:
        c_desc(t, cj).start()
    for t in c_peers:
        c_desc(t, cj).wait_send()
        c_desc(cj, t).wait_recv()
    tot = col
    for t in c_peers:
        tot = tot + nrm_cls[t]
    factor = jnp.minimum(1.0, limit / jnp.sqrt(tot))
    fac = jnp.broadcast_to(factor[0:1, 0:1], summed.shape)
    own = kc * half + xc * quarter + zc * piece
    gath[rows(own, piece), :] = (summed * fac).astype(gath.dtype)

    def g3(p, mine):
        src = own if mine else kc * half + xc * quarter + p * piece
        return pltpu.make_async_remote_copy(
            src_ref=gath.at[rows(src, piece)], dst_ref=gath.at[rows(src, piece)],
            send_sem=g3s.at[p], recv_sem=g3r.at[zc if mine else p],
            device_id=dev(p, xc, kc), device_id_type=MESH)
    exchange(z_peers, g3)

    def g2(p, mine):
        src = kc * half + (xc if mine else p) * quarter
        return pltpu.make_async_remote_copy(
            src_ref=gath.at[rows(src, quarter)], dst_ref=gath.at[rows(src, quarter)],
            send_sem=g2s.at[p], recv_sem=g2r.at[xc if mine else p],
            device_id=dev(zc, p, kc), device_id_type=MESH)
    exchange(x_peers, g2)

    def g1(p, mine):
        src = (kc if mine else p) * half
        return pltpu.make_async_remote_copy(
            src_ref=gath.at[rows(src, half)], dst_ref=gath.at[rows(src, half)],
            send_sem=g1s.at[p], recv_sem=g1r.at[kc if mine else p],
            device_id=dev(zc, xc, p), device_id_type=MESH)
    exchange(k_peers, g1)
    out_ref[...] = gath[...]


def grad_reduce(part_grad, n, ncls, scale, limit, nk=2, nx=4):
    nz = n // (nk * nx)
    width = part_grad.shape[1]
    total = part_grad.shape[0]
    half = total // nk
    quarter = half // nx
    piece = quarter // nz
    dma = pltpu.SemaphoreType.DMA
    return pl.pallas_call(
        functools.partial(_grad_kernel, nk, nx, nz, ncls, scale, limit),
        out_shape=jax.ShapeDtypeStruct((total, width), jnp.bfloat16),
        in_specs=[pl.BlockSpec(memory_space=pltpu.VMEM)],
        out_specs=pl.BlockSpec(memory_space=pltpu.VMEM),
        scratch_shapes=[
            pltpu.VMEM((nk, half, width), jnp.float32),
            pltpu.VMEM((half, width), jnp.float32),
            pltpu.VMEM((nx, quarter, width), jnp.float32),
            pltpu.VMEM((quarter, width), jnp.float32),
            pltpu.VMEM((nz, piece, width), jnp.float32),
            pltpu.VMEM((total, width), jnp.bfloat16),
            pltpu.VMEM((n, 8, 128), jnp.float32),
            pltpu.VMEM((ncls, 8, 128), jnp.float32),
            dma((nk,)), dma((nk,)), dma((nx,)), dma((nx,)), dma((nz,)), dma((nz,)),
            dma((n,)), dma((n,)), dma((ncls,)), dma((ncls,)),
            dma((nz,)), dma((nz,)), dma((nx,)), dma((nx,)), dma((nk,)), dma((nk,)),
        ],
        compiler_params=pltpu.CompilerParams(collective_id=0, has_side_effects=True),
    )(part_grad)


def _class_gather_kernel(ncls, x_ref, out_ref, buf, ssem, rsem):
    me = lax.axis_index("dp")
    cj = lax.axis_index("class")
    peers = [lax.rem(cj + e, ncls) for e in range(1, ncls)]
    barrier = pltpu.get_barrier_semaphore()
    for t in peers:
        pl.semaphore_signal(barrier, 1, device_id=(me, t), device_id_type=MESH)
    pl.semaphore_wait(barrier, ncls - 1)

    def desc(t, s):
        return pltpu.make_async_remote_copy(
            src_ref=x_ref, dst_ref=buf.at[s], send_sem=ssem.at[t], recv_sem=rsem.at[s],
            device_id=(me, t), device_id_type=MESH)
    for t in peers:
        desc(t, cj).start()
    buf[cj] = x_ref[...]
    for t in peers:
        desc(t, cj).wait_send()
        desc(cj, t).wait_recv()
    out_ref[...] = buf[...]


def class_gather(x, ncls, cid):
    dma = pltpu.SemaphoreType.DMA
    return pl.pallas_call(
        functools.partial(_class_gather_kernel, ncls),
        out_shape=jax.ShapeDtypeStruct((ncls,) + x.shape, x.dtype),
        in_specs=[pl.BlockSpec(memory_space=pltpu.VMEM)],
        out_specs=pl.BlockSpec(memory_space=pltpu.VMEM),
        scratch_shapes=[pltpu.VMEM((ncls,) + x.shape, x.dtype), dma((ncls,)), dma((ncls,))],
        compiler_params=pltpu.CompilerParams(collective_id=cid, has_side_effects=True),
    )(x)


def _combine_stats(local_max, local_sum, cid):
    both = class_gather(jnp.stack([local_max, local_sum], axis=0), lax.axis_size("class"), cid)
    maxes, sums = both[:, 0], both[:, 1]
    top = jnp.max(maxes, axis=0)
    total = jnp.sum(sums * jnp.exp(maxes - top[None, :]), axis=0)
    return top, total


def on_device(embeddings, labels, head_weight, send_blocks, nbr_source, nbr_offset, counts):
    rows = embeddings.shape[0]
    width_part = embeddings.shape[1]
    class_part = labels.shape[1]
    dp_count = lax.axis_size("dp")
    nbrs = nbr_source.shape[1]
    picks = send_blocks[0]
    out_emb = embeddings.reshape(rows // BLOCK, BLOCK, width_part)[picks]
    out_lab = labels.reshape(rows // BLOCK, BLOCK, class_part)[picks]
    pool_emb = lax.all_to_all(out_emb, "dp", split_axis=0, concat_axis=0, tiled=True)
    pool_lab = lax.all_to_all(out_lab, "dp", split_axis=0, concat_axis=0, tiled=True)
    pool_rows = dp_count * BLOCK
    pool_emb = pool_emb.reshape(pool_rows, width_part)
    pool_lab = pool_lab.reshape(pool_rows, class_part)
    located = nbr_source * BLOCK + nbr_offset

    full_emb = lax.all_gather(embeddings, "class", axis=1, tiled=True)
    head = jnp.dot(full_emb, head_weight, preferred_element_type=jnp.float32)
    h_top, h_total = _combine_stats(
        jnp.max(head, axis=1),
        jnp.sum(jnp.exp(head - jnp.max(head, axis=1, keepdims=True)), axis=1),
        1,
    )
    prob_head = jnp.exp(head - h_top[:, None]) / h_total[:, None]

    near = pool_emb[located]
    partial_value = jnp.einsum(
        "rd,rkd->rk", embeddings, near, preferred_element_type=jnp.float32
    )
    scores = lax.psum(partial_value, "class")
    valid = lax.broadcasted_iota(jnp.int32, (rows, nbrs), 1) < counts[:, None]
    logits = jnp.where(valid, scores / math.sqrt(D), -1e30)
    top = jnp.max(logits, axis=1, keepdims=True)
    expd = jnp.where(valid, jnp.exp(logits - top), 0.0)
    weights = (expd / jnp.sum(expd, axis=1, keepdims=True)).astype(jnp.bfloat16)

    row_ids = lax.broadcasted_iota(jnp.int32, (rows, nbrs), 0)
    dense = jnp.zeros((rows, pool_rows), jnp.float32).at[row_ids, located].add(
        weights.astype(jnp.float32)
    )
    dense_hi = dense.astype(jnp.bfloat16)
    dense_lo = (dense - dense_hi.astype(jnp.float32)).astype(jnp.bfloat16)
    spread = jnp.dot(dense_hi, pool_lab, preferred_element_type=jnp.float32) + jnp.dot(
        dense_lo, pool_lab, preferred_element_type=jnp.float32
    )
    target = 4.0 * spread + labels.astype(jnp.float32)
    z_local = jnp.max(target, axis=1)
    z_top, z_total = _combine_stats(
        z_local, jnp.sum(jnp.exp(target - z_local[:, None]), axis=1), 2
    )
    prob_target = jnp.exp(target - z_top[:, None]) / z_total[:, None]
    diff = (C * (prob_head - prob_target)).astype(jnp.bfloat16)
    part_grad = lax.dot_general(
        full_emb, diff, (((0,), (0,)), ((), ())), preferred_element_type=jnp.float32
    )
    scale = 1.0 / math.sqrt(rows * dp_count)
    limit = 0.5 * math.sqrt(D * C)
    head_grad = grad_reduce(part_grad, dp_count, lax.axis_size("class"), scale, limit)
    return (target.astype(jnp.bfloat16), head_grad)


def solution(mesh):
    return jax.shard_map(
        on_device,
        mesh=mesh,
        in_specs=(
            P("dp", "class"),
            P("dp", "class"),
            P(None, "class"),
            P("dp", None),
            P("dp", None),
            P("dp", None),
            P("dp"),
        ),
        out_specs=(P("dp", "class"), P(None, "class")),
        check_vma=False,
    )
```

```python
import math

import jax
import jax.numpy as jnp
from jax import lax
from jax.experimental import pallas as pl
from jax.experimental.pallas import tpu as pltpu
from jax.sharding import PartitionSpec as P
import functools

D = 1024
C = 4096
BLOCK = 128

MESH = pl.DeviceIdType.MESH

def _grad_kernel(nk, nx, nz, ncls, scale, limit, part_ref, out_ref,
                 recv1, acc1, recv2, acc2, recv3, gath, nrm_dp, nrm_cls,
                 s1, r1, s2, r2, s3, r3, sb, rb, sc, rc, g3s, g3r, g2s, g2r, g1s, g1r):
    n = nk * nx * nz
    me = lax.axis_index("dp")
    cj = lax.axis_index("class")
    kc = lax.rem(me, nk)
    xc = lax.rem(me // nk, nx)
    zc = me // (nk * nx)
    total = part_ref.shape[0]
    half = total // nk
    quarter = half // nx
    piece = quarter // nz

    def dev(z, x, k):
        return ((z * nx + x) * nk + k, cj)

    def rows(start, size):
        return pl.ds(pl.multiple_of(start, size), size)

    barrier = pltpu.get_barrier_semaphore()

    def greet(d, c):
        pl.semaphore_signal(barrier, 1, device_id=(lax.rem(me + d, n), cj), device_id_type=MESH)
        return c
    lax.fori_loop(1, n, greet, 0)
    for e in range(1, ncls):
        pl.semaphore_signal(barrier, 1, device_id=(me, lax.rem(cj + e, ncls)), device_id_type=MESH)
    pl.semaphore_wait(barrier, n - 1 + ncls - 1)

    def exchange(peers, make):
        for p in peers:
            make(p, True).start()
        for p in peers:
            make(p, True).wait_send()
            make(p, False).wait_recv()

    k_peers = [lax.rem(kc + e, nk) for e in range(1, nk)]

    def m1(p, mine):
        if mine:
            return pltpu.make_async_remote_copy(
                src_ref=part_ref.at[rows(p * half, half)], dst_ref=recv1.at[kc],
                send_sem=s1.at[p], recv_sem=r1.at[kc], device_id=dev(zc, xc, p), device_id_type=MESH)
        return pltpu.make_async_remote_copy(
            src_ref=part_ref.at[rows(kc * half, half)], dst_ref=recv1.at[p],
            send_sem=s1.at[kc], recv_sem=r1.at[p], device_id=dev(zc, xc, p), device_id_type=MESH)
    exchange(k_peers, m1)
    a1 = part_ref[rows(kc * half, half), :]
    for p in k_peers:
        a1 = a1 + recv1[p]
    acc1[...] = a1

    x_peers = [lax.rem(xc + e, nx) for e in range(1, nx)]

    def m2(p, mine):
        if mine:
            return pltpu.make_async_remote_copy(
                src_ref=acc1.at[rows(p * quarter, quarter)], dst_ref=recv2.at[xc],
                send_sem=s2.at[p], recv_sem=r2.at[xc], device_id=dev(zc, p, kc), device_id_type=MESH)
        return pltpu.make_async_remote_copy(
            src_ref=acc1.at[rows(xc * quarter, quarter)], dst_ref=recv2.at[p],
            send_sem=s2.at[xc], recv_sem=r2.at[p], device_id=dev(zc, p, kc), device_id_type=MESH)
    exchange(x_peers, m2)
    a2 = acc1[rows(xc * quarter, quarter), :]
    for p in x_peers:
        a2 = a2 + recv2[p]
    acc2[...] = a2

    z_peers = [lax.rem(zc + e, nz) for e in range(1, nz)]

    def m3(p, mine):
        if mine:
            return pltpu.make_async_remote_copy(
                src_ref=acc2.at[rows(p * piece, piece)], dst_ref=recv3.at[zc],
                send_sem=s3.at[p], recv_sem=r3.at[zc], device_id=dev(p, xc, kc), device_id_type=MESH)
        return pltpu.make_async_remote_copy(
            src_ref=acc2.at[rows(zc * piece, piece)], dst_ref=recv3.at[p],
            send_sem=s3.at[zc], recv_sem=r3.at[p], device_id=dev(p, xc, kc), device_id_type=MESH)
    exchange(z_peers, m3)
    a3 = acc2[rows(zc * piece, piece), :]
    for p in z_peers:
        a3 = a3 + recv3[p]
    summed = a3 * scale
    own = kc * half + xc * quarter + zc * piece
    gath[rows(own, piece), :] = summed.astype(gath.dtype)

    sq = jnp.sum(summed * summed, axis=(0, 1), keepdims=True)
    nrm_dp[me] = jnp.broadcast_to(sq, nrm_dp.shape[1:])

    def b_desc(t, s):
        return pltpu.make_async_remote_copy(
            src_ref=nrm_dp.at[s], dst_ref=nrm_dp.at[s],
            send_sem=sb.at[t], recv_sem=rb.at[s],
            device_id=(t, cj), device_id_type=MESH)

    def b_start(d, c):
        b_desc(lax.rem(me + d, n), me).start()
        return c
    lax.fori_loop(1, n, b_start, 0)

    def g3(p, mine):
        src = own if mine else kc * half + xc * quarter + p * piece
        return pltpu.make_async_remote_copy(
            src_ref=gath.at[rows(src, piece)], dst_ref=gath.at[rows(src, piece)],
            send_sem=g3s.at[p], recv_sem=g3r.at[zc if mine else p],
            device_id=dev(p, xc, kc), device_id_type=MESH)
    exchange(z_peers, g3)

    def g2(p, mine):
        src = kc * half + (xc if mine else p) * quarter
        return pltpu.make_async_remote_copy(
            src_ref=gath.at[rows(src, quarter)], dst_ref=gath.at[rows(src, quarter)],
            send_sem=g2s.at[p], recv_sem=g2r.at[xc if mine else p],
            device_id=dev(zc, p, kc), device_id_type=MESH)
    for p in x_peers:
        g2(p, True).start()

    def b_wait(d, c):
        b_desc(lax.rem(me + d, n), me).wait_send()
        b_desc(me, lax.rem(me + d, n)).wait_recv()
        return c
    lax.fori_loop(1, n, b_wait, 0)

    def b_add(d, acc):
        return acc + nrm_dp[lax.rem(me + d, n)]
    col = lax.fori_loop(1, n, b_add, nrm_dp[me])
    nrm_cls[cj] = col

    def c_desc(t, s):
        return pltpu.make_async_remote_copy(
            src_ref=nrm_cls.at[s], dst_ref=nrm_cls.at[s],
            send_sem=sc.at[t], recv_sem=rc.at[s],
            device_id=(me, t), device_id_type=MESH)

    c_peers = [lax.rem(cj + e, ncls) for e in range(1, ncls)]
    for t in c_peers:
        c_desc(t, cj).start()
    for p in x_peers:
        g2(p, True).wait_send()
        g2(p, False).wait_recv()

    def g1(p, mine):
        src = (kc if mine else p) * half
        return pltpu.make_async_remote_copy(
            src_ref=gath.at[rows(src, half)], dst_ref=gath.at[rows(src, half)],
            send_sem=g1s.at[p], recv_sem=g1r.at[kc if mine else p],
            device_id=dev(zc, xc, p), device_id_type=MESH)
    for p in k_peers:
        g1(p, True).start()
    for t in c_peers:
        c_desc(t, cj).wait_send()
        c_desc(cj, t).wait_recv()
    tot = col
    for t in c_peers:
        tot = tot + nrm_cls[t]
    factor = jnp.minimum(1.0, limit / jnp.sqrt(tot))
    for p in k_peers:
        g1(p, True).wait_send()
        g1(p, False).wait_recv()
    fac = jnp.broadcast_to(factor[0:1, 0:1], out_ref.shape)
    out_ref[...] = (gath[...].astype(jnp.float32) * fac).astype(out_ref.dtype)


def grad_reduce(part_grad, n, ncls, scale, limit, nk=2, nx=4):
    nz = n // (nk * nx)
    width = part_grad.shape[1]
    total = part_grad.shape[0]
    half = total // nk
    quarter = half // nx
    piece = quarter // nz
    dma = pltpu.SemaphoreType.DMA
    return pl.pallas_call(
        functools.partial(_grad_kernel, nk, nx, nz, ncls, scale, limit),
        out_shape=jax.ShapeDtypeStruct((total, width), jnp.bfloat16),
        in_specs=[pl.BlockSpec(memory_space=pltpu.VMEM)],
        out_specs=pl.BlockSpec(memory_space=pltpu.VMEM),
        scratch_shapes=[
            pltpu.VMEM((nk, half, width), jnp.float32),
            pltpu.VMEM((half, width), jnp.float32),
            pltpu.VMEM((nx, quarter, width), jnp.float32),
            pltpu.VMEM((quarter, width), jnp.float32),
            pltpu.VMEM((nz, piece, width), jnp.float32),
            pltpu.VMEM((total, width), jnp.bfloat16),
            pltpu.VMEM((n, 8, 128), jnp.float32),
            pltpu.VMEM((ncls, 8, 128), jnp.float32),
            dma((nk,)), dma((nk,)), dma((nx,)), dma((nx,)), dma((nz,)), dma((nz,)),
            dma((n,)), dma((n,)), dma((ncls,)), dma((ncls,)),
            dma((nz,)), dma((nz,)), dma((nx,)), dma((nx,)), dma((nk,)), dma((nk,)),
        ],
        compiler_params=pltpu.CompilerParams(collective_id=0, has_side_effects=True),
    )(part_grad)


def _class_gather_kernel(ncls, x_ref, out_ref, buf, ssem, rsem):
    me = lax.axis_index("dp")
    cj = lax.axis_index("class")
    peers = [lax.rem(cj + e, ncls) for e in range(1, ncls)]
    barrier = pltpu.get_barrier_semaphore()
    for t in peers:
        pl.semaphore_signal(barrier, 1, device_id=(me, t), device_id_type=MESH)
    pl.semaphore_wait(barrier, ncls - 1)

    def desc(t, s):
        return pltpu.make_async_remote_copy(
            src_ref=x_ref, dst_ref=buf.at[s], send_sem=ssem.at[t], recv_sem=rsem.at[s],
            device_id=(me, t), device_id_type=MESH)
    for t in peers:
        desc(t, cj).start()
    buf[cj] = x_ref[...]
    for t in peers:
        desc(t, cj).wait_send()
        desc(cj, t).wait_recv()
    out_ref[...] = buf[...]


def class_gather(x, ncls, cid):
    dma = pltpu.SemaphoreType.DMA
    return pl.pallas_call(
        functools.partial(_class_gather_kernel, ncls),
        out_shape=jax.ShapeDtypeStruct((ncls,) + x.shape, x.dtype),
        in_specs=[pl.BlockSpec(memory_space=pltpu.VMEM)],
        out_specs=pl.BlockSpec(memory_space=pltpu.VMEM),
        scratch_shapes=[pltpu.VMEM((ncls,) + x.shape, x.dtype), dma((ncls,)), dma((ncls,))],
        compiler_params=pltpu.CompilerParams(collective_id=cid, has_side_effects=True),
    )(x)


def _combine_stats(local_max, local_sum, cid):
    both = class_gather(jnp.stack([local_max, local_sum], axis=0), lax.axis_size("class"), cid)
    maxes, sums = both[:, 0], both[:, 1]
    top = jnp.max(maxes, axis=0)
    total = jnp.sum(sums * jnp.exp(maxes - top[None, :]), axis=0)
    return top, total


def on_device(embeddings, labels, head_weight, send_blocks, nbr_source, nbr_offset, counts):
    rows = embeddings.shape[0]
    width_part = embeddings.shape[1]
    class_part = labels.shape[1]
    dp_count = lax.axis_size("dp")
    nbrs = nbr_source.shape[1]
    picks = send_blocks[0]
    out_emb = embeddings.reshape(rows // BLOCK, BLOCK, width_part)[picks]
    out_lab = labels.reshape(rows // BLOCK, BLOCK, class_part)[picks]
    pool_emb = lax.all_to_all(out_emb, "dp", split_axis=0, concat_axis=0, tiled=True)
    pool_lab = lax.all_to_all(out_lab, "dp", split_axis=0, concat_axis=0, tiled=True)
    pool_rows = dp_count * BLOCK
    pool_emb = pool_emb.reshape(pool_rows, width_part)
    pool_lab = pool_lab.reshape(pool_rows, class_part)
    located = nbr_source * BLOCK + nbr_offset

    full_emb = lax.all_gather(embeddings, "class", axis=1, tiled=True)
    head = jnp.dot(full_emb, head_weight, preferred_element_type=jnp.float32)
    h_top, h_total = _combine_stats(
        jnp.max(head, axis=1),
        jnp.sum(jnp.exp(head - jnp.max(head, axis=1, keepdims=True)), axis=1),
        1,
    )
    prob_head = jnp.exp(head - h_top[:, None]) / h_total[:, None]

    near = pool_emb[located]
    partial_value = jnp.einsum(
        "rd,rkd->rk", embeddings, near, preferred_element_type=jnp.float32
    )
    scores = lax.psum(partial_value, "class")
    valid = lax.broadcasted_iota(jnp.int32, (rows, nbrs), 1) < counts[:, None]
    logits = jnp.where(valid, scores / math.sqrt(D), -1e30)
    top = jnp.max(logits, axis=1, keepdims=True)
    expd = jnp.where(valid, jnp.exp(logits - top), 0.0)
    weights = (expd / jnp.sum(expd, axis=1, keepdims=True)).astype(jnp.bfloat16)

    row_ids = lax.broadcasted_iota(jnp.int32, (rows, nbrs), 0)
    dense = jnp.zeros((rows, pool_rows), jnp.float32).at[row_ids, located].add(
        weights.astype(jnp.float32)
    )
    dense_hi = dense.astype(jnp.bfloat16)
    dense_lo = (dense - dense_hi.astype(jnp.float32)).astype(jnp.bfloat16)
    spread = jnp.dot(dense_hi, pool_lab, preferred_element_type=jnp.float32) + jnp.dot(
        dense_lo, pool_lab, preferred_element_type=jnp.float32
    )
    target = 4.0 * spread + labels.astype(jnp.float32)
    z_local = jnp.max(target, axis=1)
    z_top, z_total = _combine_stats(
        z_local, jnp.sum(jnp.exp(target - z_local[:, None]), axis=1), 2
    )
    prob_target = jnp.exp(target - z_top[:, None]) / z_total[:, None]
    diff = (C * (prob_head - prob_target)).astype(jnp.bfloat16)
    part_grad = lax.dot_general(
        full_emb, diff, (((0,), (0,)), ((), ())), preferred_element_type=jnp.float32
    )
    scale = 1.0 / math.sqrt(rows * dp_count)
    limit = 0.5 * math.sqrt(D * C)
    head_grad = grad_reduce(part_grad, dp_count, lax.axis_size("class"), scale, limit)
    return (target.astype(jnp.bfloat16), head_grad)


def solution(mesh):
    return jax.shard_map(
        on_device,
        mesh=mesh,
        in_specs=(
            P("dp", "class"),
            P("dp", "class"),
            P(None, "class"),
            P("dp", None),
            P("dp", None),
            P("dp", None),
            P("dp"),
        ),
        out_specs=(P("dp", "class"), P(None, "class")),
        check_vma=False,
    )
```

```python
import math

import jax
import jax.numpy as jnp
from jax import lax
from jax.experimental import pallas as pl
from jax.experimental.pallas import tpu as pltpu
from jax.sharding import PartitionSpec as P
import functools

D = 1024
C = 4096
BLOCK = 128

MESH = pl.DeviceIdType.MESH

def _grad_kernel(nk, nx, nz, ncls, scale, limit, part_ref, out_ref,
                 recv1, acc1, recv2, acc2, recv3, gath, nrm_dp, nrm_cls,
                 s1, r1, s2, r2, s3, r3, sb, rb, sc, rc, g3s, g3r, g2s, g2r, g1s, g1r):
    n = nk * nx * nz
    me = lax.axis_index("dp")
    cj = lax.axis_index("class")
    kc = lax.rem(me, nk)
    xc = lax.rem(me // nk, nx)
    zc = me // (nk * nx)
    total = part_ref.shape[0]
    half = total // nk
    quarter = half // nx
    piece = quarter // nz

    def dev(z, x, k):
        return ((z * nx + x) * nk + k, cj)

    def rows(start, size):
        return pl.ds(pl.multiple_of(start, size), size)

    barrier = pltpu.get_barrier_semaphore()

    def greet(d, c):
        pl.semaphore_signal(barrier, 1, device_id=(lax.rem(me + d, n), cj), device_id_type=MESH)
        return c
    lax.fori_loop(1, n, greet, 0)
    for e in range(1, ncls):
        pl.semaphore_signal(barrier, 1, device_id=(me, lax.rem(cj + e, ncls)), device_id_type=MESH)
    pl.semaphore_wait(barrier, n - 1 + ncls - 1)

    def exchange(peers, make):
        for p in peers:
            make(p, True).start()
        for p in peers:
            make(p, True).wait_send()
            make(p, False).wait_recv()

    k_peers = [lax.rem(kc + e, nk) for e in range(1, nk)]

    def m1(p, mine):
        if mine:
            return pltpu.make_async_remote_copy(
                src_ref=part_ref.at[rows(p * half, half)], dst_ref=recv1.at[kc],
                send_sem=s1.at[p], recv_sem=r1.at[kc], device_id=dev(zc, xc, p), device_id_type=MESH)
        return pltpu.make_async_remote_copy(
            src_ref=part_ref.at[rows(kc * half, half)], dst_ref=recv1.at[p],
            send_sem=s1.at[kc], recv_sem=r1.at[p], device_id=dev(zc, xc, p), device_id_type=MESH)
    exchange(k_peers, m1)
    a1 = part_ref[rows(kc * half, half), :]
    for p in k_peers:
        a1 = a1 + recv1[p]
    acc1[...] = a1

    x_peers = [lax.rem(xc + e, nx) for e in range(1, nx)]

    def m2(p, mine):
        if mine:
            return pltpu.make_async_remote_copy(
                src_ref=acc1.at[rows(p * quarter, quarter)], dst_ref=recv2.at[xc],
                send_sem=s2.at[p], recv_sem=r2.at[xc], device_id=dev(zc, p, kc), device_id_type=MESH)
        return pltpu.make_async_remote_copy(
            src_ref=acc1.at[rows(xc * quarter, quarter)], dst_ref=recv2.at[p],
            send_sem=s2.at[xc], recv_sem=r2.at[p], device_id=dev(zc, p, kc), device_id_type=MESH)
    exchange(x_peers, m2)
    a2 = acc1[rows(xc * quarter, quarter), :]
    for p in x_peers:
        a2 = a2 + recv2[p]
    acc2[...] = a2

    z_peers = [lax.rem(zc + e, nz) for e in range(1, nz)]

    def m3(p, mine):
        if mine:
            return pltpu.make_async_remote_copy(
                src_ref=acc2.at[rows(p * piece, piece)], dst_ref=recv3.at[zc],
                send_sem=s3.at[p], recv_sem=r3.at[zc], device_id=dev(p, xc, kc), device_id_type=MESH)
        return pltpu.make_async_remote_copy(
            src_ref=acc2.at[rows(zc * piece, piece)], dst_ref=recv3.at[p],
            send_sem=s3.at[zc], recv_sem=r3.at[p], device_id=dev(p, xc, kc), device_id_type=MESH)
    exchange(z_peers, m3)
    a3 = acc2[rows(zc * piece, piece), :]
    for p in z_peers:
        a3 = a3 + recv3[p]
    summed = a3 * scale
    own = kc * half + xc * quarter + zc * piece
    gath[rows(own, piece), :] = summed.astype(gath.dtype)

    sq = jnp.sum(summed * summed, axis=(0, 1), keepdims=True)
    nrm_dp[me] = jnp.broadcast_to(sq, nrm_dp.shape[1:])

    def b_desc(t, s):
        return pltpu.make_async_remote_copy(
            src_ref=nrm_dp.at[s], dst_ref=nrm_dp.at[s],
            send_sem=sb.at[t], recv_sem=rb.at[s],
            device_id=(t, cj), device_id_type=MESH)

    def b_start(d, c):
        b_desc(lax.rem(me + d, n), me).start()
        return c
    lax.fori_loop(1, n, b_start, 0)

    def g3(p, mine):
        src = own if mine else kc * half + xc * quarter + p * piece
        return pltpu.make_async_remote_copy(
            src_ref=gath.at[rows(src, piece)], dst_ref=gath.at[rows(src, piece)],
            send_sem=g3s.at[p], recv_sem=g3r.at[zc if mine else p],
            device_id=dev(p, xc, kc), device_id_type=MESH)
    exchange(z_peers, g3)

    def g2(p, mine):
        src = kc * half + (xc if mine else p) * quarter
        return pltpu.make_async_remote_copy(
            src_ref=gath.at[rows(src, quarter)], dst_ref=gath.at[rows(src, quarter)],
            send_sem=g2s.at[p], recv_sem=g2r.at[xc if mine else p],
            device_id=dev(zc, p, kc), device_id_type=MESH)
    for p in x_peers:
        g2(p, True).start()

    def b_wait(d, c):
        b_desc(lax.rem(me + d, n), me).wait_send()
        b_desc(me, lax.rem(me + d, n)).wait_recv()
        return c
    lax.fori_loop(1, n, b_wait, 0)

    def b_add(d, acc):
        return acc + nrm_dp[lax.rem(me + d, n)]
    col = lax.fori_loop(1, n, b_add, nrm_dp[me])
    nrm_cls[cj] = col

    def c_desc(t, s):
        return pltpu.make_async_remote_copy(
            src_ref=nrm_cls.at[s], dst_ref=nrm_cls.at[s],
            send_sem=sc.at[t], recv_sem=rc.at[s],
            device_id=(me, t), device_id_type=MESH)

    c_peers = [lax.rem(cj + e, ncls) for e in range(1, ncls)]
    for t in c_peers:
        c_desc(t, cj).start()
    for p in x_peers:
        g2(p, True).wait_send()
        g2(p, False).wait_recv()

    def g1(p, mine):
        src = (kc if mine else p) * half
        return pltpu.make_async_remote_copy(
            src_ref=gath.at[rows(src, half)], dst_ref=gath.at[rows(src, half)],
            send_sem=g1s.at[p], recv_sem=g1r.at[kc if mine else p],
            device_id=dev(zc, xc, p), device_id_type=MESH)
    for p in k_peers:
        g1(p, True).start()
    for t in c_peers:
        c_desc(t, cj).wait_send()
        c_desc(cj, t).wait_recv()
    tot = col
    for t in c_peers:
        tot = tot + nrm_cls[t]
    factor = jnp.minimum(1.0, limit / jnp.sqrt(tot))
    for p in k_peers:
        g1(p, True).wait_send()
        g1(p, False).wait_recv()
    fac = jnp.broadcast_to(factor[0:1, 0:1], out_ref.shape)
    out_ref[...] = (gath[...].astype(jnp.float32) * fac).astype(out_ref.dtype)


def grad_reduce(part_grad, n, ncls, scale, limit, nk=2, nx=4):
    nz = n // (nk * nx)
    width = part_grad.shape[1]
    total = part_grad.shape[0]
    half = total // nk
    quarter = half // nx
    piece = quarter // nz
    dma = pltpu.SemaphoreType.DMA
    return pl.pallas_call(
        functools.partial(_grad_kernel, nk, nx, nz, ncls, scale, limit),
        out_shape=jax.ShapeDtypeStruct((total, width), jnp.bfloat16),
        in_specs=[pl.BlockSpec(memory_space=pltpu.VMEM)],
        out_specs=pl.BlockSpec(memory_space=pltpu.VMEM),
        scratch_shapes=[
            pltpu.VMEM((nk, half, width), jnp.float32),
            pltpu.VMEM((half, width), jnp.float32),
            pltpu.VMEM((nx, quarter, width), jnp.float32),
            pltpu.VMEM((quarter, width), jnp.float32),
            pltpu.VMEM((nz, piece, width), jnp.float32),
            pltpu.VMEM((total, width), jnp.bfloat16),
            pltpu.VMEM((n, 8, 128), jnp.float32),
            pltpu.VMEM((ncls, 8, 128), jnp.float32),
            dma((nk,)), dma((nk,)), dma((nx,)), dma((nx,)), dma((nz,)), dma((nz,)),
            dma((n,)), dma((n,)), dma((ncls,)), dma((ncls,)),
            dma((nz,)), dma((nz,)), dma((nx,)), dma((nx,)), dma((nk,)), dma((nk,)),
        ],
        compiler_params=pltpu.CompilerParams(collective_id=0, has_side_effects=True),
    )(part_grad)


def _class_gather_kernel(ncls, x_ref, out_ref, buf, ssem, rsem):
    me = lax.axis_index("dp")
    cj = lax.axis_index("class")
    peers = [lax.rem(cj + e, ncls) for e in range(1, ncls)]
    barrier = pltpu.get_barrier_semaphore()
    for t in peers:
        pl.semaphore_signal(barrier, 1, device_id=(me, t), device_id_type=MESH)
    pl.semaphore_wait(barrier, ncls - 1)

    def desc(t, s):
        return pltpu.make_async_remote_copy(
            src_ref=x_ref, dst_ref=buf.at[s], send_sem=ssem.at[t], recv_sem=rsem.at[s],
            device_id=(me, t), device_id_type=MESH)
    for t in peers:
        desc(t, cj).start()
    buf[cj] = x_ref[...]
    for t in peers:
        desc(t, cj).wait_send()
        desc(cj, t).wait_recv()
    out_ref[...] = buf[...]


def class_gather(x, ncls, cid):
    dma = pltpu.SemaphoreType.DMA
    return pl.pallas_call(
        functools.partial(_class_gather_kernel, ncls),
        out_shape=jax.ShapeDtypeStruct((ncls,) + x.shape, x.dtype),
        in_specs=[pl.BlockSpec(memory_space=pltpu.VMEM)],
        out_specs=pl.BlockSpec(memory_space=pltpu.VMEM),
        scratch_shapes=[pltpu.VMEM((ncls,) + x.shape, x.dtype), dma((ncls,)), dma((ncls,))],
        compiler_params=pltpu.CompilerParams(collective_id=cid, has_side_effects=True),
    )(x)


def _combine_stats(local_max, local_sum, cid):
    both = class_gather(jnp.stack([local_max, local_sum], axis=0), lax.axis_size("class"), cid)
    maxes, sums = both[:, 0], both[:, 1]
    top = jnp.max(maxes, axis=0)
    total = jnp.sum(sums * jnp.exp(maxes - top[None, :]), axis=0)
    return top, total


def on_device(embeddings, labels, head_weight, send_blocks, nbr_source, nbr_offset, counts):
    rows = embeddings.shape[0]
    width_part = embeddings.shape[1]
    class_part = labels.shape[1]
    dp_count = lax.axis_size("dp")
    nbrs = nbr_source.shape[1]
    picks = send_blocks[0]
    out_emb = embeddings.reshape(rows // BLOCK, BLOCK, width_part)[picks]
    out_lab = labels.reshape(rows // BLOCK, BLOCK, class_part)[picks]
    pool_emb = lax.all_to_all(out_emb, "dp", split_axis=0, concat_axis=0, tiled=True)
    pool_lab = lax.all_to_all(out_lab, "dp", split_axis=0, concat_axis=0, tiled=True)
    pool_rows = dp_count * BLOCK
    pool_emb = pool_emb.reshape(pool_rows, width_part)
    pool_lab = pool_lab.reshape(pool_rows, class_part)
    located = nbr_source * BLOCK + nbr_offset

    full_emb = lax.all_gather(embeddings, "class", axis=1, tiled=True)
    head = jnp.dot(full_emb, head_weight, preferred_element_type=jnp.float32)
    h_top, h_total = _combine_stats(
        jnp.max(head, axis=1),
        jnp.sum(jnp.exp(head - jnp.max(head, axis=1, keepdims=True)), axis=1),
        1,
    )
    prob_head = jnp.exp(head - h_top[:, None]) / h_total[:, None]

    near = pool_emb[located]
    partial_value = jnp.einsum(
        "rd,rkd->rk", embeddings, near, preferred_element_type=jnp.float32
    )
    scores = lax.psum(partial_value, "class")
    valid = lax.broadcasted_iota(jnp.int32, (rows, nbrs), 1) < counts[:, None]
    logits = jnp.where(valid, scores / math.sqrt(D), -1e30)
    top = jnp.max(logits, axis=1, keepdims=True)
    expd = jnp.where(valid, jnp.exp(logits - top), 0.0)
    weights = (expd / jnp.sum(expd, axis=1, keepdims=True)).astype(jnp.bfloat16)

    row_ids = lax.broadcasted_iota(jnp.int32, (rows, nbrs), 0)
    dense = jnp.zeros((rows, pool_rows), jnp.float32).at[row_ids, located].add(
        weights.astype(jnp.float32)
    )
    dense_hi = dense.astype(jnp.bfloat16)
    dense_lo = (dense - dense_hi.astype(jnp.float32)).astype(jnp.bfloat16)
    stacked = lax.optimization_barrier(jnp.concatenate([dense_hi, dense_lo], axis=0))
    both = jnp.dot(stacked, pool_lab, preferred_element_type=jnp.float32)
    spread = both[:rows] + both[rows:]
    target = 4.0 * spread + labels.astype(jnp.float32)
    z_local = jnp.max(target, axis=1)
    z_top, z_total = _combine_stats(
        z_local, jnp.sum(jnp.exp(target - z_local[:, None]), axis=1), 2
    )
    prob_target = jnp.exp(target - z_top[:, None]) / z_total[:, None]
    diff = (C * (prob_head - prob_target)).astype(jnp.bfloat16)
    part_grad = lax.dot_general(
        full_emb, diff, (((0,), (0,)), ((), ())), preferred_element_type=jnp.float32
    )
    scale = 1.0 / math.sqrt(rows * dp_count)
    limit = 0.5 * math.sqrt(D * C)
    head_grad = grad_reduce(part_grad, dp_count, lax.axis_size("class"), scale, limit)
    return (target.astype(jnp.bfloat16), head_grad)


def solution(mesh):
    return jax.shard_map(
        on_device,
        mesh=mesh,
        in_specs=(
            P("dp", "class"),
            P("dp", "class"),
            P(None, "class"),
            P("dp", None),
            P("dp", None),
            P("dp", None),
            P("dp"),
        ),
        out_specs=(P("dp", "class"), P(None, "class")),
        check_vma=False,
    )
```

```python
import math

import jax
import jax.numpy as jnp
from jax import lax
from jax.experimental import pallas as pl
from jax.experimental.pallas import tpu as pltpu
from jax.sharding import PartitionSpec as P
import functools

D = 1024
C = 4096
BLOCK = 128

MESH = pl.DeviceIdType.MESH

def _grad_kernel(nk, nx, nz, ncls, scale, limit, part_ref, out_ref,
                 recv1, acc1, recv2, acc2, recv3, gath, nrm_dp, nrm_cls,
                 s1, r1, s2, r2, s3, r3, sb, rb, sc, rc, g3s, g3r, g2s, g2r, g1s, g1r):
    n = nk * nx * nz
    me = lax.axis_index("dp")
    cj = lax.axis_index("class")
    kc = lax.rem(me, nk)
    xc = lax.rem(me // nk, nx)
    zc = me // (nk * nx)
    total = part_ref.shape[0]
    half = total // nk
    quarter = half // nx
    piece = quarter // nz

    def dev(z, x, k):
        return ((z * nx + x) * nk + k, cj)

    def rows(start, size):
        return pl.ds(pl.multiple_of(start, size), size)

    barrier = pltpu.get_barrier_semaphore()

    def greet(d, c):
        pl.semaphore_signal(barrier, 1, device_id=(lax.rem(me + d, n), cj), device_id_type=MESH)
        return c
    lax.fori_loop(1, n, greet, 0)
    for e in range(1, ncls):
        pl.semaphore_signal(barrier, 1, device_id=(me, lax.rem(cj + e, ncls)), device_id_type=MESH)
    pl.semaphore_wait(barrier, n - 1 + ncls - 1)

    def exchange(peers, make):
        for p in peers:
            make(p, True).start()
        for p in peers:
            make(p, True).wait_send()
            make(p, False).wait_recv()

    k_peers = [lax.rem(kc + e, nk) for e in range(1, nk)]

    def m1(p, mine):
        if mine:
            return pltpu.make_async_remote_copy(
                src_ref=part_ref.at[rows(p * half, half)], dst_ref=recv1.at[kc],
                send_sem=s1.at[p], recv_sem=r1.at[kc], device_id=dev(zc, xc, p), device_id_type=MESH)
        return pltpu.make_async_remote_copy(
            src_ref=part_ref.at[rows(kc * half, half)], dst_ref=recv1.at[p],
            send_sem=s1.at[kc], recv_sem=r1.at[p], device_id=dev(zc, xc, p), device_id_type=MESH)
    exchange(k_peers, m1)
    a1 = part_ref[rows(kc * half, half), :]
    for p in k_peers:
        a1 = a1 + recv1[p]
    acc1[...] = a1

    x_peers = [lax.rem(xc + e, nx) for e in range(1, nx)]

    def m2(p, mine):
        if mine:
            return pltpu.make_async_remote_copy(
                src_ref=acc1.at[rows(p * quarter, quarter)], dst_ref=recv2.at[xc],
                send_sem=s2.at[p], recv_sem=r2.at[xc], device_id=dev(zc, p, kc), device_id_type=MESH)
        return pltpu.make_async_remote_copy(
            src_ref=acc1.at[rows(xc * quarter, quarter)], dst_ref=recv2.at[p],
            send_sem=s2.at[xc], recv_sem=r2.at[p], device_id=dev(zc, p, kc), device_id_type=MESH)
    exchange(x_peers, m2)
    a2 = acc1[rows(xc * quarter, quarter), :]
    for p in x_peers:
        a2 = a2 + recv2[p]
    acc2[...] = a2

    z_peers = [lax.rem(zc + e, nz) for e in range(1, nz)]

    def m3(p, mine):
        if mine:
            return pltpu.make_async_remote_copy(
                src_ref=acc2.at[rows(p * piece, piece)], dst_ref=recv3.at[zc],
                send_sem=s3.at[p], recv_sem=r3.at[zc], device_id=dev(p, xc, kc), device_id_type=MESH)
        return pltpu.make_async_remote_copy(
            src_ref=acc2.at[rows(zc * piece, piece)], dst_ref=recv3.at[p],
            send_sem=s3.at[zc], recv_sem=r3.at[p], device_id=dev(p, xc, kc), device_id_type=MESH)
    exchange(z_peers, m3)
    a3 = acc2[rows(zc * piece, piece), :]
    for p in z_peers:
        a3 = a3 + recv3[p]
    summed = a3 * scale
    own = kc * half + xc * quarter + zc * piece
    gath[rows(own, piece), :] = summed.astype(gath.dtype)

    sq = jnp.sum(summed * summed, axis=(0, 1), keepdims=True)
    nrm_dp[me] = jnp.broadcast_to(sq, nrm_dp.shape[1:])

    def b_desc(t, s):
        return pltpu.make_async_remote_copy(
            src_ref=nrm_dp.at[s], dst_ref=nrm_dp.at[s],
            send_sem=sb.at[t], recv_sem=rb.at[s],
            device_id=(t, cj), device_id_type=MESH)

    def b_start(d, c):
        b_desc(lax.rem(me + d, n), me).start()
        return c
    lax.fori_loop(1, n, b_start, 0)

    def g3(p, mine):
        src = own if mine else kc * half + xc * quarter + p * piece
        return pltpu.make_async_remote_copy(
            src_ref=gath.at[rows(src, piece)], dst_ref=gath.at[rows(src, piece)],
            send_sem=g3s.at[p], recv_sem=g3r.at[zc if mine else p],
            device_id=dev(p, xc, kc), device_id_type=MESH)
    exchange(z_peers, g3)

    def g2(p, mine):
        src = kc * half + (xc if mine else p) * quarter
        return pltpu.make_async_remote_copy(
            src_ref=gath.at[rows(src, quarter)], dst_ref=gath.at[rows(src, quarter)],
            send_sem=g2s.at[p], recv_sem=g2r.at[xc if mine else p],
            device_id=dev(zc, p, kc), device_id_type=MESH)
    for p in x_peers:
        g2(p, True).start()

    def b_wait(d, c):
        b_desc(lax.rem(me + d, n), me).wait_send()
        b_desc(me, lax.rem(me + d, n)).wait_recv()
        return c
    lax.fori_loop(1, n, b_wait, 0)

    def b_add(d, acc):
        return acc + nrm_dp[lax.rem(me + d, n)]
    col = lax.fori_loop(1, n, b_add, nrm_dp[me])
    nrm_cls[cj] = col

    def c_desc(t, s):
        return pltpu.make_async_remote_copy(
            src_ref=nrm_cls.at[s], dst_ref=nrm_cls.at[s],
            send_sem=sc.at[t], recv_sem=rc.at[s],
            device_id=(me, t), device_id_type=MESH)

    c_peers = [lax.rem(cj + e, ncls) for e in range(1, ncls)]
    for t in c_peers:
        c_desc(t, cj).start()
    for p in x_peers:
        g2(p, True).wait_send()
        g2(p, False).wait_recv()

    def g1(p, mine):
        src = (kc if mine else p) * half
        return pltpu.make_async_remote_copy(
            src_ref=gath.at[rows(src, half)], dst_ref=gath.at[rows(src, half)],
            send_sem=g1s.at[p], recv_sem=g1r.at[kc if mine else p],
            device_id=dev(zc, xc, p), device_id_type=MESH)
    for p in k_peers:
        g1(p, True).start()
    for t in c_peers:
        c_desc(t, cj).wait_send()
        c_desc(cj, t).wait_recv()
    tot = col
    for t in c_peers:
        tot = tot + nrm_cls[t]
    factor = jnp.minimum(1.0, limit / jnp.sqrt(tot))
    for p in k_peers:
        g1(p, True).wait_send()
        g1(p, False).wait_recv()
    fac = jnp.broadcast_to(factor[0:1, 0:1], out_ref.shape)
    out_ref[...] = (gath[...].astype(jnp.float32) * fac).astype(out_ref.dtype)


def grad_reduce(part_grad, n, ncls, scale, limit, nk=2, nx=4):
    nz = n // (nk * nx)
    width = part_grad.shape[1]
    total = part_grad.shape[0]
    half = total // nk
    quarter = half // nx
    piece = quarter // nz
    dma = pltpu.SemaphoreType.DMA
    return pl.pallas_call(
        functools.partial(_grad_kernel, nk, nx, nz, ncls, scale, limit),
        out_shape=jax.ShapeDtypeStruct((total, width), jnp.bfloat16),
        in_specs=[pl.BlockSpec(memory_space=pltpu.VMEM)],
        out_specs=pl.BlockSpec(memory_space=pltpu.VMEM),
        scratch_shapes=[
            pltpu.VMEM((nk, half, width), jnp.float32),
            pltpu.VMEM((half, width), jnp.float32),
            pltpu.VMEM((nx, quarter, width), jnp.float32),
            pltpu.VMEM((quarter, width), jnp.float32),
            pltpu.VMEM((nz, piece, width), jnp.float32),
            pltpu.VMEM((total, width), jnp.bfloat16),
            pltpu.VMEM((n, 8, 128), jnp.float32),
            pltpu.VMEM((ncls, 8, 128), jnp.float32),
            dma((nk,)), dma((nk,)), dma((nx,)), dma((nx,)), dma((nz,)), dma((nz,)),
            dma((n,)), dma((n,)), dma((ncls,)), dma((ncls,)),
            dma((nz,)), dma((nz,)), dma((nx,)), dma((nx,)), dma((nk,)), dma((nk,)),
        ],
        compiler_params=pltpu.CompilerParams(collective_id=0, has_side_effects=True),
    )(part_grad)


def _class_gather_kernel(ncls, x_ref, out_ref, buf, ssem, rsem):
    me = lax.axis_index("dp")
    cj = lax.axis_index("class")
    peers = [lax.rem(cj + e, ncls) for e in range(1, ncls)]
    barrier = pltpu.get_barrier_semaphore()
    for t in peers:
        pl.semaphore_signal(barrier, 1, device_id=(me, t), device_id_type=MESH)
    pl.semaphore_wait(barrier, ncls - 1)

    def desc(t, s):
        return pltpu.make_async_remote_copy(
            src_ref=x_ref, dst_ref=buf.at[s], send_sem=ssem.at[t], recv_sem=rsem.at[s],
            device_id=(me, t), device_id_type=MESH)
    for t in peers:
        desc(t, cj).start()
    buf[cj] = x_ref[...]
    for t in peers:
        desc(t, cj).wait_send()
        desc(cj, t).wait_recv()
    out_ref[...] = buf[...]


def class_gather(x, ncls, cid):
    dma = pltpu.SemaphoreType.DMA
    return pl.pallas_call(
        functools.partial(_class_gather_kernel, ncls),
        out_shape=jax.ShapeDtypeStruct((ncls,) + x.shape, x.dtype),
        in_specs=[pl.BlockSpec(memory_space=pltpu.VMEM)],
        out_specs=pl.BlockSpec(memory_space=pltpu.VMEM),
        scratch_shapes=[pltpu.VMEM((ncls,) + x.shape, x.dtype), dma((ncls,)), dma((ncls,))],
        compiler_params=pltpu.CompilerParams(collective_id=cid, has_side_effects=True),
    )(x)


def _combine_stats(local_max, local_sum, cid):
    both = class_gather(jnp.stack([local_max, local_sum], axis=0), lax.axis_size("class"), cid)
    maxes, sums = both[:, 0], both[:, 1]
    top = jnp.max(maxes, axis=0)
    total = jnp.sum(sums * jnp.exp(maxes - top[None, :]), axis=0)
    return top, total


def on_device(embeddings, labels, head_weight, send_blocks, nbr_source, nbr_offset, counts):
    rows = embeddings.shape[0]
    width_part = embeddings.shape[1]
    class_part = labels.shape[1]
    dp_count = lax.axis_size("dp")
    nbrs = nbr_source.shape[1]
    picks = send_blocks[0]
    out_emb = embeddings.reshape(rows // BLOCK, BLOCK, width_part)[picks]
    out_lab = labels.reshape(rows // BLOCK, BLOCK, class_part)[picks]
    pool_emb = lax.all_to_all(out_emb, "dp", split_axis=0, concat_axis=0, tiled=True)
    pool_lab = lax.all_to_all(out_lab, "dp", split_axis=0, concat_axis=0, tiled=True)
    pool_rows = dp_count * BLOCK
    pool_emb = pool_emb.reshape(pool_rows, width_part)
    pool_lab = pool_lab.reshape(pool_rows, class_part)
    located = nbr_source * BLOCK + nbr_offset

    ncls = lax.axis_size("class")
    emb_all = class_gather(embeddings, ncls, 3)
    full_emb = jnp.transpose(emb_all, (1, 0, 2)).reshape(rows, ncls * width_part)
    head = jnp.dot(full_emb, head_weight, preferred_element_type=jnp.float32)
    h_max = jnp.max(head, axis=1)
    h_sum = jnp.sum(jnp.exp(head - h_max[:, None]), axis=1)

    near = pool_emb[located]
    partial_value = jnp.einsum(
        "rd,rkd->kr", embeddings, near, preferred_element_type=jnp.float32
    )
    packed = class_gather(
        jnp.concatenate([partial_value, h_max[None, :], h_sum[None, :]], axis=0), ncls, 1
    )
    scores = jnp.sum(packed[:, :nbrs], axis=0).T
    h_maxes, h_sums = packed[:, nbrs], packed[:, nbrs + 1]
    h_top = jnp.max(h_maxes, axis=0)
    h_total = jnp.sum(h_sums * jnp.exp(h_maxes - h_top[None, :]), axis=0)
    prob_head = jnp.exp(head - h_top[:, None]) / h_total[:, None]
    valid = lax.broadcasted_iota(jnp.int32, (rows, nbrs), 1) < counts[:, None]
    logits = jnp.where(valid, scores / math.sqrt(D), -1e30)
    top = jnp.max(logits, axis=1, keepdims=True)
    expd = jnp.where(valid, jnp.exp(logits - top), 0.0)
    weights = (expd / jnp.sum(expd, axis=1, keepdims=True)).astype(jnp.bfloat16)

    row_ids = lax.broadcasted_iota(jnp.int32, (rows, nbrs), 0)
    dense = jnp.zeros((rows, pool_rows), jnp.float32).at[row_ids, located].add(
        weights.astype(jnp.float32)
    )
    dense_hi = dense.astype(jnp.bfloat16)
    dense_lo = (dense - dense_hi.astype(jnp.float32)).astype(jnp.bfloat16)
    stacked = lax.optimization_barrier(jnp.concatenate([dense_hi, dense_lo], axis=0))
    both = jnp.dot(stacked, pool_lab, preferred_element_type=jnp.float32)
    spread = both[:rows] + both[rows:]
    target = 4.0 * spread + labels.astype(jnp.float32)
    z_local = jnp.max(target, axis=1)
    z_top, z_total = _combine_stats(
        z_local, jnp.sum(jnp.exp(target - z_local[:, None]), axis=1), 2
    )
    prob_target = jnp.exp(target - z_top[:, None]) / z_total[:, None]
    diff = (C * (prob_head - prob_target)).astype(jnp.bfloat16)
    part_grad = lax.dot_general(
        full_emb, diff, (((0,), (0,)), ((), ())), preferred_element_type=jnp.float32
    )
    scale = 1.0 / math.sqrt(rows * dp_count)
    limit = 0.5 * math.sqrt(D * C)
    head_grad = grad_reduce(part_grad, dp_count, lax.axis_size("class"), scale, limit)
    return (target.astype(jnp.bfloat16), head_grad)


def solution(mesh):
    return jax.shard_map(
        on_device,
        mesh=mesh,
        in_specs=(
            P("dp", "class"),
            P("dp", "class"),
            P(None, "class"),
            P("dp", None),
            P("dp", None),
            P("dp", None),
            P("dp"),
        ),
        out_specs=(P("dp", "class"), P(None, "class")),
        check_vma=False,
    )
```

```python
import math

import jax
import jax.numpy as jnp
from jax import lax
from jax.experimental import pallas as pl
from jax.experimental.pallas import tpu as pltpu
from jax.sharding import PartitionSpec as P
import functools

D = 1024
C = 4096
BLOCK = 128

MESH = pl.DeviceIdType.MESH

def _grad_kernel(nk, nx, nz, ncls, scale, limit, part_ref, out_ref,
                 recv1, acc1, recv2, acc2, recv3, gath, nrm_dp, nrm_cls,
                 s1, r1, s2, r2, s3, r3, sb, rb, sc, rc, g3s, g3r, g2s, g2r, g1s, g1r):
    n = nk * nx * nz
    me = lax.axis_index("dp")
    cj = lax.axis_index("class")
    kc = lax.rem(me, nk)
    xc = lax.rem(me // nk, nx)
    zc = me // (nk * nx)
    total = part_ref.shape[0]
    half = total // nk
    quarter = half // nx
    piece = quarter // nz

    def dev(z, x, k):
        return ((z * nx + x) * nk + k, cj)

    def rows(start, size):
        return pl.ds(pl.multiple_of(start, size), size)

    barrier = pltpu.get_barrier_semaphore()

    def greet(d, c):
        pl.semaphore_signal(barrier, 1, device_id=(lax.rem(me + d, n), cj), device_id_type=MESH)
        return c
    lax.fori_loop(1, n, greet, 0)
    for e in range(1, ncls):
        pl.semaphore_signal(barrier, 1, device_id=(me, lax.rem(cj + e, ncls)), device_id_type=MESH)
    pl.semaphore_wait(barrier, n - 1 + ncls - 1)

    def exchange(peers, make):
        for p in peers:
            make(p, True).start()
        for p in peers:
            make(p, True).wait_send()
            make(p, False).wait_recv()

    k_peers = [lax.rem(kc + e, nk) for e in range(1, nk)]

    def m1(p, mine):
        if mine:
            return pltpu.make_async_remote_copy(
                src_ref=part_ref.at[rows(p * half, half)], dst_ref=recv1.at[kc],
                send_sem=s1.at[p], recv_sem=r1.at[kc], device_id=dev(zc, xc, p), device_id_type=MESH)
        return pltpu.make_async_remote_copy(
            src_ref=part_ref.at[rows(kc * half, half)], dst_ref=recv1.at[p],
            send_sem=s1.at[kc], recv_sem=r1.at[p], device_id=dev(zc, xc, p), device_id_type=MESH)
    exchange(k_peers, m1)
    a1 = part_ref[rows(kc * half, half), :]
    for p in k_peers:
        a1 = a1 + recv1[p]
    acc1[...] = a1

    x_peers = [lax.rem(xc + e, nx) for e in range(1, nx)]

    def m2(p, mine):
        if mine:
            return pltpu.make_async_remote_copy(
                src_ref=acc1.at[rows(p * quarter, quarter)], dst_ref=recv2.at[xc],
                send_sem=s2.at[p], recv_sem=r2.at[xc], device_id=dev(zc, p, kc), device_id_type=MESH)
        return pltpu.make_async_remote_copy(
            src_ref=acc1.at[rows(xc * quarter, quarter)], dst_ref=recv2.at[p],
            send_sem=s2.at[xc], recv_sem=r2.at[p], device_id=dev(zc, p, kc), device_id_type=MESH)
    exchange(x_peers, m2)
    a2 = acc1[rows(xc * quarter, quarter), :]
    for p in x_peers:
        a2 = a2 + recv2[p]
    acc2[...] = a2

    z_peers = [lax.rem(zc + e, nz) for e in range(1, nz)]

    def m3(p, mine):
        if mine:
            return pltpu.make_async_remote_copy(
                src_ref=acc2.at[rows(p * piece, piece)], dst_ref=recv3.at[zc],
                send_sem=s3.at[p], recv_sem=r3.at[zc], device_id=dev(p, xc, kc), device_id_type=MESH)
        return pltpu.make_async_remote_copy(
            src_ref=acc2.at[rows(zc * piece, piece)], dst_ref=recv3.at[p],
            send_sem=s3.at[zc], recv_sem=r3.at[p], device_id=dev(p, xc, kc), device_id_type=MESH)
    exchange(z_peers, m3)
    a3 = acc2[rows(zc * piece, piece), :]
    for p in z_peers:
        a3 = a3 + recv3[p]
    summed = a3 * scale
    own = kc * half + xc * quarter + zc * piece
    gath[rows(own, piece), :] = summed.astype(gath.dtype)

    sq = jnp.sum(summed * summed, axis=(0, 1), keepdims=True)
    nrm_dp[me] = jnp.broadcast_to(sq, nrm_dp.shape[1:])

    def b_desc(t, s):
        return pltpu.make_async_remote_copy(
            src_ref=nrm_dp.at[s], dst_ref=nrm_dp.at[s],
            send_sem=sb.at[t], recv_sem=rb.at[s],
            device_id=(t, cj), device_id_type=MESH)

    def b_start(d, c):
        b_desc(lax.rem(me + d, n), me).start()
        return c
    lax.fori_loop(1, n, b_start, 0)

    def g3(p, mine):
        src = own if mine else kc * half + xc * quarter + p * piece
        return pltpu.make_async_remote_copy(
            src_ref=gath.at[rows(src, piece)], dst_ref=gath.at[rows(src, piece)],
            send_sem=g3s.at[p], recv_sem=g3r.at[zc if mine else p],
            device_id=dev(p, xc, kc), device_id_type=MESH)
    exchange(z_peers, g3)

    def g2(p, mine):
        src = kc * half + (xc if mine else p) * quarter
        return pltpu.make_async_remote_copy(
            src_ref=gath.at[rows(src, quarter)], dst_ref=gath.at[rows(src, quarter)],
            send_sem=g2s.at[p], recv_sem=g2r.at[xc if mine else p],
            device_id=dev(zc, p, kc), device_id_type=MESH)
    for p in x_peers:
        g2(p, True).start()

    def b_wait(d, c):
        b_desc(lax.rem(me + d, n), me).wait_send()
        b_desc(me, lax.rem(me + d, n)).wait_recv()
        return c
    lax.fori_loop(1, n, b_wait, 0)

    def b_add(d, acc):
        return acc + nrm_dp[lax.rem(me + d, n)]
    col = lax.fori_loop(1, n, b_add, nrm_dp[me])
    nrm_cls[cj] = col

    def c_desc(t, s):
        return pltpu.make_async_remote_copy(
            src_ref=nrm_cls.at[s], dst_ref=nrm_cls.at[s],
            send_sem=sc.at[t], recv_sem=rc.at[s],
            device_id=(me, t), device_id_type=MESH)

    c_peers = [lax.rem(cj + e, ncls) for e in range(1, ncls)]
    for t in c_peers:
        c_desc(t, cj).start()
    for p in x_peers:
        g2(p, True).wait_send()
        g2(p, False).wait_recv()

    def g1(p, mine):
        src = (kc if mine else p) * half
        return pltpu.make_async_remote_copy(
            src_ref=gath.at[rows(src, half)], dst_ref=gath.at[rows(src, half)],
            send_sem=g1s.at[p], recv_sem=g1r.at[kc if mine else p],
            device_id=dev(zc, xc, p), device_id_type=MESH)
    for p in k_peers:
        g1(p, True).start()
    for t in c_peers:
        c_desc(t, cj).wait_send()
        c_desc(cj, t).wait_recv()
    tot = col
    for t in c_peers:
        tot = tot + nrm_cls[t]
    factor = jnp.minimum(1.0, limit / jnp.sqrt(tot))
    for p in k_peers:
        g1(p, True).wait_send()
        g1(p, False).wait_recv()
    fac = jnp.broadcast_to(factor[0:1, 0:1], out_ref.shape)
    out_ref[...] = (gath[...].astype(jnp.float32) * fac).astype(out_ref.dtype)


def grad_reduce(part_grad, n, ncls, scale, limit, nk=2, nx=4):
    nz = n // (nk * nx)
    width = part_grad.shape[1]
    total = part_grad.shape[0]
    half = total // nk
    quarter = half // nx
    piece = quarter // nz
    dma = pltpu.SemaphoreType.DMA
    return pl.pallas_call(
        functools.partial(_grad_kernel, nk, nx, nz, ncls, scale, limit),
        out_shape=jax.ShapeDtypeStruct((total, width), jnp.bfloat16),
        in_specs=[pl.BlockSpec(memory_space=pltpu.VMEM)],
        out_specs=pl.BlockSpec(memory_space=pltpu.VMEM),
        scratch_shapes=[
            pltpu.VMEM((nk, half, width), jnp.float32),
            pltpu.VMEM((half, width), jnp.float32),
            pltpu.VMEM((nx, quarter, width), jnp.float32),
            pltpu.VMEM((quarter, width), jnp.float32),
            pltpu.VMEM((nz, piece, width), jnp.float32),
            pltpu.VMEM((total, width), jnp.bfloat16),
            pltpu.VMEM((n, 8, 128), jnp.float32),
            pltpu.VMEM((ncls, 8, 128), jnp.float32),
            dma((nk,)), dma((nk,)), dma((nx,)), dma((nx,)), dma((nz,)), dma((nz,)),
            dma((n,)), dma((n,)), dma((ncls,)), dma((ncls,)),
            dma((nz,)), dma((nz,)), dma((nx,)), dma((nx,)), dma((nk,)), dma((nk,)),
        ],
        compiler_params=pltpu.CompilerParams(collective_id=0, has_side_effects=True),
    )(part_grad)


def _class_gather_kernel(ncls, x_ref, out_ref, buf, ssem, rsem):
    me = lax.axis_index("dp")
    cj = lax.axis_index("class")
    peers = [lax.rem(cj + e, ncls) for e in range(1, ncls)]
    barrier = pltpu.get_barrier_semaphore()
    for t in peers:
        pl.semaphore_signal(barrier, 1, device_id=(me, t), device_id_type=MESH)
    pl.semaphore_wait(barrier, ncls - 1)

    def desc(t, s):
        return pltpu.make_async_remote_copy(
            src_ref=x_ref, dst_ref=buf.at[s], send_sem=ssem.at[t], recv_sem=rsem.at[s],
            device_id=(me, t), device_id_type=MESH)
    for t in peers:
        desc(t, cj).start()
    buf[cj] = x_ref[...]
    for t in peers:
        desc(t, cj).wait_send()
        desc(cj, t).wait_recv()
    out_ref[...] = buf[...]


def class_gather(x, ncls, cid):
    dma = pltpu.SemaphoreType.DMA
    return pl.pallas_call(
        functools.partial(_class_gather_kernel, ncls),
        out_shape=jax.ShapeDtypeStruct((ncls,) + x.shape, x.dtype),
        in_specs=[pl.BlockSpec(memory_space=pltpu.VMEM)],
        out_specs=pl.BlockSpec(memory_space=pltpu.VMEM),
        scratch_shapes=[pltpu.VMEM((ncls,) + x.shape, x.dtype), dma((ncls,)), dma((ncls,))],
        compiler_params=pltpu.CompilerParams(collective_id=cid, has_side_effects=True),
    )(x)


def _exchange_kernel(n, src_ref, out_ref, buf, ssem, rsem):
    me = lax.axis_index("dp")
    cj = lax.axis_index("class")
    barrier = pltpu.get_barrier_semaphore()

    def greet(d, c):
        pl.semaphore_signal(barrier, 1, device_id=(lax.rem(me + d, n), cj), device_id_type=MESH)
        return c
    lax.fori_loop(1, n, greet, 0)
    pl.semaphore_wait(barrier, n - 1)

    def desc(t, s):
        return pltpu.make_async_remote_copy(
            src_ref=src_ref.at[t], dst_ref=buf.at[s], send_sem=ssem.at[t], recv_sem=rsem.at[s],
            device_id=(t, cj), device_id_type=MESH)

    def start(d, c):
        desc(lax.rem(me + d, n), me).start()
        return c
    lax.fori_loop(1, n, start, 0)
    buf[me] = src_ref[me]

    def wait(d, c):
        desc(lax.rem(me + d, n), me).wait_send()
        desc(me, lax.rem(me + d, n)).wait_recv()
        return c
    lax.fori_loop(1, n, wait, 0)
    out_ref[...] = buf[...]


def dp_exchange(blocks, n, cid):
    dma = pltpu.SemaphoreType.DMA
    return pl.pallas_call(
        functools.partial(_exchange_kernel, n),
        out_shape=jax.ShapeDtypeStruct(blocks.shape, blocks.dtype),
        in_specs=[pl.BlockSpec(memory_space=pltpu.VMEM)],
        out_specs=pl.BlockSpec(memory_space=pltpu.VMEM),
        scratch_shapes=[pltpu.VMEM(blocks.shape, blocks.dtype), dma((n,)), dma((n,))],
        compiler_params=pltpu.CompilerParams(collective_id=cid, has_side_effects=True),
    )(blocks)


def _combine_stats(local_max, local_sum, cid):
    both = class_gather(jnp.stack([local_max, local_sum], axis=0), lax.axis_size("class"), cid)
    maxes, sums = both[:, 0], both[:, 1]
    top = jnp.max(maxes, axis=0)
    total = jnp.sum(sums * jnp.exp(maxes - top[None, :]), axis=0)
    return top, total


def on_device(embeddings, labels, head_weight, send_blocks, nbr_source, nbr_offset, counts):
    rows = embeddings.shape[0]
    width_part = embeddings.shape[1]
    class_part = labels.shape[1]
    dp_count = lax.axis_size("dp")
    nbrs = nbr_source.shape[1]
    picks = send_blocks[0]
    out_emb = embeddings.reshape(rows // BLOCK, BLOCK, width_part)[picks]
    out_lab = labels.reshape(rows // BLOCK, BLOCK, class_part)[picks]
    pool_lab = lax.all_to_all(out_lab, "dp", split_axis=0, concat_axis=0, tiled=True)
    pool_emb = dp_exchange(out_emb, dp_count, 4)
    pool_rows = dp_count * BLOCK
    pool_emb = pool_emb.reshape(pool_rows, width_part)
    pool_lab = pool_lab.reshape(pool_rows, class_part)
    located = nbr_source * BLOCK + nbr_offset

    ncls = lax.axis_size("class")
    emb_all = class_gather(embeddings, ncls, 3)
    full_emb = jnp.transpose(emb_all, (1, 0, 2)).reshape(rows, ncls * width_part)
    head = jnp.dot(full_emb, head_weight, preferred_element_type=jnp.float32)
    h_max = jnp.max(head, axis=1)
    h_sum = jnp.sum(jnp.exp(head - h_max[:, None]), axis=1)

    near = pool_emb[located]
    partial_value = jnp.einsum(
        "rd,rkd->kr", embeddings, near, preferred_element_type=jnp.float32
    )
    packed = class_gather(
        jnp.concatenate([partial_value, h_max[None, :], h_sum[None, :]], axis=0), ncls, 1
    )
    scores = jnp.sum(packed[:, :nbrs], axis=0).T
    h_maxes, h_sums = packed[:, nbrs], packed[:, nbrs + 1]
    h_top = jnp.max(h_maxes, axis=0)
    h_total = jnp.sum(h_sums * jnp.exp(h_maxes - h_top[None, :]), axis=0)
    prob_head = jnp.exp(head - h_top[:, None]) / h_total[:, None]
    valid = lax.broadcasted_iota(jnp.int32, (rows, nbrs), 1) < counts[:, None]
    logits = jnp.where(valid, scores / math.sqrt(D), -1e30)
    top = jnp.max(logits, axis=1, keepdims=True)
    expd = jnp.where(valid, jnp.exp(logits - top), 0.0)
    weights = (expd / jnp.sum(expd, axis=1, keepdims=True)).astype(jnp.bfloat16)

    row_ids = lax.broadcasted_iota(jnp.int32, (rows, nbrs), 0)
    dense = jnp.zeros((rows, pool_rows), jnp.float32).at[row_ids, located].add(
        weights.astype(jnp.float32)
    )
    dense_hi = dense.astype(jnp.bfloat16)
    dense_lo = (dense - dense_hi.astype(jnp.float32)).astype(jnp.bfloat16)
    stacked = lax.optimization_barrier(jnp.concatenate([dense_hi, dense_lo], axis=0))
    both = jnp.dot(stacked, pool_lab, preferred_element_type=jnp.float32)
    spread = both[:rows] + both[rows:]
    target = 4.0 * spread + labels.astype(jnp.float32)
    z_local = jnp.max(target, axis=1)
    z_top, z_total = _combine_stats(
        z_local, jnp.sum(jnp.exp(target - z_local[:, None]), axis=1), 2
    )
    prob_target = jnp.exp(target - z_top[:, None]) / z_total[:, None]
    diff = (C * (prob_head - prob_target)).astype(jnp.bfloat16)
    part_grad = lax.dot_general(
        full_emb, diff, (((0,), (0,)), ((), ())), preferred_element_type=jnp.float32
    )
    scale = 1.0 / math.sqrt(rows * dp_count)
    limit = 0.5 * math.sqrt(D * C)
    head_grad = grad_reduce(part_grad, dp_count, lax.axis_size("class"), scale, limit)
    return (target.astype(jnp.bfloat16), head_grad)


def solution(mesh):
    return jax.shard_map(
        on_device,
        mesh=mesh,
        in_specs=(
            P("dp", "class"),
            P("dp", "class"),
            P(None, "class"),
            P("dp", None),
            P("dp", None),
            P("dp", None),
            P("dp"),
        ),
        out_specs=(P("dp", "class"), P(None, "class")),
        check_vma=False,
    )
```

```python
import math

import jax
import jax.numpy as jnp
from jax import lax
from jax.experimental import pallas as pl
from jax.experimental.pallas import tpu as pltpu
from jax.sharding import PartitionSpec as P
import functools

D = 1024
C = 4096
BLOCK = 128

MESH = pl.DeviceIdType.MESH

def _grad_kernel(nk, nx, nz, ncls, scale, limit, part_ref, out_ref,
                 recv1, acc1, recv2, acc2, recv3, gath, nrm_dp, nrm_cls,
                 s1, r1, s2, r2, s3, r3, sb, rb, sc, rc, g3s, g3r, g2s, g2r, g1s, g1r):
    n = nk * nx * nz
    me = lax.axis_index("dp")
    cj = lax.axis_index("class")
    kc = lax.rem(me, nk)
    xc = lax.rem(me // nk, nx)
    zc = me // (nk * nx)
    total = part_ref.shape[0]
    half = total // nk
    quarter = half // nx
    piece = quarter // nz

    def dev(z, x, k):
        return ((z * nx + x) * nk + k, cj)

    def rows(start, size):
        return pl.ds(pl.multiple_of(start, size), size)

    barrier = pltpu.get_barrier_semaphore()

    def greet(d, c):
        pl.semaphore_signal(barrier, 1, device_id=(lax.rem(me + d, n), cj), device_id_type=MESH)
        return c
    lax.fori_loop(1, n, greet, 0)
    for e in range(1, ncls):
        pl.semaphore_signal(barrier, 1, device_id=(me, lax.rem(cj + e, ncls)), device_id_type=MESH)
    pl.semaphore_wait(barrier, n - 1 + ncls - 1)

    def exchange(peers, make):
        for p in peers:
            make(p, True).start()
        for p in peers:
            make(p, True).wait_send()
            make(p, False).wait_recv()

    k_peers = [lax.rem(kc + e, nk) for e in range(1, nk)]

    def m1(p, mine):
        if mine:
            return pltpu.make_async_remote_copy(
                src_ref=part_ref.at[rows(p * half, half)], dst_ref=recv1.at[kc],
                send_sem=s1.at[p], recv_sem=r1.at[kc], device_id=dev(zc, xc, p), device_id_type=MESH)
        return pltpu.make_async_remote_copy(
            src_ref=part_ref.at[rows(kc * half, half)], dst_ref=recv1.at[p],
            send_sem=s1.at[kc], recv_sem=r1.at[p], device_id=dev(zc, xc, p), device_id_type=MESH)
    exchange(k_peers, m1)
    a1 = part_ref[rows(kc * half, half), :]
    for p in k_peers:
        a1 = a1 + recv1[p]
    acc1[...] = a1

    x_peers = [lax.rem(xc + e, nx) for e in range(1, nx)]

    def m2(p, mine):
        if mine:
            return pltpu.make_async_remote_copy(
                src_ref=acc1.at[rows(p * quarter, quarter)], dst_ref=recv2.at[xc],
                send_sem=s2.at[p], recv_sem=r2.at[xc], device_id=dev(zc, p, kc), device_id_type=MESH)
        return pltpu.make_async_remote_copy(
            src_ref=acc1.at[rows(xc * quarter, quarter)], dst_ref=recv2.at[p],
            send_sem=s2.at[xc], recv_sem=r2.at[p], device_id=dev(zc, p, kc), device_id_type=MESH)
    exchange(x_peers, m2)
    a2 = acc1[rows(xc * quarter, quarter), :]
    for p in x_peers:
        a2 = a2 + recv2[p]
    acc2[...] = a2

    z_peers = [lax.rem(zc + e, nz) for e in range(1, nz)]

    def m3(p, mine):
        if mine:
            return pltpu.make_async_remote_copy(
                src_ref=acc2.at[rows(p * piece, piece)], dst_ref=recv3.at[zc],
                send_sem=s3.at[p], recv_sem=r3.at[zc], device_id=dev(p, xc, kc), device_id_type=MESH)
        return pltpu.make_async_remote_copy(
            src_ref=acc2.at[rows(zc * piece, piece)], dst_ref=recv3.at[p],
            send_sem=s3.at[zc], recv_sem=r3.at[p], device_id=dev(p, xc, kc), device_id_type=MESH)
    exchange(z_peers, m3)
    a3 = acc2[rows(zc * piece, piece), :]
    for p in z_peers:
        a3 = a3 + recv3[p]
    summed = a3 * scale
    own = kc * half + xc * quarter + zc * piece
    gath[rows(own, piece), :] = summed.astype(gath.dtype)

    sq = jnp.sum(summed * summed, axis=(0, 1), keepdims=True)
    nrm_dp[me] = jnp.broadcast_to(sq, nrm_dp.shape[1:])

    def b_desc(t, s):
        return pltpu.make_async_remote_copy(
            src_ref=nrm_dp.at[s], dst_ref=nrm_dp.at[s],
            send_sem=sb.at[t], recv_sem=rb.at[s],
            device_id=(t, cj), device_id_type=MESH)

    def b_start(d, c):
        b_desc(lax.rem(me + d, n), me).start()
        return c
    lax.fori_loop(1, n, b_start, 0)

    def g3(p, mine):
        src = own if mine else kc * half + xc * quarter + p * piece
        return pltpu.make_async_remote_copy(
            src_ref=gath.at[rows(src, piece)], dst_ref=gath.at[rows(src, piece)],
            send_sem=g3s.at[p], recv_sem=g3r.at[zc if mine else p],
            device_id=dev(p, xc, kc), device_id_type=MESH)
    exchange(z_peers, g3)

    def g2(p, mine):
        src = kc * half + (xc if mine else p) * quarter
        return pltpu.make_async_remote_copy(
            src_ref=gath.at[rows(src, quarter)], dst_ref=gath.at[rows(src, quarter)],
            send_sem=g2s.at[p], recv_sem=g2r.at[xc if mine else p],
            device_id=dev(zc, p, kc), device_id_type=MESH)
    for p in x_peers:
        g2(p, True).start()

    def b_wait(d, c):
        b_desc(lax.rem(me + d, n), me).wait_send()
        b_desc(me, lax.rem(me + d, n)).wait_recv()
        return c
    lax.fori_loop(1, n, b_wait, 0)

    def b_add(d, acc):
        return acc + nrm_dp[lax.rem(me + d, n)]
    col = lax.fori_loop(1, n, b_add, nrm_dp[me])
    nrm_cls[cj] = col

    def c_desc(t, s):
        return pltpu.make_async_remote_copy(
            src_ref=nrm_cls.at[s], dst_ref=nrm_cls.at[s],
            send_sem=sc.at[t], recv_sem=rc.at[s],
            device_id=(me, t), device_id_type=MESH)

    c_peers = [lax.rem(cj + e, ncls) for e in range(1, ncls)]
    for t in c_peers:
        c_desc(t, cj).start()
    for p in x_peers:
        g2(p, True).wait_send()
        g2(p, False).wait_recv()

    def g1(p, mine):
        src = (kc if mine else p) * half
        return pltpu.make_async_remote_copy(
            src_ref=gath.at[rows(src, half)], dst_ref=gath.at[rows(src, half)],
            send_sem=g1s.at[p], recv_sem=g1r.at[kc if mine else p],
            device_id=dev(zc, xc, p), device_id_type=MESH)
    for p in k_peers:
        g1(p, True).start()
    for t in c_peers:
        c_desc(t, cj).wait_send()
        c_desc(cj, t).wait_recv()
    tot = col
    for t in c_peers:
        tot = tot + nrm_cls[t]
    factor = jnp.minimum(1.0, limit / jnp.sqrt(tot))
    for p in k_peers:
        g1(p, True).wait_send()
        g1(p, False).wait_recv()
    fac = jnp.broadcast_to(factor[0:1, 0:1], out_ref.shape)
    out_ref[...] = (gath[...].astype(jnp.float32) * fac).astype(out_ref.dtype)


def grad_reduce(part_grad, n, ncls, scale, limit, nk=2, nx=4):
    nz = n // (nk * nx)
    width = part_grad.shape[1]
    total = part_grad.shape[0]
    half = total // nk
    quarter = half // nx
    piece = quarter // nz
    dma = pltpu.SemaphoreType.DMA
    return pl.pallas_call(
        functools.partial(_grad_kernel, nk, nx, nz, ncls, scale, limit),
        out_shape=jax.ShapeDtypeStruct((total, width), jnp.bfloat16),
        in_specs=[pl.BlockSpec(memory_space=pltpu.VMEM)],
        out_specs=pl.BlockSpec(memory_space=pltpu.VMEM),
        scratch_shapes=[
            pltpu.VMEM((nk, half, width), jnp.float32),
            pltpu.VMEM((half, width), jnp.float32),
            pltpu.VMEM((nx, quarter, width), jnp.float32),
            pltpu.VMEM((quarter, width), jnp.float32),
            pltpu.VMEM((nz, piece, width), jnp.float32),
            pltpu.VMEM((total, width), jnp.bfloat16),
            pltpu.VMEM((n, 8, 128), jnp.float32),
            pltpu.VMEM((ncls, 8, 128), jnp.float32),
            dma((nk,)), dma((nk,)), dma((nx,)), dma((nx,)), dma((nz,)), dma((nz,)),
            dma((n,)), dma((n,)), dma((ncls,)), dma((ncls,)),
            dma((nz,)), dma((nz,)), dma((nx,)), dma((nx,)), dma((nk,)), dma((nk,)),
        ],
        compiler_params=pltpu.CompilerParams(collective_id=0, has_side_effects=True),
    )(part_grad)


def _class_gather_kernel(ncls, x_ref, out_ref, buf, ssem, rsem):
    me = lax.axis_index("dp")
    cj = lax.axis_index("class")
    peers = [lax.rem(cj + e, ncls) for e in range(1, ncls)]
    barrier = pltpu.get_barrier_semaphore()
    for t in peers:
        pl.semaphore_signal(barrier, 1, device_id=(me, t), device_id_type=MESH)
    pl.semaphore_wait(barrier, ncls - 1)

    def desc(t, s):
        return pltpu.make_async_remote_copy(
            src_ref=x_ref, dst_ref=buf.at[s], send_sem=ssem.at[t], recv_sem=rsem.at[s],
            device_id=(me, t), device_id_type=MESH)
    for t in peers:
        desc(t, cj).start()
    buf[cj] = x_ref[...]
    for t in peers:
        desc(t, cj).wait_send()
        desc(cj, t).wait_recv()
    out_ref[...] = buf[...]


def class_gather(x, ncls, cid):
    dma = pltpu.SemaphoreType.DMA
    return pl.pallas_call(
        functools.partial(_class_gather_kernel, ncls),
        out_shape=jax.ShapeDtypeStruct((ncls,) + x.shape, x.dtype),
        in_specs=[pl.BlockSpec(memory_space=pltpu.VMEM)],
        out_specs=pl.BlockSpec(memory_space=pltpu.VMEM),
        scratch_shapes=[pltpu.VMEM((ncls,) + x.shape, x.dtype), dma((ncls,)), dma((ncls,))],
        compiler_params=pltpu.CompilerParams(collective_id=cid, has_side_effects=True),
    )(x)


def _exchange_kernel(n, src_ref, out_ref, buf, ssem, rsem):
    me = lax.axis_index("dp")
    cj = lax.axis_index("class")
    barrier = pltpu.get_barrier_semaphore()

    def greet(d, c):
        pl.semaphore_signal(barrier, 1, device_id=(lax.rem(me + d, n), cj), device_id_type=MESH)
        return c
    lax.fori_loop(1, n, greet, 0)
    pl.semaphore_wait(barrier, n - 1)

    def desc(t, s):
        return pltpu.make_async_remote_copy(
            src_ref=src_ref.at[t], dst_ref=buf.at[s], send_sem=ssem.at[t], recv_sem=rsem.at[s],
            device_id=(t, cj), device_id_type=MESH)

    def start(d, c):
        desc(lax.rem(me + d, n), me).start()
        return c
    lax.fori_loop(1, n, start, 0)
    buf[me] = src_ref[me]

    def wait(d, c):
        desc(lax.rem(me + d, n), me).wait_send()
        desc(me, lax.rem(me + d, n)).wait_recv()
        return c
    lax.fori_loop(1, n, wait, 0)
    out_ref[...] = buf[...]


def dp_exchange(blocks, n, cid):
    dma = pltpu.SemaphoreType.DMA
    return pl.pallas_call(
        functools.partial(_exchange_kernel, n),
        out_shape=jax.ShapeDtypeStruct(blocks.shape, blocks.dtype),
        in_specs=[pl.BlockSpec(memory_space=pltpu.VMEM)],
        out_specs=pl.BlockSpec(memory_space=pltpu.VMEM),
        scratch_shapes=[pltpu.VMEM(blocks.shape, blocks.dtype), dma((n,)), dma((n,))],
        compiler_params=pltpu.CompilerParams(collective_id=cid, has_side_effects=True),
    )(blocks)


def _combine_stats(local_max, local_sum, cid):
    both = class_gather(jnp.stack([local_max, local_sum], axis=0), lax.axis_size("class"), cid)
    maxes, sums = both[:, 0], both[:, 1]
    top = jnp.max(maxes, axis=0)
    total = jnp.sum(sums * jnp.exp(maxes - top[None, :]), axis=0)
    return top, total


def on_device(embeddings, labels, head_weight, send_blocks, nbr_source, nbr_offset, counts):
    rows = embeddings.shape[0]
    width_part = embeddings.shape[1]
    class_part = labels.shape[1]
    dp_count = lax.axis_size("dp")
    nbrs = nbr_source.shape[1]
    picks = send_blocks[0]
    out_emb = embeddings.reshape(rows // BLOCK, BLOCK, width_part)[picks]
    out_lab = labels.reshape(rows // BLOCK, BLOCK, class_part)[picks]
    pool_emb = dp_exchange(out_emb, dp_count, 4)
    pool_emb, out_lab = lax.optimization_barrier((pool_emb, out_lab))
    pool_lab = lax.all_to_all(out_lab, "dp", split_axis=0, concat_axis=0, tiled=True)
    pool_rows = dp_count * BLOCK
    pool_emb = pool_emb.reshape(pool_rows, width_part)
    pool_lab = pool_lab.reshape(pool_rows, class_part)
    located = nbr_source * BLOCK + nbr_offset

    ncls = lax.axis_size("class")
    emb_all = class_gather(embeddings, ncls, 3)
    full_emb = jnp.transpose(emb_all, (1, 0, 2)).reshape(rows, ncls * width_part)
    head = jnp.dot(full_emb, head_weight, preferred_element_type=jnp.float32)
    h_max = jnp.max(head, axis=1)
    h_sum = jnp.sum(jnp.exp(head - h_max[:, None]), axis=1)

    near = pool_emb[located]
    partial_value = jnp.einsum(
        "rd,rkd->kr", embeddings, near, preferred_element_type=jnp.float32
    )
    packed = class_gather(
        jnp.concatenate([partial_value, h_max[None, :], h_sum[None, :]], axis=0), ncls, 1
    )
    scores = jnp.sum(packed[:, :nbrs], axis=0).T
    h_maxes, h_sums = packed[:, nbrs], packed[:, nbrs + 1]
    h_top = jnp.max(h_maxes, axis=0)
    h_total = jnp.sum(h_sums * jnp.exp(h_maxes - h_top[None, :]), axis=0)
    prob_head = jnp.exp(head - h_top[:, None]) / h_total[:, None]
    valid = lax.broadcasted_iota(jnp.int32, (rows, nbrs), 1) < counts[:, None]
    logits = jnp.where(valid, scores / math.sqrt(D), -1e30)
    top = jnp.max(logits, axis=1, keepdims=True)
    expd = jnp.where(valid, jnp.exp(logits - top), 0.0)
    weights = (expd / jnp.sum(expd, axis=1, keepdims=True)).astype(jnp.bfloat16)

    row_ids = lax.broadcasted_iota(jnp.int32, (rows, nbrs), 0)
    dense = jnp.zeros((rows, pool_rows), jnp.float32).at[row_ids, located].add(
        weights.astype(jnp.float32)
    )
    dense_hi = dense.astype(jnp.bfloat16)
    dense_lo = (dense - dense_hi.astype(jnp.float32)).astype(jnp.bfloat16)
    stacked = lax.optimization_barrier(jnp.concatenate([dense_hi, dense_lo], axis=0))
    both = jnp.dot(stacked, pool_lab, preferred_element_type=jnp.float32)
    spread = both[:rows] + both[rows:]
    target = 4.0 * spread + labels.astype(jnp.float32)
    z_local = jnp.max(target, axis=1)
    z_top, z_total = _combine_stats(
        z_local, jnp.sum(jnp.exp(target - z_local[:, None]), axis=1), 2
    )
    prob_target = jnp.exp(target - z_top[:, None]) / z_total[:, None]
    diff = (C * (prob_head - prob_target)).astype(jnp.bfloat16)
    part_grad = lax.dot_general(
        full_emb, diff, (((0,), (0,)), ((), ())), preferred_element_type=jnp.float32
    )
    scale = 1.0 / math.sqrt(rows * dp_count)
    limit = 0.5 * math.sqrt(D * C)
    head_grad = grad_reduce(part_grad, dp_count, lax.axis_size("class"), scale, limit)
    return (target.astype(jnp.bfloat16), head_grad)


def solution(mesh):
    return jax.shard_map(
        on_device,
        mesh=mesh,
        in_specs=(
            P("dp", "class"),
            P("dp", "class"),
            P(None, "class"),
            P("dp", None),
            P("dp", None),
            P("dp", None),
            P("dp"),
        ),
        out_specs=(P("dp", "class"), P(None, "class")),
        check_vma=False,
    )
```

```python
import math

import jax
import jax.numpy as jnp
from jax import lax
from jax.experimental import pallas as pl
from jax.experimental.pallas import tpu as pltpu
from jax.sharding import PartitionSpec as P
import functools

D = 1024
C = 4096
BLOCK = 128

MESH = pl.DeviceIdType.MESH

def _grad_kernel(nk, nx, nz, nch, ncls, scale, limit, part_ref, out_ref,
                 recv1, acc1, recv2, acc2, recv3, gath, nrm_dp, nrm_cls,
                 s1, r1, s2, r2, s3, r3, sb, rb, sc, rc, g3s, g3r, g2s, g2r, g1s, g1r):
    n = nk * nx * nz
    me = lax.axis_index("dp")
    cj = lax.axis_index("class")
    kc = lax.rem(me, nk)
    xc = lax.rem(me // nk, nx)
    zc = me // (nk * nx)
    total = part_ref.shape[0]
    half = total // nk
    quarter = half // nx
    piece = quarter // nz

    def dev(z, x, k):
        return ((z * nx + x) * nk + k, cj)

    def rows(start, size):
        return pl.ds(pl.multiple_of(start, size), size)

    barrier = pltpu.get_barrier_semaphore()

    def greet(d, c):
        pl.semaphore_signal(barrier, 1, device_id=(lax.rem(me + d, n), cj), device_id_type=MESH)
        return c
    lax.fori_loop(1, n, greet, 0)
    for e in range(1, ncls):
        pl.semaphore_signal(barrier, 1, device_id=(me, lax.rem(cj + e, ncls)), device_id_type=MESH)
    pl.semaphore_wait(barrier, n - 1 + ncls - 1)

    def exchange(peers, make):
        for p in peers:
            make(p, True).start()
        for p in peers:
            make(p, True).wait_send()
            make(p, False).wait_recv()

    k_peers = [lax.rem(kc + e, nk) for e in range(1, nk)]

    chunk = half // nch

    def m1(p, mine, c):
        part = rows(c * chunk, chunk)
        if mine:
            return pltpu.make_async_remote_copy(
                src_ref=part_ref.at[rows(p * half + c * chunk, chunk)], dst_ref=recv1.at[kc, part],
                send_sem=s1.at[p * nch + c], recv_sem=r1.at[kc * nch + c],
                device_id=dev(zc, xc, p), device_id_type=MESH)
        return pltpu.make_async_remote_copy(
            src_ref=part_ref.at[rows(kc * half + c * chunk, chunk)], dst_ref=recv1.at[p, part],
            send_sem=s1.at[kc * nch + c], recv_sem=r1.at[p * nch + c],
            device_id=dev(zc, xc, p), device_id_type=MESH)
    for p in k_peers:
        for c in range(nch):
            m1(p, True, c).start()
    for p in k_peers:
        for c in range(nch):
            m1(p, True, c).wait_send()
            m1(p, False, c).wait_recv()
    a1 = part_ref[rows(kc * half, half), :]
    for p in k_peers:
        a1 = a1 + recv1[p]
    acc1[...] = a1

    x_peers = [lax.rem(xc + e, nx) for e in range(1, nx)]

    def m2(p, mine):
        if mine:
            return pltpu.make_async_remote_copy(
                src_ref=acc1.at[rows(p * quarter, quarter)], dst_ref=recv2.at[xc],
                send_sem=s2.at[p], recv_sem=r2.at[xc], device_id=dev(zc, p, kc), device_id_type=MESH)
        return pltpu.make_async_remote_copy(
            src_ref=acc1.at[rows(xc * quarter, quarter)], dst_ref=recv2.at[p],
            send_sem=s2.at[xc], recv_sem=r2.at[p], device_id=dev(zc, p, kc), device_id_type=MESH)
    exchange(x_peers, m2)
    a2 = acc1[rows(xc * quarter, quarter), :]
    for p in x_peers:
        a2 = a2 + recv2[p]
    acc2[...] = a2

    z_peers = [lax.rem(zc + e, nz) for e in range(1, nz)]

    def m3(p, mine):
        if mine:
            return pltpu.make_async_remote_copy(
                src_ref=acc2.at[rows(p * piece, piece)], dst_ref=recv3.at[zc],
                send_sem=s3.at[p], recv_sem=r3.at[zc], device_id=dev(p, xc, kc), device_id_type=MESH)
        return pltpu.make_async_remote_copy(
            src_ref=acc2.at[rows(zc * piece, piece)], dst_ref=recv3.at[p],
            send_sem=s3.at[zc], recv_sem=r3.at[p], device_id=dev(p, xc, kc), device_id_type=MESH)
    exchange(z_peers, m3)
    a3 = acc2[rows(zc * piece, piece), :]
    for p in z_peers:
        a3 = a3 + recv3[p]
    summed = a3 * scale
    own = kc * half + xc * quarter + zc * piece
    gath[rows(own, piece), :] = summed.astype(gath.dtype)

    sq = jnp.sum(summed * summed, axis=(0, 1), keepdims=True)
    nrm_dp[me] = jnp.broadcast_to(sq, nrm_dp.shape[1:])

    def b_desc(t, s):
        return pltpu.make_async_remote_copy(
            src_ref=nrm_dp.at[s], dst_ref=nrm_dp.at[s],
            send_sem=sb.at[t], recv_sem=rb.at[s],
            device_id=(t, cj), device_id_type=MESH)

    def b_start(d, c):
        b_desc(lax.rem(me + d, n), me).start()
        return c
    lax.fori_loop(1, n, b_start, 0)

    def g3(p, mine):
        src = own if mine else kc * half + xc * quarter + p * piece
        return pltpu.make_async_remote_copy(
            src_ref=gath.at[rows(src, piece)], dst_ref=gath.at[rows(src, piece)],
            send_sem=g3s.at[p], recv_sem=g3r.at[zc if mine else p],
            device_id=dev(p, xc, kc), device_id_type=MESH)
    exchange(z_peers, g3)

    def g2(p, mine):
        src = kc * half + (xc if mine else p) * quarter
        return pltpu.make_async_remote_copy(
            src_ref=gath.at[rows(src, quarter)], dst_ref=gath.at[rows(src, quarter)],
            send_sem=g2s.at[p], recv_sem=g2r.at[xc if mine else p],
            device_id=dev(zc, p, kc), device_id_type=MESH)
    for p in x_peers:
        g2(p, True).start()

    def b_wait(d, c):
        b_desc(lax.rem(me + d, n), me).wait_send()
        b_desc(me, lax.rem(me + d, n)).wait_recv()
        return c
    lax.fori_loop(1, n, b_wait, 0)

    def b_add(d, acc):
        return acc + nrm_dp[lax.rem(me + d, n)]
    col = lax.fori_loop(1, n, b_add, nrm_dp[me])
    nrm_cls[cj] = col

    def c_desc(t, s):
        return pltpu.make_async_remote_copy(
            src_ref=nrm_cls.at[s], dst_ref=nrm_cls.at[s],
            send_sem=sc.at[t], recv_sem=rc.at[s],
            device_id=(me, t), device_id_type=MESH)

    c_peers = [lax.rem(cj + e, ncls) for e in range(1, ncls)]
    for t in c_peers:
        c_desc(t, cj).start()
    for p in x_peers:
        g2(p, True).wait_send()
        g2(p, False).wait_recv()

    def g1(p, mine, c):
        src = (kc if mine else p) * half + c * chunk
        return pltpu.make_async_remote_copy(
            src_ref=gath.at[rows(src, chunk)], dst_ref=gath.at[rows(src, chunk)],
            send_sem=g1s.at[p * nch + c], recv_sem=g1r.at[(kc if mine else p) * nch + c],
            device_id=dev(zc, xc, p), device_id_type=MESH)
    for p in k_peers:
        for c in range(nch):
            g1(p, True, c).start()
    for t in c_peers:
        c_desc(t, cj).wait_send()
        c_desc(cj, t).wait_recv()
    tot = col
    for t in c_peers:
        tot = tot + nrm_cls[t]
    factor = jnp.minimum(1.0, limit / jnp.sqrt(tot))
    for p in k_peers:
        for c in range(nch):
            g1(p, True, c).wait_send()
            g1(p, False, c).wait_recv()
    fac = jnp.broadcast_to(factor[0:1, 0:1], out_ref.shape)
    out_ref[...] = (gath[...].astype(jnp.float32) * fac).astype(out_ref.dtype)


def grad_reduce(part_grad, n, ncls, scale, limit, nk=2, nx=4, nch=4):
    nz = n // (nk * nx)
    width = part_grad.shape[1]
    total = part_grad.shape[0]
    half = total // nk
    quarter = half // nx
    piece = quarter // nz
    dma = pltpu.SemaphoreType.DMA
    return pl.pallas_call(
        functools.partial(_grad_kernel, nk, nx, nz, nch, ncls, scale, limit),
        out_shape=jax.ShapeDtypeStruct((total, width), jnp.bfloat16),
        in_specs=[pl.BlockSpec(memory_space=pltpu.VMEM)],
        out_specs=pl.BlockSpec(memory_space=pltpu.VMEM),
        scratch_shapes=[
            pltpu.VMEM((nk, half, width), jnp.float32),
            pltpu.VMEM((half, width), jnp.float32),
            pltpu.VMEM((nx, quarter, width), jnp.float32),
            pltpu.VMEM((quarter, width), jnp.float32),
            pltpu.VMEM((nz, piece, width), jnp.float32),
            pltpu.VMEM((total, width), jnp.bfloat16),
            pltpu.VMEM((n, 8, 128), jnp.float32),
            pltpu.VMEM((ncls, 8, 128), jnp.float32),
            dma((nk * nch,)), dma((nk * nch,)), dma((nx,)), dma((nx,)), dma((nz,)), dma((nz,)),
            dma((n,)), dma((n,)), dma((ncls,)), dma((ncls,)),
            dma((nz,)), dma((nz,)), dma((nx,)), dma((nx,)), dma((nk * nch,)), dma((nk * nch,)),
        ],
        compiler_params=pltpu.CompilerParams(collective_id=0, has_side_effects=True),
    )(part_grad)


def _class_gather_kernel(ncls, x_ref, out_ref, buf, ssem, rsem):
    me = lax.axis_index("dp")
    cj = lax.axis_index("class")
    peers = [lax.rem(cj + e, ncls) for e in range(1, ncls)]
    barrier = pltpu.get_barrier_semaphore()
    for t in peers:
        pl.semaphore_signal(barrier, 1, device_id=(me, t), device_id_type=MESH)
    pl.semaphore_wait(barrier, ncls - 1)

    def desc(t, s):
        return pltpu.make_async_remote_copy(
            src_ref=x_ref, dst_ref=buf.at[s], send_sem=ssem.at[t], recv_sem=rsem.at[s],
            device_id=(me, t), device_id_type=MESH)
    for t in peers:
        desc(t, cj).start()
    buf[cj] = x_ref[...]
    for t in peers:
        desc(t, cj).wait_send()
        desc(cj, t).wait_recv()
    out_ref[...] = buf[...]


def class_gather(x, ncls, cid):
    dma = pltpu.SemaphoreType.DMA
    return pl.pallas_call(
        functools.partial(_class_gather_kernel, ncls),
        out_shape=jax.ShapeDtypeStruct((ncls,) + x.shape, x.dtype),
        in_specs=[pl.BlockSpec(memory_space=pltpu.VMEM)],
        out_specs=pl.BlockSpec(memory_space=pltpu.VMEM),
        scratch_shapes=[pltpu.VMEM((ncls,) + x.shape, x.dtype), dma((ncls,)), dma((ncls,))],
        compiler_params=pltpu.CompilerParams(collective_id=cid, has_side_effects=True),
    )(x)


def _combine_stats(local_max, local_sum, cid):
    both = class_gather(jnp.stack([local_max, local_sum], axis=0), lax.axis_size("class"), cid)
    maxes, sums = both[:, 0], both[:, 1]
    top = jnp.max(maxes, axis=0)
    total = jnp.sum(sums * jnp.exp(maxes - top[None, :]), axis=0)
    return top, total


def on_device(embeddings, labels, head_weight, send_blocks, nbr_source, nbr_offset, counts):
    rows = embeddings.shape[0]
    width_part = embeddings.shape[1]
    class_part = labels.shape[1]
    dp_count = lax.axis_size("dp")
    nbrs = nbr_source.shape[1]
    picks = send_blocks[0]
    out_emb = embeddings.reshape(rows // BLOCK, BLOCK, width_part)[picks]
    out_lab = labels.reshape(rows // BLOCK, BLOCK, class_part)[picks]
    pool_emb = lax.all_to_all(out_emb, "dp", split_axis=0, concat_axis=0, tiled=True)
    pool_lab = lax.all_to_all(out_lab, "dp", split_axis=0, concat_axis=0, tiled=True)
    pool_rows = dp_count * BLOCK
    pool_emb = pool_emb.reshape(pool_rows, width_part)
    pool_lab = pool_lab.reshape(pool_rows, class_part)
    located = nbr_source * BLOCK + nbr_offset

    full_emb = lax.all_gather(embeddings, "class", axis=1, tiled=True)
    head = jnp.dot(full_emb, head_weight, preferred_element_type=jnp.float32)
    h_top, h_total = _combine_stats(
        jnp.max(head, axis=1),
        jnp.sum(jnp.exp(head - jnp.max(head, axis=1, keepdims=True)), axis=1),
        1,
    )
    prob_head = jnp.exp(head - h_top[:, None]) / h_total[:, None]

    near = pool_emb[located]
    partial_value = jnp.einsum(
        "rd,rkd->rk", embeddings, near, preferred_element_type=jnp.float32
    )
    scores = lax.psum(partial_value, "class")
    valid = lax.broadcasted_iota(jnp.int32, (rows, nbrs), 1) < counts[:, None]
    logits = jnp.where(valid, scores / math.sqrt(D), -1e30)
    top = jnp.max(logits, axis=1, keepdims=True)
    expd = jnp.where(valid, jnp.exp(logits - top), 0.0)
    weights = (expd / jnp.sum(expd, axis=1, keepdims=True)).astype(jnp.bfloat16)

    row_ids = lax.broadcasted_iota(jnp.int32, (rows, nbrs), 0)
    dense = jnp.zeros((rows, pool_rows), jnp.float32).at[row_ids, located].add(
        weights.astype(jnp.float32)
    )
    dense_hi = dense.astype(jnp.bfloat16)
    dense_lo = (dense - dense_hi.astype(jnp.float32)).astype(jnp.bfloat16)
    stacked = lax.optimization_barrier(jnp.concatenate([dense_hi, dense_lo], axis=0))
    both = jnp.dot(stacked, pool_lab, preferred_element_type=jnp.float32)
    spread = both[:rows] + both[rows:]
    target = 4.0 * spread + labels.astype(jnp.float32)
    z_local = jnp.max(target, axis=1)
    z_top, z_total = _combine_stats(
        z_local, jnp.sum(jnp.exp(target - z_local[:, None]), axis=1), 2
    )
    prob_target = jnp.exp(target - z_top[:, None]) / z_total[:, None]
    diff = (C * (prob_head - prob_target)).astype(jnp.bfloat16)
    part_grad = lax.dot_general(
        full_emb, diff, (((0,), (0,)), ((), ())), preferred_element_type=jnp.float32
    )
    scale = 1.0 / math.sqrt(rows * dp_count)
    limit = 0.5 * math.sqrt(D * C)
    head_grad = grad_reduce(part_grad, dp_count, lax.axis_size("class"), scale, limit)
    return (target.astype(jnp.bfloat16), head_grad)


def solution(mesh):
    return jax.shard_map(
        on_device,
        mesh=mesh,
        in_specs=(
            P("dp", "class"),
            P("dp", "class"),
            P(None, "class"),
            P("dp", None),
            P("dp", None),
            P("dp", None),
            P("dp"),
        ),
        out_specs=(P("dp", "class"), P(None, "class")),
        check_vma=False,
    )
```

```python
import math

import jax
import jax.numpy as jnp
from jax import lax
from jax.experimental import pallas as pl
from jax.experimental.pallas import tpu as pltpu
from jax.sharding import PartitionSpec as P
import functools

D = 1024
C = 4096
BLOCK = 128

MESH = pl.DeviceIdType.MESH

def _grad_kernel(nk, nx, nz, nch, ncls, scale, limit, stats_ref, zt_ref, qt_ref, embt_ref,
                 out_ref, part_ref, sbuf, recv1, acc1, recv2, acc2, recv3, gath, nrm_dp, nrm_cls,
                 ss, rs, s1, r1, s2, r2, s3, r3, sb, rb, sc, rc, g3s, g3r, g2s, g2r, g1s, g1r):
    n = nk * nx * nz
    me = lax.axis_index("dp")
    cj = lax.axis_index("class")
    kc = lax.rem(me, nk)
    xc = lax.rem(me // nk, nx)
    zc = me // (nk * nx)
    total = part_ref.shape[0]
    half = total // nk
    quarter = half // nx
    piece = quarter // nz

    def dev(z, x, k):
        return ((z * nx + x) * nk + k, cj)

    def rows(start, size):
        return pl.ds(pl.multiple_of(start, size), size)

    barrier = pltpu.get_barrier_semaphore()

    def greet(d, c):
        pl.semaphore_signal(barrier, 1, device_id=(lax.rem(me + d, n), cj), device_id_type=MESH)
        return c
    lax.fori_loop(1, n, greet, 0)
    for e in range(1, ncls):
        pl.semaphore_signal(barrier, 1, device_id=(me, lax.rem(cj + e, ncls)), device_id_type=MESH)
    pl.semaphore_wait(barrier, n - 1 + ncls - 1)

    c_peers = [lax.rem(cj + e, ncls) for e in range(1, ncls)]

    def st_desc(t, s):
        return pltpu.make_async_remote_copy(
            src_ref=stats_ref, dst_ref=sbuf.at[s], send_sem=ss.at[t], recv_sem=rs.at[s],
            device_id=(me, t), device_id_type=MESH)
    for t in c_peers:
        st_desc(t, cj).start()
    sbuf[cj] = stats_ref[...]
    for t in c_peers:
        st_desc(t, cj).wait_send()
        st_desc(cj, t).wait_recv()
    top = sbuf[0, 0:1, :]
    for e in range(1, ncls):
        top = jnp.maximum(top, sbuf[e, 0:1, :])
    tot_exp = sbuf[0, 1:2, :] * jnp.exp(sbuf[0, 0:1, :] - top)
    for e in range(1, ncls):
        tot_exp = tot_exp + sbuf[e, 1:2, :] * jnp.exp(sbuf[e, 0:1, :] - top)
    prob_t = jnp.exp(zt_ref[...] - top) / tot_exp
    diff_t = (qt_ref.shape[0] * ncls * (qt_ref[...] - prob_t)).astype(jnp.bfloat16)
    part_ref[...] = lax.dot_general(
        embt_ref[...], diff_t, (((1,), (1,)), ((), ())), preferred_element_type=jnp.float32)

    def exchange(peers, make):
        for p in peers:
            make(p, True).start()
        for p in peers:
            make(p, True).wait_send()
            make(p, False).wait_recv()

    k_peers = [lax.rem(kc + e, nk) for e in range(1, nk)]

    chunk = half // nch

    def m1(p, mine, c):
        part = rows(c * chunk, chunk)
        if mine:
            return pltpu.make_async_remote_copy(
                src_ref=part_ref.at[rows(p * half + c * chunk, chunk)], dst_ref=recv1.at[kc, part],
                send_sem=s1.at[p * nch + c], recv_sem=r1.at[kc * nch + c],
                device_id=dev(zc, xc, p), device_id_type=MESH)
        return pltpu.make_async_remote_copy(
            src_ref=part_ref.at[rows(kc * half + c * chunk, chunk)], dst_ref=recv1.at[p, part],
            send_sem=s1.at[kc * nch + c], recv_sem=r1.at[p * nch + c],
            device_id=dev(zc, xc, p), device_id_type=MESH)
    for p in k_peers:
        for c in range(nch):
            m1(p, True, c).start()
    for p in k_peers:
        for c in range(nch):
            m1(p, True, c).wait_send()
            m1(p, False, c).wait_recv()
    a1 = part_ref[rows(kc * half, half), :]
    for p in k_peers:
        a1 = a1 + recv1[p]
    acc1[...] = a1

    x_peers = [lax.rem(xc + e, nx) for e in range(1, nx)]

    def m2(p, mine):
        if mine:
            return pltpu.make_async_remote_copy(
                src_ref=acc1.at[rows(p * quarter, quarter)], dst_ref=recv2.at[xc],
                send_sem=s2.at[p], recv_sem=r2.at[xc], device_id=dev(zc, p, kc), device_id_type=MESH)
        return pltpu.make_async_remote_copy(
            src_ref=acc1.at[rows(xc * quarter, quarter)], dst_ref=recv2.at[p],
            send_sem=s2.at[xc], recv_sem=r2.at[p], device_id=dev(zc, p, kc), device_id_type=MESH)
    exchange(x_peers, m2)
    a2 = acc1[rows(xc * quarter, quarter), :]
    for p in x_peers:
        a2 = a2 + recv2[p]
    acc2[...] = a2

    z_peers = [lax.rem(zc + e, nz) for e in range(1, nz)]

    def m3(p, mine):
        if mine:
            return pltpu.make_async_remote_copy(
                src_ref=acc2.at[rows(p * piece, piece)], dst_ref=recv3.at[zc],
                send_sem=s3.at[p], recv_sem=r3.at[zc], device_id=dev(p, xc, kc), device_id_type=MESH)
        return pltpu.make_async_remote_copy(
            src_ref=acc2.at[rows(zc * piece, piece)], dst_ref=recv3.at[p],
            send_sem=s3.at[zc], recv_sem=r3.at[p], device_id=dev(p, xc, kc), device_id_type=MESH)
    exchange(z_peers, m3)
    a3 = acc2[rows(zc * piece, piece), :]
    for p in z_peers:
        a3 = a3 + recv3[p]
    summed = a3 * scale
    own = kc * half + xc * quarter + zc * piece
    gath[rows(own, piece), :] = summed.astype(gath.dtype)

    sq = jnp.sum(summed * summed, axis=(0, 1), keepdims=True)
    nrm_dp[me] = jnp.broadcast_to(sq, nrm_dp.shape[1:])

    def b_desc(t, s):
        return pltpu.make_async_remote_copy(
            src_ref=nrm_dp.at[s], dst_ref=nrm_dp.at[s],
            send_sem=sb.at[t], recv_sem=rb.at[s],
            device_id=(t, cj), device_id_type=MESH)

    def b_start(d, c):
        b_desc(lax.rem(me + d, n), me).start()
        return c
    lax.fori_loop(1, n, b_start, 0)

    def g3(p, mine):
        src = own if mine else kc * half + xc * quarter + p * piece
        return pltpu.make_async_remote_copy(
            src_ref=gath.at[rows(src, piece)], dst_ref=gath.at[rows(src, piece)],
            send_sem=g3s.at[p], recv_sem=g3r.at[zc if mine else p],
            device_id=dev(p, xc, kc), device_id_type=MESH)
    exchange(z_peers, g3)

    def g2(p, mine):
        src = kc * half + (xc if mine else p) * quarter
        return pltpu.make_async_remote_copy(
            src_ref=gath.at[rows(src, quarter)], dst_ref=gath.at[rows(src, quarter)],
            send_sem=g2s.at[p], recv_sem=g2r.at[xc if mine else p],
            device_id=dev(zc, p, kc), device_id_type=MESH)
    for p in x_peers:
        g2(p, True).start()

    def b_wait(d, c):
        b_desc(lax.rem(me + d, n), me).wait_send()
        b_desc(me, lax.rem(me + d, n)).wait_recv()
        return c
    lax.fori_loop(1, n, b_wait, 0)

    def b_add(d, acc):
        return acc + nrm_dp[lax.rem(me + d, n)]
    col = lax.fori_loop(1, n, b_add, nrm_dp[me])
    nrm_cls[cj] = col

    def c_desc(t, s):
        return pltpu.make_async_remote_copy(
            src_ref=nrm_cls.at[s], dst_ref=nrm_cls.at[s],
            send_sem=sc.at[t], recv_sem=rc.at[s],
            device_id=(me, t), device_id_type=MESH)

    for t in c_peers:
        c_desc(t, cj).start()
    for p in x_peers:
        g2(p, True).wait_send()
        g2(p, False).wait_recv()

    def g1(p, mine, c):
        src = (kc if mine else p) * half + c * chunk
        return pltpu.make_async_remote_copy(
            src_ref=gath.at[rows(src, chunk)], dst_ref=gath.at[rows(src, chunk)],
            send_sem=g1s.at[p * nch + c], recv_sem=g1r.at[(kc if mine else p) * nch + c],
            device_id=dev(zc, xc, p), device_id_type=MESH)
    for p in k_peers:
        for c in range(nch):
            g1(p, True, c).start()
    for t in c_peers:
        c_desc(t, cj).wait_send()
        c_desc(cj, t).wait_recv()
    tot = col
    for t in c_peers:
        tot = tot + nrm_cls[t]
    factor = jnp.minimum(1.0, limit / jnp.sqrt(tot))
    for p in k_peers:
        for c in range(nch):
            g1(p, True, c).wait_send()
            g1(p, False, c).wait_recv()
    fac = jnp.broadcast_to(factor[0:1, 0:1], out_ref.shape)
    out_ref[...] = (gath[...].astype(jnp.float32) * fac).astype(out_ref.dtype)


def grad_reduce(stats, z_t, q_t, emb_t, n, ncls, scale, limit, nk=2, nx=4, nch=4):
    nz = n // (nk * nx)
    width = z_t.shape[0]
    total = emb_t.shape[0]
    half = total // nk
    quarter = half // nx
    piece = quarter // nz
    dma = pltpu.SemaphoreType.DMA
    vmem = pl.BlockSpec(memory_space=pltpu.VMEM)
    return pl.pallas_call(
        functools.partial(_grad_kernel, nk, nx, nz, nch, ncls, scale, limit),
        out_shape=jax.ShapeDtypeStruct((total, width), jnp.bfloat16),
        in_specs=[vmem] * 4,
        out_specs=vmem,
        scratch_shapes=[
            pltpu.VMEM((total, width), jnp.float32),
            pltpu.VMEM((ncls,) + stats.shape, jnp.float32),
            pltpu.VMEM((nk, half, width), jnp.float32),
            pltpu.VMEM((half, width), jnp.float32),
            pltpu.VMEM((nx, quarter, width), jnp.float32),
            pltpu.VMEM((quarter, width), jnp.float32),
            pltpu.VMEM((nz, piece, width), jnp.float32),
            pltpu.VMEM((total, width), jnp.bfloat16),
            pltpu.VMEM((n, 8, 128), jnp.float32),
            pltpu.VMEM((ncls, 8, 128), jnp.float32),
            dma((ncls,)), dma((ncls,)),
            dma((nk * nch,)), dma((nk * nch,)), dma((nx,)), dma((nx,)), dma((nz,)), dma((nz,)),
            dma((n,)), dma((n,)), dma((ncls,)), dma((ncls,)),
            dma((nz,)), dma((nz,)), dma((nx,)), dma((nx,)), dma((nk * nch,)), dma((nk * nch,)),
        ],
        compiler_params=pltpu.CompilerParams(collective_id=0, has_side_effects=True),
    )(stats, z_t, q_t, emb_t)


def _class_gather_kernel(ncls, x_ref, out_ref, buf, ssem, rsem):
    me = lax.axis_index("dp")
    cj = lax.axis_index("class")
    peers = [lax.rem(cj + e, ncls) for e in range(1, ncls)]
    barrier = pltpu.get_barrier_semaphore()
    for t in peers:
        pl.semaphore_signal(barrier, 1, device_id=(me, t), device_id_type=MESH)
    pl.semaphore_wait(barrier, ncls - 1)

    def desc(t, s):
        return pltpu.make_async_remote_copy(
            src_ref=x_ref, dst_ref=buf.at[s], send_sem=ssem.at[t], recv_sem=rsem.at[s],
            device_id=(me, t), device_id_type=MESH)
    for t in peers:
        desc(t, cj).start()
    buf[cj] = x_ref[...]
    for t in peers:
        desc(t, cj).wait_send()
        desc(cj, t).wait_recv()
    out_ref[...] = buf[...]


def class_gather(x, ncls, cid):
    dma = pltpu.SemaphoreType.DMA
    return pl.pallas_call(
        functools.partial(_class_gather_kernel, ncls),
        out_shape=jax.ShapeDtypeStruct((ncls,) + x.shape, x.dtype),
        in_specs=[pl.BlockSpec(memory_space=pltpu.VMEM)],
        out_specs=pl.BlockSpec(memory_space=pltpu.VMEM),
        scratch_shapes=[pltpu.VMEM((ncls,) + x.shape, x.dtype), dma((ncls,)), dma((ncls,))],
        compiler_params=pltpu.CompilerParams(collective_id=cid, has_side_effects=True),
    )(x)


def _combine_stats(local_max, local_sum, cid):
    both = class_gather(jnp.stack([local_max, local_sum], axis=0), lax.axis_size("class"), cid)
    maxes, sums = both[:, 0], both[:, 1]
    top = jnp.max(maxes, axis=0)
    total = jnp.sum(sums * jnp.exp(maxes - top[None, :]), axis=0)
    return top, total


def on_device(embeddings, labels, head_weight, send_blocks, nbr_source, nbr_offset, counts):
    rows = embeddings.shape[0]
    width_part = embeddings.shape[1]
    class_part = labels.shape[1]
    dp_count = lax.axis_size("dp")
    nbrs = nbr_source.shape[1]
    picks = send_blocks[0]
    out_emb = embeddings.reshape(rows // BLOCK, BLOCK, width_part)[picks]
    out_lab = labels.reshape(rows // BLOCK, BLOCK, class_part)[picks]
    pool_emb = lax.all_to_all(out_emb, "dp", split_axis=0, concat_axis=0, tiled=True)
    pool_lab = lax.all_to_all(out_lab, "dp", split_axis=0, concat_axis=0, tiled=True)
    pool_rows = dp_count * BLOCK
    pool_emb = pool_emb.reshape(pool_rows, width_part)
    pool_lab = pool_lab.reshape(pool_rows, class_part)
    located = nbr_source * BLOCK + nbr_offset

    full_emb = lax.all_gather(embeddings, "class", axis=1, tiled=True)
    head = jnp.dot(full_emb, head_weight, preferred_element_type=jnp.float32)
    h_top, h_total = _combine_stats(
        jnp.max(head, axis=1),
        jnp.sum(jnp.exp(head - jnp.max(head, axis=1, keepdims=True)), axis=1),
        1,
    )
    prob_head = jnp.exp(head - h_top[:, None]) / h_total[:, None]

    near = pool_emb[located]
    partial_value = jnp.einsum(
        "rd,rkd->rk", embeddings, near, preferred_element_type=jnp.float32
    )
    scores = lax.psum(partial_value, "class")
    valid = lax.broadcasted_iota(jnp.int32, (rows, nbrs), 1) < counts[:, None]
    logits = jnp.where(valid, scores / math.sqrt(D), -1e30)
    top = jnp.max(logits, axis=1, keepdims=True)
    expd = jnp.where(valid, jnp.exp(logits - top), 0.0)
    weights = (expd / jnp.sum(expd, axis=1, keepdims=True)).astype(jnp.bfloat16)

    row_ids = lax.broadcasted_iota(jnp.int32, (rows, nbrs), 0)
    dense = jnp.zeros((rows, pool_rows), jnp.float32).at[row_ids, located].add(
        weights.astype(jnp.float32)
    )
    dense_hi = dense.astype(jnp.bfloat16)
    dense_lo = (dense - dense_hi.astype(jnp.float32)).astype(jnp.bfloat16)
    stacked = lax.optimization_barrier(jnp.concatenate([dense_hi, dense_lo], axis=0))
    both = jnp.dot(stacked, pool_lab, preferred_element_type=jnp.float32)
    spread = both[:rows] + both[rows:]
    target = 4.0 * spread + labels.astype(jnp.float32)
    z_local = jnp.max(target, axis=1)
    z_sum = jnp.sum(jnp.exp(target - z_local[:, None]), axis=1)
    scale = 1.0 / math.sqrt(rows * dp_count)
    limit = 0.5 * math.sqrt(D * C)
    head_grad = grad_reduce(
        jnp.stack([z_local, z_sum], axis=0), target.T, prob_head.T, full_emb.T,
        dp_count, lax.axis_size("class"), scale, limit,
    )
    return (target.astype(jnp.bfloat16), head_grad)


def solution(mesh):
    return jax.shard_map(
        on_device,
        mesh=mesh,
        in_specs=(
            P("dp", "class"),
            P("dp", "class"),
            P(None, "class"),
            P("dp", None),
            P("dp", None),
            P("dp", None),
            P("dp"),
        ),
        out_specs=(P("dp", "class"), P(None, "class")),
        check_vma=False,
    )
```

```python
import math

import jax
import jax.numpy as jnp
from jax import lax
from jax.experimental import pallas as pl
from jax.experimental.pallas import tpu as pltpu
from jax.sharding import PartitionSpec as P
import functools

D = 1024
C = 4096
BLOCK = 128

MESH = pl.DeviceIdType.MESH

def _grad_kernel(nk, nx, nz, nch, ncls, scale, limit, stats_ref, zt_ref, qt_ref, embt_ref,
                 out_ref, part_ref, sbuf, recv1, acc1, recv2, acc2, recv3, gath, nrm_dp, nrm_cls,
                 ss, rs, s1, r1, s2, r2, s3, r3, sb, rb, sc, rc, g3s, g3r, g2s, g2r, g1s, g1r):
    n = nk * nx * nz
    me = lax.axis_index("dp")
    cj = lax.axis_index("class")
    kc = lax.rem(me, nk)
    xc = lax.rem(me // nk, nx)
    zc = me // (nk * nx)
    total = part_ref.shape[0]
    half = total // nk
    quarter = half // nx
    piece = quarter // nz

    def dev(z, x, k):
        return ((z * nx + x) * nk + k, cj)

    def rows(start, size):
        return pl.ds(pl.multiple_of(start, size), size)

    barrier = pltpu.get_barrier_semaphore()

    def greet(d, c):
        pl.semaphore_signal(barrier, 1, device_id=(lax.rem(me + d, n), cj), device_id_type=MESH)
        return c
    lax.fori_loop(1, n, greet, 0)
    for e in range(1, ncls):
        pl.semaphore_signal(barrier, 1, device_id=(me, lax.rem(cj + e, ncls)), device_id_type=MESH)
    pl.semaphore_wait(barrier, n - 1 + ncls - 1)

    c_peers = [lax.rem(cj + e, ncls) for e in range(1, ncls)]

    def st_desc(t, s):
        return pltpu.make_async_remote_copy(
            src_ref=stats_ref, dst_ref=sbuf.at[s], send_sem=ss.at[t], recv_sem=rs.at[s],
            device_id=(me, t), device_id_type=MESH)
    for t in c_peers:
        st_desc(t, cj).start()
    sbuf[cj] = stats_ref[...]
    for t in c_peers:
        st_desc(cj, t).wait_recv()
    top = sbuf[0, 0:1, :]
    for e in range(1, ncls):
        top = jnp.maximum(top, sbuf[e, 0:1, :])
    tot_exp = sbuf[0, 1:2, :] * jnp.exp(sbuf[0, 0:1, :] - top)
    for e in range(1, ncls):
        tot_exp = tot_exp + sbuf[e, 1:2, :] * jnp.exp(sbuf[e, 0:1, :] - top)
    prob_t = jnp.exp(zt_ref[...] - top) / tot_exp
    diff_t = (qt_ref.shape[0] * ncls * (qt_ref[...] - prob_t)).astype(jnp.bfloat16)
    part_ref[...] = lax.dot_general(
        embt_ref[...], diff_t, (((1,), (1,)), ((), ())), preferred_element_type=jnp.float32)

    sent = []

    def exchange(peers, make):
        for p in peers:
            make(p, True).start()
            sent.append(make(p, True))
        for p in peers:
            make(p, False).wait_recv()

    k_peers = [lax.rem(kc + e, nk) for e in range(1, nk)]

    chunk = half // nch

    def m1(p, mine, c):
        part = rows(c * chunk, chunk)
        if mine:
            return pltpu.make_async_remote_copy(
                src_ref=part_ref.at[rows(p * half + c * chunk, chunk)], dst_ref=recv1.at[kc, part],
                send_sem=s1.at[p * nch + c], recv_sem=r1.at[kc * nch + c],
                device_id=dev(zc, xc, p), device_id_type=MESH)
        return pltpu.make_async_remote_copy(
            src_ref=part_ref.at[rows(kc * half + c * chunk, chunk)], dst_ref=recv1.at[p, part],
            send_sem=s1.at[kc * nch + c], recv_sem=r1.at[p * nch + c],
            device_id=dev(zc, xc, p), device_id_type=MESH)
    for p in k_peers:
        for c in range(nch):
            m1(p, True, c).start()
    for p in k_peers:
        for c in range(nch):
            sent.append(m1(p, True, c))
            m1(p, False, c).wait_recv()
    a1 = part_ref[rows(kc * half, half), :]
    for p in k_peers:
        a1 = a1 + recv1[p]
    acc1[...] = a1

    x_peers = [lax.rem(xc + e, nx) for e in range(1, nx)]

    def m2(p, mine):
        if mine:
            return pltpu.make_async_remote_copy(
                src_ref=acc1.at[rows(p * quarter, quarter)], dst_ref=recv2.at[xc],
                send_sem=s2.at[p], recv_sem=r2.at[xc], device_id=dev(zc, p, kc), device_id_type=MESH)
        return pltpu.make_async_remote_copy(
            src_ref=acc1.at[rows(xc * quarter, quarter)], dst_ref=recv2.at[p],
            send_sem=s2.at[xc], recv_sem=r2.at[p], device_id=dev(zc, p, kc), device_id_type=MESH)
    exchange(x_peers, m2)
    a2 = acc1[rows(xc * quarter, quarter), :]
    for p in x_peers:
        a2 = a2 + recv2[p]
    acc2[...] = a2

    z_peers = [lax.rem(zc + e, nz) for e in range(1, nz)]

    def m3(p, mine):
        if mine:
            return pltpu.make_async_remote_copy(
                src_ref=acc2.at[rows(p * piece, piece)], dst_ref=recv3.at[zc],
                send_sem=s3.at[p], recv_sem=r3.at[zc], device_id=dev(p, xc, kc), device_id_type=MESH)
        return pltpu.make_async_remote_copy(
            src_ref=acc2.at[rows(zc * piece, piece)], dst_ref=recv3.at[p],
            send_sem=s3.at[zc], recv_sem=r3.at[p], device_id=dev(p, xc, kc), device_id_type=MESH)
    exchange(z_peers, m3)
    a3 = acc2[rows(zc * piece, piece), :]
    for p in z_peers:
        a3 = a3 + recv3[p]
    summed = a3 * scale
    own = kc * half + xc * quarter + zc * piece
    gath[rows(own, piece), :] = summed.astype(gath.dtype)

    sq = jnp.sum(summed * summed, axis=(0, 1), keepdims=True)
    nrm_dp[me] = jnp.broadcast_to(sq, nrm_dp.shape[1:])

    def b_desc(t, s):
        return pltpu.make_async_remote_copy(
            src_ref=nrm_dp.at[s], dst_ref=nrm_dp.at[s],
            send_sem=sb.at[t], recv_sem=rb.at[s],
            device_id=(t, cj), device_id_type=MESH)

    def b_start(d, c):
        b_desc(lax.rem(me + d, n), me).start()
        return c
    lax.fori_loop(1, n, b_start, 0)

    def g3(p, mine):
        src = own if mine else kc * half + xc * quarter + p * piece
        return pltpu.make_async_remote_copy(
            src_ref=gath.at[rows(src, piece)], dst_ref=gath.at[rows(src, piece)],
            send_sem=g3s.at[p], recv_sem=g3r.at[zc if mine else p],
            device_id=dev(p, xc, kc), device_id_type=MESH)
    exchange(z_peers, g3)

    def g2(p, mine):
        src = kc * half + (xc if mine else p) * quarter
        return pltpu.make_async_remote_copy(
            src_ref=gath.at[rows(src, quarter)], dst_ref=gath.at[rows(src, quarter)],
            send_sem=g2s.at[p], recv_sem=g2r.at[xc if mine else p],
            device_id=dev(zc, p, kc), device_id_type=MESH)
    for p in x_peers:
        g2(p, True).start()

    def b_wait(d, c):
        b_desc(me, lax.rem(me + d, n)).wait_recv()
        return c
    lax.fori_loop(1, n, b_wait, 0)

    def b_add(d, acc):
        return acc + nrm_dp[lax.rem(me + d, n)]
    col = lax.fori_loop(1, n, b_add, nrm_dp[me])
    nrm_cls[cj] = col

    def c_desc(t, s):
        return pltpu.make_async_remote_copy(
            src_ref=nrm_cls.at[s], dst_ref=nrm_cls.at[s],
            send_sem=sc.at[t], recv_sem=rc.at[s],
            device_id=(me, t), device_id_type=MESH)

    for t in c_peers:
        c_desc(t, cj).start()
    for p in x_peers:
        sent.append(g2(p, True))
        g2(p, False).wait_recv()

    def g1(p, mine, c):
        src = (kc if mine else p) * half + c * chunk
        return pltpu.make_async_remote_copy(
            src_ref=gath.at[rows(src, chunk)], dst_ref=gath.at[rows(src, chunk)],
            send_sem=g1s.at[p * nch + c], recv_sem=g1r.at[(kc if mine else p) * nch + c],
            device_id=dev(zc, xc, p), device_id_type=MESH)
    for p in k_peers:
        for c in range(nch):
            g1(p, True, c).start()
    for t in c_peers:
        sent.append(c_desc(t, cj))
        c_desc(cj, t).wait_recv()
    tot = col
    for t in c_peers:
        tot = tot + nrm_cls[t]
    factor = jnp.minimum(1.0, limit / jnp.sqrt(tot))
    for p in k_peers:
        for c in range(nch):
            sent.append(g1(p, True, c))
            g1(p, False, c).wait_recv()
    fac = jnp.broadcast_to(factor[0:1, 0:1], out_ref.shape)
    out_ref[...] = (gath[...].astype(jnp.float32) * fac).astype(out_ref.dtype)
    for t in c_peers:
        st_desc(t, cj).wait_send()
    for desc in sent:
        desc.wait_send()

    def b_sent(d, c):
        b_desc(lax.rem(me + d, n), me).wait_send()
        return c
    lax.fori_loop(1, n, b_sent, 0)


def grad_reduce(stats, z_t, q_t, emb_t, n, ncls, scale, limit, nk=2, nx=4, nch=4):
    nz = n // (nk * nx)
    width = z_t.shape[0]
    total = emb_t.shape[0]
    half = total // nk
    quarter = half // nx
    piece = quarter // nz
    dma = pltpu.SemaphoreType.DMA
    vmem = pl.BlockSpec(memory_space=pltpu.VMEM)
    return pl.pallas_call(
        functools.partial(_grad_kernel, nk, nx, nz, nch, ncls, scale, limit),
        out_shape=jax.ShapeDtypeStruct((total, width), jnp.bfloat16),
        in_specs=[vmem] * 4,
        out_specs=vmem,
        scratch_shapes=[
            pltpu.VMEM((total, width), jnp.float32),
            pltpu.VMEM((ncls,) + stats.shape, jnp.float32),
            pltpu.VMEM((nk, half, width), jnp.float32),
            pltpu.VMEM((half, width), jnp.float32),
            pltpu.VMEM((nx, quarter, width), jnp.float32),
            pltpu.VMEM((quarter, width), jnp.float32),
            pltpu.VMEM((nz, piece, width), jnp.float32),
            pltpu.VMEM((total, width), jnp.bfloat16),
            pltpu.VMEM((n, 8, 128), jnp.float32),
            pltpu.VMEM((ncls, 8, 128), jnp.float32),
            dma((ncls,)), dma((ncls,)),
            dma((nk * nch,)), dma((nk * nch,)), dma((nx,)), dma((nx,)), dma((nz,)), dma((nz,)),
            dma((n,)), dma((n,)), dma((ncls,)), dma((ncls,)),
            dma((nz,)), dma((nz,)), dma((nx,)), dma((nx,)), dma((nk * nch,)), dma((nk * nch,)),
        ],
        compiler_params=pltpu.CompilerParams(collective_id=0, has_side_effects=True),
    )(stats, z_t, q_t, emb_t)


def _class_gather_kernel(ncls, x_ref, out_ref, buf, ssem, rsem):
    me = lax.axis_index("dp")
    cj = lax.axis_index("class")
    peers = [lax.rem(cj + e, ncls) for e in range(1, ncls)]
    barrier = pltpu.get_barrier_semaphore()
    for t in peers:
        pl.semaphore_signal(barrier, 1, device_id=(me, t), device_id_type=MESH)
    pl.semaphore_wait(barrier, ncls - 1)

    def desc(t, s):
        return pltpu.make_async_remote_copy(
            src_ref=x_ref, dst_ref=buf.at[s], send_sem=ssem.at[t], recv_sem=rsem.at[s],
            device_id=(me, t), device_id_type=MESH)
    for t in peers:
        desc(t, cj).start()
    buf[cj] = x_ref[...]
    for t in peers:
        desc(t, cj).wait_send()
        desc(cj, t).wait_recv()
    out_ref[...] = buf[...]


def class_gather(x, ncls, cid):
    dma = pltpu.SemaphoreType.DMA
    return pl.pallas_call(
        functools.partial(_class_gather_kernel, ncls),
        out_shape=jax.ShapeDtypeStruct((ncls,) + x.shape, x.dtype),
        in_specs=[pl.BlockSpec(memory_space=pltpu.VMEM)],
        out_specs=pl.BlockSpec(memory_space=pltpu.VMEM),
        scratch_shapes=[pltpu.VMEM((ncls,) + x.shape, x.dtype), dma((ncls,)), dma((ncls,))],
        compiler_params=pltpu.CompilerParams(collective_id=cid, has_side_effects=True),
    )(x)


def _combine_stats(local_max, local_sum, cid):
    both = class_gather(jnp.stack([local_max, local_sum], axis=0), lax.axis_size("class"), cid)
    maxes, sums = both[:, 0], both[:, 1]
    top = jnp.max(maxes, axis=0)
    total = jnp.sum(sums * jnp.exp(maxes - top[None, :]), axis=0)
    return top, total


def on_device(embeddings, labels, head_weight, send_blocks, nbr_source, nbr_offset, counts):
    rows = embeddings.shape[0]
    width_part = embeddings.shape[1]
    class_part = labels.shape[1]
    dp_count = lax.axis_size("dp")
    nbrs = nbr_source.shape[1]
    picks = send_blocks[0]
    out_emb = embeddings.reshape(rows // BLOCK, BLOCK, width_part)[picks]
    out_lab = labels.reshape(rows // BLOCK, BLOCK, class_part)[picks]
    pool_emb = lax.all_to_all(out_emb, "dp", split_axis=0, concat_axis=0, tiled=True)
    pool_lab = lax.all_to_all(out_lab, "dp", split_axis=0, concat_axis=0, tiled=True)
    pool_rows = dp_count * BLOCK
    pool_emb = pool_emb.reshape(pool_rows, width_part)
    pool_lab = pool_lab.reshape(pool_rows, class_part)
    located = nbr_source * BLOCK + nbr_offset

    full_emb = lax.all_gather(embeddings, "class", axis=1, tiled=True)
    head = jnp.dot(full_emb, head_weight, preferred_element_type=jnp.float32)
    h_top, h_total = _combine_stats(
        jnp.max(head, axis=1),
        jnp.sum(jnp.exp(head - jnp.max(head, axis=1, keepdims=True)), axis=1),
        1,
    )
    prob_head = jnp.exp(head - h_top[:, None]) / h_total[:, None]

    near = pool_emb[located]
    partial_value = jnp.einsum(
        "rd,rkd->rk", embeddings, near, preferred_element_type=jnp.float32
    )
    scores = lax.psum(partial_value, "class")
    valid = lax.broadcasted_iota(jnp.int32, (rows, nbrs), 1) < counts[:, None]
    logits = jnp.where(valid, scores / math.sqrt(D), -1e30)
    top = jnp.max(logits, axis=1, keepdims=True)
    expd = jnp.where(valid, jnp.exp(logits - top), 0.0)
    weights = (expd / jnp.sum(expd, axis=1, keepdims=True)).astype(jnp.bfloat16)

    row_ids = lax.broadcasted_iota(jnp.int32, (rows, nbrs), 0)
    dense = jnp.zeros((rows, pool_rows), jnp.float32).at[row_ids, located].add(
        weights.astype(jnp.float32)
    )
    dense_hi = dense.astype(jnp.bfloat16)
    dense_lo = (dense - dense_hi.astype(jnp.float32)).astype(jnp.bfloat16)
    stacked = lax.optimization_barrier(jnp.concatenate([dense_hi, dense_lo], axis=0))
    both = jnp.dot(stacked, pool_lab, preferred_element_type=jnp.float32)
    spread = both[:rows] + both[rows:]
    target = 4.0 * spread + labels.astype(jnp.float32)
    z_local = jnp.max(target, axis=1)
    z_sum = jnp.sum(jnp.exp(target - z_local[:, None]), axis=1)
    scale = 1.0 / math.sqrt(rows * dp_count)
    limit = 0.5 * math.sqrt(D * C)
    head_grad = grad_reduce(
        jnp.stack([z_local, z_sum], axis=0), target.T, prob_head.T, full_emb.T,
        dp_count, lax.axis_size("class"), scale, limit,
    )
    return (target.astype(jnp.bfloat16), head_grad)


def solution(mesh):
    return jax.shard_map(
        on_device,
        mesh=mesh,
        in_specs=(
            P("dp", "class"),
            P("dp", "class"),
            P(None, "class"),
            P("dp", None),
            P("dp", None),
            P("dp", None),
            P("dp"),
        ),
        out_specs=(P("dp", "class"), P(None, "class")),
        check_vma=False,
    )
```

```python
import math

import jax
import jax.numpy as jnp
from jax import lax
from jax.experimental import pallas as pl
from jax.experimental.pallas import tpu as pltpu
from jax.sharding import PartitionSpec as P
import functools

D = 1024
C = 4096
BLOCK = 128

MESH = pl.DeviceIdType.MESH

def _grad_kernel(nk, nx, nz, nch, ncls, scale, limit, stats_ref, zt_ref, qt_ref, embt_ref,
                 out_ref, part_ref, sbuf, recv1, acc1, recv2, acc2, recv3, gath, nrm_dp, nrm_cls,
                 ss, rs, s1, r1, s2, r2, s3, r3, sb, rb, sc, rc, g3s, g3r, g2s, g2r, g1s, g1r):
    n = nk * nx * nz
    me = lax.axis_index("dp")
    cj = lax.axis_index("class")
    kc = lax.rem(me, nk)
    xc = lax.rem(me // nk, nx)
    zc = me // (nk * nx)
    total = part_ref.shape[0]
    half = total // nk
    quarter = half // nx
    piece = quarter // nz

    def dev(z, x, k):
        return ((z * nx + x) * nk + k, cj)

    def rows(start, size):
        return pl.ds(pl.multiple_of(start, size), size)

    barrier = pltpu.get_barrier_semaphore()

    def greet(d, c):
        pl.semaphore_signal(barrier, 1, device_id=(lax.rem(me + d, n), cj), device_id_type=MESH)
        return c
    lax.fori_loop(1, n, greet, 0)
    for e in range(1, ncls):
        pl.semaphore_signal(barrier, 1, device_id=(me, lax.rem(cj + e, ncls)), device_id_type=MESH)
    pl.semaphore_wait(barrier, n - 1 + ncls - 1)

    c_peers = [lax.rem(cj + e, ncls) for e in range(1, ncls)]

    def st_desc(t, s):
        return pltpu.make_async_remote_copy(
            src_ref=stats_ref, dst_ref=sbuf.at[s], send_sem=ss.at[t], recv_sem=rs.at[s],
            device_id=(me, t), device_id_type=MESH)
    for t in c_peers:
        st_desc(t, cj).start()
    sbuf[cj] = stats_ref[...]
    for t in c_peers:
        st_desc(t, cj).wait_send()
        st_desc(cj, t).wait_recv()
    top = sbuf[0, 0:1, :]
    for e in range(1, ncls):
        top = jnp.maximum(top, sbuf[e, 0:1, :])
    tot_exp = sbuf[0, 1:2, :] * jnp.exp(sbuf[0, 0:1, :] - top)
    for e in range(1, ncls):
        tot_exp = tot_exp + sbuf[e, 1:2, :] * jnp.exp(sbuf[e, 0:1, :] - top)
    prob_t = jnp.exp(zt_ref[...] - top) / tot_exp
    diff_t = (qt_ref.shape[0] * ncls * (qt_ref[...] - prob_t)).astype(jnp.bfloat16)
    part_ref[...] = lax.dot_general(
        embt_ref[...], diff_t, (((1,), (1,)), ((), ())), preferred_element_type=jnp.float32)

    def exchange(peers, make):
        for p in peers:
            make(p, True).start()
        for p in peers:
            make(p, True).wait_send()
            make(p, False).wait_recv()

    k_peers = [lax.rem(kc + e, nk) for e in range(1, nk)]

    chunk = half // nch

    def m1(p, mine, c):
        part = rows(c * chunk, chunk)
        if mine:
            return pltpu.make_async_remote_copy(
                src_ref=part_ref.at[rows(p * half + c * chunk, chunk)], dst_ref=recv1.at[kc, part],
                send_sem=s1.at[p * nch + c], recv_sem=r1.at[kc * nch + c],
                device_id=dev(zc, xc, p), device_id_type=MESH)
        return pltpu.make_async_remote_copy(
            src_ref=part_ref.at[rows(kc * half + c * chunk, chunk)], dst_ref=recv1.at[p, part],
            send_sem=s1.at[kc * nch + c], recv_sem=r1.at[p * nch + c],
            device_id=dev(zc, xc, p), device_id_type=MESH)
    for p in k_peers:
        for c in range(nch):
            m1(p, True, c).start()
    for p in k_peers:
        for c in range(nch):
            m1(p, True, c).wait_send()
            m1(p, False, c).wait_recv()
    a1 = part_ref[rows(kc * half, half), :]
    for p in k_peers:
        a1 = a1 + recv1[p]
    acc1[...] = a1

    x_peers = [lax.rem(xc + e, nx) for e in range(1, nx)]

    def m2(p, mine):
        if mine:
            return pltpu.make_async_remote_copy(
                src_ref=acc1.at[rows(p * quarter, quarter)], dst_ref=recv2.at[xc],
                send_sem=s2.at[p], recv_sem=r2.at[xc], device_id=dev(zc, p, kc), device_id_type=MESH)
        return pltpu.make_async_remote_copy(
            src_ref=acc1.at[rows(xc * quarter, quarter)], dst_ref=recv2.at[p],
            send_sem=s2.at[xc], recv_sem=r2.at[p], device_id=dev(zc, p, kc), device_id_type=MESH)
    exchange(x_peers, m2)
    a2 = acc1[rows(xc * quarter, quarter), :]
    for p in x_peers:
        a2 = a2 + recv2[p]
    acc2[...] = a2

    z_peers = [lax.rem(zc + e, nz) for e in range(1, nz)]

    def m3(p, mine):
        if mine:
            return pltpu.make_async_remote_copy(
                src_ref=acc2.at[rows(p * piece, piece)], dst_ref=recv3.at[zc],
                send_sem=s3.at[p], recv_sem=r3.at[zc], device_id=dev(p, xc, kc), device_id_type=MESH)
        return pltpu.make_async_remote_copy(
            src_ref=acc2.at[rows(zc * piece, piece)], dst_ref=recv3.at[p],
            send_sem=s3.at[zc], recv_sem=r3.at[p], device_id=dev(p, xc, kc), device_id_type=MESH)
    exchange(z_peers, m3)
    a3 = acc2[rows(zc * piece, piece), :]
    for p in z_peers:
        a3 = a3 + recv3[p]
    summed = a3 * scale
    own = kc * half + xc * quarter + zc * piece
    gath[rows(own, piece), :] = summed.astype(gath.dtype)

    sq = jnp.sum(summed * summed, axis=(0, 1), keepdims=True)
    nrm_dp[me] = jnp.broadcast_to(sq, nrm_dp.shape[1:])

    def b_desc(t, s):
        return pltpu.make_async_remote_copy(
            src_ref=nrm_dp.at[s], dst_ref=nrm_dp.at[s],
            send_sem=sb.at[t], recv_sem=rb.at[s],
            device_id=(t, cj), device_id_type=MESH)

    def b_start(d, c):
        b_desc(lax.rem(me + d, n), me).start()
        return c
    lax.fori_loop(1, n, b_start, 0)

    def g3(p, mine):
        src = own if mine else kc * half + xc * quarter + p * piece
        return pltpu.make_async_remote_copy(
            src_ref=gath.at[rows(src, piece)], dst_ref=gath.at[rows(src, piece)],
            send_sem=g3s.at[p], recv_sem=g3r.at[zc if mine else p],
            device_id=dev(p, xc, kc), device_id_type=MESH)
    exchange(z_peers, g3)

    def g2(p, mine):
        src = kc * half + (xc if mine else p) * quarter
        return pltpu.make_async_remote_copy(
            src_ref=gath.at[rows(src, quarter)], dst_ref=gath.at[rows(src, quarter)],
            send_sem=g2s.at[p], recv_sem=g2r.at[xc if mine else p],
            device_id=dev(zc, p, kc), device_id_type=MESH)
    for p in x_peers:
        g2(p, True).start()

    def b_wait(d, c):
        b_desc(lax.rem(me + d, n), me).wait_send()
        b_desc(me, lax.rem(me + d, n)).wait_recv()
        return c
    lax.fori_loop(1, n, b_wait, 0)

    def b_add(d, acc):
        return acc + nrm_dp[lax.rem(me + d, n)]
    col = lax.fori_loop(1, n, b_add, nrm_dp[me])
    nrm_cls[cj] = col

    def c_desc(t, s):
        return pltpu.make_async_remote_copy(
            src_ref=nrm_cls.at[s], dst_ref=nrm_cls.at[s],
            send_sem=sc.at[t], recv_sem=rc.at[s],
            device_id=(me, t), device_id_type=MESH)

    for t in c_peers:
        c_desc(t, cj).start()
    for p in x_peers:
        g2(p, True).wait_send()
        g2(p, False).wait_recv()

    def g1(p, mine, c):
        src = (kc if mine else p) * half + c * chunk
        return pltpu.make_async_remote_copy(
            src_ref=gath.at[rows(src, chunk)], dst_ref=gath.at[rows(src, chunk)],
            send_sem=g1s.at[p * nch + c], recv_sem=g1r.at[(kc if mine else p) * nch + c],
            device_id=dev(zc, xc, p), device_id_type=MESH)
    for p in k_peers:
        for c in range(nch):
            g1(p, True, c).start()
    for t in c_peers:
        c_desc(t, cj).wait_send()
        c_desc(cj, t).wait_recv()
    tot = col
    for t in c_peers:
        tot = tot + nrm_cls[t]
    factor = jnp.minimum(1.0, limit / jnp.sqrt(tot))
    for p in k_peers:
        for c in range(nch):
            g1(p, True, c).wait_send()
            g1(p, False, c).wait_recv()
    fac = jnp.broadcast_to(factor[0:1, 0:1], out_ref.shape)
    out_ref[...] = (gath[...].astype(jnp.float32) * fac).astype(out_ref.dtype)


def grad_reduce(stats, z_t, q_t, emb_t, n, ncls, scale, limit, nk=2, nx=4, nch=4):
    nz = n // (nk * nx)
    width = z_t.shape[0]
    total = emb_t.shape[0]
    half = total // nk
    quarter = half // nx
    piece = quarter // nz
    dma = pltpu.SemaphoreType.DMA
    vmem = pl.BlockSpec(memory_space=pltpu.VMEM)
    return pl.pallas_call(
        functools.partial(_grad_kernel, nk, nx, nz, nch, ncls, scale, limit),
        out_shape=jax.ShapeDtypeStruct((total, width), jnp.bfloat16),
        in_specs=[vmem] * 4,
        out_specs=vmem,
        scratch_shapes=[
            pltpu.VMEM((total, width), jnp.float32),
            pltpu.VMEM((ncls,) + stats.shape, jnp.float32),
            pltpu.VMEM((nk, half, width), jnp.float32),
            pltpu.VMEM((half, width), jnp.float32),
            pltpu.VMEM((nx, quarter, width), jnp.float32),
            pltpu.VMEM((quarter, width), jnp.float32),
            pltpu.VMEM((nz, piece, width), jnp.float32),
            pltpu.VMEM((total, width), jnp.bfloat16),
            pltpu.VMEM((n, 8, 128), jnp.float32),
            pltpu.VMEM((ncls, 8, 128), jnp.float32),
            dma((ncls,)), dma((ncls,)),
            dma((nk * nch,)), dma((nk * nch,)), dma((nx,)), dma((nx,)), dma((nz,)), dma((nz,)),
            dma((n,)), dma((n,)), dma((ncls,)), dma((ncls,)),
            dma((nz,)), dma((nz,)), dma((nx,)), dma((nx,)), dma((nk * nch,)), dma((nk * nch,)),
        ],
        compiler_params=pltpu.CompilerParams(collective_id=0, has_side_effects=True),
    )(stats, z_t, q_t, emb_t)


def _class_gather_kernel(ncls, x_ref, out_ref, buf, ssem, rsem):
    me = lax.axis_index("dp")
    cj = lax.axis_index("class")
    peers = [lax.rem(cj + e, ncls) for e in range(1, ncls)]
    barrier = pltpu.get_barrier_semaphore()
    for t in peers:
        pl.semaphore_signal(barrier, 1, device_id=(me, t), device_id_type=MESH)
    pl.semaphore_wait(barrier, ncls - 1)

    def desc(t, s):
        return pltpu.make_async_remote_copy(
            src_ref=x_ref, dst_ref=buf.at[s], send_sem=ssem.at[t], recv_sem=rsem.at[s],
            device_id=(me, t), device_id_type=MESH)
    for t in peers:
        desc(t, cj).start()
    buf[cj] = x_ref[...]
    for t in peers:
        desc(t, cj).wait_send()
        desc(cj, t).wait_recv()
    out_ref[...] = buf[...]


def class_gather(x, ncls, cid):
    dma = pltpu.SemaphoreType.DMA
    return pl.pallas_call(
        functools.partial(_class_gather_kernel, ncls),
        out_shape=jax.ShapeDtypeStruct((ncls,) + x.shape, x.dtype),
        in_specs=[pl.BlockSpec(memory_space=pltpu.VMEM)],
        out_specs=pl.BlockSpec(memory_space=pltpu.VMEM),
        scratch_shapes=[pltpu.VMEM((ncls,) + x.shape, x.dtype), dma((ncls,)), dma((ncls,))],
        compiler_params=pltpu.CompilerParams(collective_id=cid, has_side_effects=True),
    )(x)


def _combine_stats(local_max, local_sum, cid):
    both = class_gather(jnp.stack([local_max, local_sum], axis=0), lax.axis_size("class"), cid)
    maxes, sums = both[:, 0], both[:, 1]
    top = jnp.max(maxes, axis=0)
    total = jnp.sum(sums * jnp.exp(maxes - top[None, :]), axis=0)
    return top, total


def on_device(embeddings, labels, head_weight, send_blocks, nbr_source, nbr_offset, counts):
    rows = embeddings.shape[0]
    width_part = embeddings.shape[1]
    class_part = labels.shape[1]
    dp_count = lax.axis_size("dp")
    nbrs = nbr_source.shape[1]
    picks = send_blocks[0]
    out_emb = embeddings.reshape(rows // BLOCK, BLOCK, width_part)[picks]
    out_lab = labels.reshape(rows // BLOCK, BLOCK, class_part)[picks]
    pool_emb = lax.all_to_all(out_emb, "dp", split_axis=0, concat_axis=0, tiled=True)
    pool_lab = lax.all_to_all(out_lab, "dp", split_axis=0, concat_axis=0, tiled=True)
    pool_rows = dp_count * BLOCK
    pool_emb = pool_emb.reshape(pool_rows, width_part)
    pool_lab = pool_lab.reshape(pool_rows, class_part)
    located = nbr_source * BLOCK + nbr_offset

    ncls = lax.axis_size("class")
    emb_all = class_gather(embeddings, ncls, 3)
    full_emb = jnp.transpose(emb_all, (1, 0, 2)).reshape(rows, ncls * width_part)
    head = jnp.dot(full_emb, head_weight, preferred_element_type=jnp.float32)
    h_max = jnp.max(head, axis=1)
    h_sum = jnp.sum(jnp.exp(head - h_max[:, None]), axis=1)

    near = pool_emb[located]
    partial_value = jnp.einsum(
        "rd,rkd->kr", embeddings, near, preferred_element_type=jnp.float32
    )
    packed = class_gather(
        jnp.concatenate([partial_value, h_max[None, :], h_sum[None, :]], axis=0), ncls, 1
    )
    scores = jnp.sum(packed[:, :nbrs], axis=0).T
    h_maxes, h_sums = packed[:, nbrs], packed[:, nbrs + 1]
    h_top = jnp.max(h_maxes, axis=0)
    h_total = jnp.sum(h_sums * jnp.exp(h_maxes - h_top[None, :]), axis=0)
    prob_head = jnp.exp(head - h_top[:, None]) / h_total[:, None]
    valid = lax.broadcasted_iota(jnp.int32, (rows, nbrs), 1) < counts[:, None]
    logits = jnp.where(valid, scores / math.sqrt(D), -1e30)
    top = jnp.max(logits, axis=1, keepdims=True)
    expd = jnp.where(valid, jnp.exp(logits - top), 0.0)
    weights = (expd / jnp.sum(expd, axis=1, keepdims=True)).astype(jnp.bfloat16)

    row_ids = lax.broadcasted_iota(jnp.int32, (rows, nbrs), 0)
    dense = jnp.zeros((rows, pool_rows), jnp.float32).at[row_ids, located].add(
        weights.astype(jnp.float32)
    )
    dense_hi = dense.astype(jnp.bfloat16)
    dense_lo = (dense - dense_hi.astype(jnp.float32)).astype(jnp.bfloat16)
    stacked = lax.optimization_barrier(jnp.concatenate([dense_hi, dense_lo], axis=0))
    both = jnp.dot(stacked, pool_lab, preferred_element_type=jnp.float32)
    spread = both[:rows] + both[rows:]
    target = 4.0 * spread + labels.astype(jnp.float32)
    z_local = jnp.max(target, axis=1)
    z_sum = jnp.sum(jnp.exp(target - z_local[:, None]), axis=1)
    scale = 1.0 / math.sqrt(rows * dp_count)
    limit = 0.5 * math.sqrt(D * C)
    head_grad = grad_reduce(
        jnp.stack([z_local, z_sum], axis=0), target.T, prob_head.T, full_emb.T,
        dp_count, lax.axis_size("class"), scale, limit,
    )
    return (target.astype(jnp.bfloat16), head_grad)


def solution(mesh):
    return jax.shard_map(
        on_device,
        mesh=mesh,
        in_specs=(
            P("dp", "class"),
            P("dp", "class"),
            P(None, "class"),
            P("dp", None),
            P("dp", None),
            P("dp", None),
            P("dp"),
        ),
        out_specs=(P("dp", "class"), P(None, "class")),
        check_vma=False,
    )
```

```python
import math

import jax
import jax.numpy as jnp
from jax import lax
from jax.experimental import pallas as pl
from jax.experimental.pallas import tpu as pltpu
from jax.sharding import PartitionSpec as P
import functools

D = 1024
C = 4096
BLOCK = 128

MESH = pl.DeviceIdType.MESH

def _grad_kernel(nk, nx, nz, nch, ncls, scale, limit, stats_ref, zt_ref, qt_ref, embt_ref,
                 out_ref, fac_ref, part_ref, sbuf, recv1, acc1, recv2, acc2, recv3, gath, nrm_dp, nrm_cls,
                 ss, rs, s1, r1, s2, r2, s3, r3, sb, rb, sc, rc, g3s, g3r, g2s, g2r, g1s, g1r):
    n = nk * nx * nz
    me = lax.axis_index("dp")
    cj = lax.axis_index("class")
    kc = lax.rem(me, nk)
    xc = lax.rem(me // nk, nx)
    zc = me // (nk * nx)
    total = part_ref.shape[0]
    half = total // nk
    quarter = half // nx
    piece = quarter // nz

    def dev(z, x, k):
        return ((z * nx + x) * nk + k, cj)

    def rows(start, size):
        return pl.ds(pl.multiple_of(start, size), size)

    barrier = pltpu.get_barrier_semaphore()

    def greet(d, c):
        pl.semaphore_signal(barrier, 1, device_id=(lax.rem(me + d, n), cj), device_id_type=MESH)
        return c
    lax.fori_loop(1, n, greet, 0)
    for e in range(1, ncls):
        pl.semaphore_signal(barrier, 1, device_id=(me, lax.rem(cj + e, ncls)), device_id_type=MESH)
    pl.semaphore_wait(barrier, n - 1 + ncls - 1)

    c_peers = [lax.rem(cj + e, ncls) for e in range(1, ncls)]

    def st_desc(t, s):
        return pltpu.make_async_remote_copy(
            src_ref=stats_ref, dst_ref=sbuf.at[s], send_sem=ss.at[t], recv_sem=rs.at[s],
            device_id=(me, t), device_id_type=MESH)
    for t in c_peers:
        st_desc(t, cj).start()
    sbuf[cj] = stats_ref[...]
    for t in c_peers:
        st_desc(t, cj).wait_send()
        st_desc(cj, t).wait_recv()
    top = sbuf[0, 0:1, :]
    for e in range(1, ncls):
        top = jnp.maximum(top, sbuf[e, 0:1, :])
    tot_exp = sbuf[0, 1:2, :] * jnp.exp(sbuf[0, 0:1, :] - top)
    for e in range(1, ncls):
        tot_exp = tot_exp + sbuf[e, 1:2, :] * jnp.exp(sbuf[e, 0:1, :] - top)
    prob_t = jnp.exp(zt_ref[...] - top) / tot_exp
    diff_t = (qt_ref.shape[0] * ncls * (qt_ref[...] - prob_t)).astype(jnp.bfloat16)
    part_ref[...] = lax.dot_general(
        embt_ref[...], diff_t, (((1,), (1,)), ((), ())), preferred_element_type=jnp.float32)

    def exchange(peers, make):
        for p in peers:
            make(p, True).start()
        for p in peers:
            make(p, True).wait_send()
            make(p, False).wait_recv()

    k_peers = [lax.rem(kc + e, nk) for e in range(1, nk)]

    chunk = half // nch

    def m1(p, mine, c):
        part = rows(c * chunk, chunk)
        if mine:
            return pltpu.make_async_remote_copy(
                src_ref=part_ref.at[rows(p * half + c * chunk, chunk)], dst_ref=recv1.at[kc, part],
                send_sem=s1.at[p * nch + c], recv_sem=r1.at[kc * nch + c],
                device_id=dev(zc, xc, p), device_id_type=MESH)
        return pltpu.make_async_remote_copy(
            src_ref=part_ref.at[rows(kc * half + c * chunk, chunk)], dst_ref=recv1.at[p, part],
            send_sem=s1.at[kc * nch + c], recv_sem=r1.at[p * nch + c],
            device_id=dev(zc, xc, p), device_id_type=MESH)
    for p in k_peers:
        for c in range(nch):
            m1(p, True, c).start()
    for p in k_peers:
        for c in range(nch):
            m1(p, True, c).wait_send()
            m1(p, False, c).wait_recv()
    a1 = part_ref[rows(kc * half, half), :]
    for p in k_peers:
        a1 = a1 + recv1[p]
    acc1[...] = a1

    x_peers = [lax.rem(xc + e, nx) for e in range(1, nx)]

    def m2(p, mine):
        if mine:
            return pltpu.make_async_remote_copy(
                src_ref=acc1.at[rows(p * quarter, quarter)], dst_ref=recv2.at[xc],
                send_sem=s2.at[p], recv_sem=r2.at[xc], device_id=dev(zc, p, kc), device_id_type=MESH)
        return pltpu.make_async_remote_copy(
            src_ref=acc1.at[rows(xc * quarter, quarter)], dst_ref=recv2.at[p],
            send_sem=s2.at[xc], recv_sem=r2.at[p], device_id=dev(zc, p, kc), device_id_type=MESH)
    exchange(x_peers, m2)
    a2 = acc1[rows(xc * quarter, quarter), :]
    for p in x_peers:
        a2 = a2 + recv2[p]
    acc2[...] = a2

    z_peers = [lax.rem(zc + e, nz) for e in range(1, nz)]

    def m3(p, mine):
        if mine:
            return pltpu.make_async_remote_copy(
                src_ref=acc2.at[rows(p * piece, piece)], dst_ref=recv3.at[zc],
                send_sem=s3.at[p], recv_sem=r3.at[zc], device_id=dev(p, xc, kc), device_id_type=MESH)
        return pltpu.make_async_remote_copy(
            src_ref=acc2.at[rows(zc * piece, piece)], dst_ref=recv3.at[p],
            send_sem=s3.at[zc], recv_sem=r3.at[p], device_id=dev(p, xc, kc), device_id_type=MESH)
    exchange(z_peers, m3)
    a3 = acc2[rows(zc * piece, piece), :]
    for p in z_peers:
        a3 = a3 + recv3[p]
    summed = a3 * scale
    own = kc * half + xc * quarter + zc * piece
    gath[rows(own, piece), :] = summed.astype(gath.dtype)

    sq = jnp.sum(summed * summed, axis=(0, 1), keepdims=True)
    nrm_dp[me] = jnp.broadcast_to(sq, nrm_dp.shape[1:])

    def b_desc(t, s):
        return pltpu.make_async_remote_copy(
            src_ref=nrm_dp.at[s], dst_ref=nrm_dp.at[s],
            send_sem=sb.at[t], recv_sem=rb.at[s],
            device_id=(t, cj), device_id_type=MESH)

    def b_start(d, c):
        b_desc(lax.rem(me + d, n), me).start()
        return c
    lax.fori_loop(1, n, b_start, 0)

    def g3(p, mine):
        src = own if mine else kc * half + xc * quarter + p * piece
        return pltpu.make_async_remote_copy(
            src_ref=gath.at[rows(src, piece)], dst_ref=gath.at[rows(src, piece)],
            send_sem=g3s.at[p], recv_sem=g3r.at[zc if mine else p],
            device_id=dev(p, xc, kc), device_id_type=MESH)
    exchange(z_peers, g3)

    def g2(p, mine):
        src = kc * half + (xc if mine else p) * quarter
        return pltpu.make_async_remote_copy(
            src_ref=gath.at[rows(src, quarter)], dst_ref=gath.at[rows(src, quarter)],
            send_sem=g2s.at[p], recv_sem=g2r.at[xc if mine else p],
            device_id=dev(zc, p, kc), device_id_type=MESH)
    for p in x_peers:
        g2(p, True).start()

    def b_wait(d, c):
        b_desc(lax.rem(me + d, n), me).wait_send()
        b_desc(me, lax.rem(me + d, n)).wait_recv()
        return c
    lax.fori_loop(1, n, b_wait, 0)

    def b_add(d, acc):
        return acc + nrm_dp[lax.rem(me + d, n)]
    col = lax.fori_loop(1, n, b_add, nrm_dp[me])
    nrm_cls[cj] = col

    def c_desc(t, s):
        return pltpu.make_async_remote_copy(
            src_ref=nrm_cls.at[s], dst_ref=nrm_cls.at[s],
            send_sem=sc.at[t], recv_sem=rc.at[s],
            device_id=(me, t), device_id_type=MESH)

    for t in c_peers:
        c_desc(t, cj).start()
    for p in x_peers:
        g2(p, True).wait_send()
        g2(p, False).wait_recv()

    def g1(p, mine, c):
        src = (kc if mine else p) * half + c * chunk
        return pltpu.make_async_remote_copy(
            src_ref=gath.at[rows(src, chunk)], dst_ref=gath.at[rows(src, chunk)],
            send_sem=g1s.at[p * nch + c], recv_sem=g1r.at[(kc if mine else p) * nch + c],
            device_id=dev(zc, xc, p), device_id_type=MESH)
    for p in k_peers:
        for c in range(nch):
            g1(p, True, c).start()
    for t in c_peers:
        c_desc(t, cj).wait_send()
        c_desc(cj, t).wait_recv()
    tot = col
    for t in c_peers:
        tot = tot + nrm_cls[t]
    factor = jnp.minimum(1.0, limit / jnp.sqrt(tot))
    for p in k_peers:
        for c in range(nch):
            g1(p, True, c).wait_send()
            g1(p, False, c).wait_recv()
    fac_ref[...] = jnp.broadcast_to(factor[0:1, 0:1], fac_ref.shape)
    out_ref[...] = gath[...]


def grad_reduce(stats, z_t, q_t, emb_t, n, ncls, scale, limit, nk=2, nx=4, nch=4):
    nz = n // (nk * nx)
    width = z_t.shape[0]
    total = emb_t.shape[0]
    half = total // nk
    quarter = half // nx
    piece = quarter // nz
    dma = pltpu.SemaphoreType.DMA
    vmem = pl.BlockSpec(memory_space=pltpu.VMEM)
    return pl.pallas_call(
        functools.partial(_grad_kernel, nk, nx, nz, nch, ncls, scale, limit),
        out_shape=(
            jax.ShapeDtypeStruct((total, width), jnp.bfloat16),
            jax.ShapeDtypeStruct((8, 128), jnp.float32),
        ),
        in_specs=[vmem] * 4,
        out_specs=(vmem, vmem),
        scratch_shapes=[
            pltpu.VMEM((total, width), jnp.float32),
            pltpu.VMEM((ncls,) + stats.shape, jnp.float32),
            pltpu.VMEM((nk, half, width), jnp.float32),
            pltpu.VMEM((half, width), jnp.float32),
            pltpu.VMEM((nx, quarter, width), jnp.float32),
            pltpu.VMEM((quarter, width), jnp.float32),
            pltpu.VMEM((nz, piece, width), jnp.float32),
            pltpu.VMEM((total, width), jnp.bfloat16),
            pltpu.VMEM((n, 8, 128), jnp.float32),
            pltpu.VMEM((ncls, 8, 128), jnp.float32),
            dma((ncls,)), dma((ncls,)),
            dma((nk * nch,)), dma((nk * nch,)), dma((nx,)), dma((nx,)), dma((nz,)), dma((nz,)),
            dma((n,)), dma((n,)), dma((ncls,)), dma((ncls,)),
            dma((nz,)), dma((nz,)), dma((nx,)), dma((nx,)), dma((nk * nch,)), dma((nk * nch,)),
        ],
        compiler_params=pltpu.CompilerParams(collective_id=0, has_side_effects=True),
    )(stats, z_t, q_t, emb_t)


def _class_gather_kernel(ncls, x_ref, out_ref, buf, ssem, rsem):
    me = lax.axis_index("dp")
    cj = lax.axis_index("class")
    peers = [lax.rem(cj + e, ncls) for e in range(1, ncls)]
    barrier = pltpu.get_barrier_semaphore()
    for t in peers:
        pl.semaphore_signal(barrier, 1, device_id=(me, t), device_id_type=MESH)
    pl.semaphore_wait(barrier, ncls - 1)

    def desc(t, s):
        return pltpu.make_async_remote_copy(
            src_ref=x_ref, dst_ref=buf.at[s], send_sem=ssem.at[t], recv_sem=rsem.at[s],
            device_id=(me, t), device_id_type=MESH)
    for t in peers:
        desc(t, cj).start()
    buf[cj] = x_ref[...]
    for t in peers:
        desc(t, cj).wait_send()
        desc(cj, t).wait_recv()
    out_ref[...] = buf[...]


def class_gather(x, ncls, cid):
    dma = pltpu.SemaphoreType.DMA
    return pl.pallas_call(
        functools.partial(_class_gather_kernel, ncls),
        out_shape=jax.ShapeDtypeStruct((ncls,) + x.shape, x.dtype),
        in_specs=[pl.BlockSpec(memory_space=pltpu.VMEM)],
        out_specs=pl.BlockSpec(memory_space=pltpu.VMEM),
        scratch_shapes=[pltpu.VMEM((ncls,) + x.shape, x.dtype), dma((ncls,)), dma((ncls,))],
        compiler_params=pltpu.CompilerParams(collective_id=cid, has_side_effects=True),
    )(x)


def _combine_stats(local_max, local_sum, cid):
    both = class_gather(jnp.stack([local_max, local_sum], axis=0), lax.axis_size("class"), cid)
    maxes, sums = both[:, 0], both[:, 1]
    top = jnp.max(maxes, axis=0)
    total = jnp.sum(sums * jnp.exp(maxes - top[None, :]), axis=0)
    return top, total


def on_device(embeddings, labels, head_weight, send_blocks, nbr_source, nbr_offset, counts):
    rows = embeddings.shape[0]
    width_part = embeddings.shape[1]
    class_part = labels.shape[1]
    dp_count = lax.axis_size("dp")
    nbrs = nbr_source.shape[1]
    picks = send_blocks[0]
    out_emb = embeddings.reshape(rows // BLOCK, BLOCK, width_part)[picks]
    out_lab = labels.reshape(rows // BLOCK, BLOCK, class_part)[picks]
    pool_emb = lax.all_to_all(out_emb, "dp", split_axis=0, concat_axis=0, tiled=True)
    pool_lab = lax.all_to_all(out_lab, "dp", split_axis=0, concat_axis=0, tiled=True)
    pool_rows = dp_count * BLOCK
    pool_emb = pool_emb.reshape(pool_rows, width_part)
    pool_lab = pool_lab.reshape(pool_rows, class_part)
    located = nbr_source * BLOCK + nbr_offset

    full_emb = lax.all_gather(embeddings, "class", axis=1, tiled=True)
    head = jnp.dot(full_emb, head_weight, preferred_element_type=jnp.float32)
    h_top, h_total = _combine_stats(
        jnp.max(head, axis=1),
        jnp.sum(jnp.exp(head - jnp.max(head, axis=1, keepdims=True)), axis=1),
        1,
    )
    prob_head = jnp.exp(head - h_top[:, None]) / h_total[:, None]

    near = pool_emb[located]
    partial_value = jnp.einsum(
        "rd,rkd->rk", embeddings, near, preferred_element_type=jnp.float32
    )
    scores = lax.psum(partial_value, "class")
    valid = lax.broadcasted_iota(jnp.int32, (rows, nbrs), 1) < counts[:, None]
    logits = jnp.where(valid, scores / math.sqrt(D), -1e30)
    top = jnp.max(logits, axis=1, keepdims=True)
    expd = jnp.where(valid, jnp.exp(logits - top), 0.0)
    weights = (expd / jnp.sum(expd, axis=1, keepdims=True)).astype(jnp.bfloat16)

    row_ids = lax.broadcasted_iota(jnp.int32, (rows, nbrs), 0)
    dense = jnp.zeros((rows, pool_rows), jnp.float32).at[row_ids, located].add(
        weights.astype(jnp.float32)
    )
    dense_hi = dense.astype(jnp.bfloat16)
    dense_lo = (dense - dense_hi.astype(jnp.float32)).astype(jnp.bfloat16)
    stacked = lax.optimization_barrier(jnp.concatenate([dense_hi, dense_lo], axis=0))
    both = jnp.dot(stacked, pool_lab, preferred_element_type=jnp.float32)
    spread = both[:rows] + both[rows:]
    target = 4.0 * spread + labels.astype(jnp.float32)
    z_local = jnp.max(target, axis=1)
    z_sum = jnp.sum(jnp.exp(target - z_local[:, None]), axis=1)
    scale = 1.0 / math.sqrt(rows * dp_count)
    limit = 0.5 * math.sqrt(D * C)
    gathered, factor = grad_reduce(
        jnp.stack([z_local, z_sum], axis=0), target.T, prob_head.T, full_emb.T,
        dp_count, lax.axis_size("class"), scale, limit,
    )
    head_grad = (gathered.astype(jnp.float32) * factor[0, 0]).astype(jnp.bfloat16)
    return (target.astype(jnp.bfloat16), head_grad)


def solution(mesh):
    return jax.shard_map(
        on_device,
        mesh=mesh,
        in_specs=(
            P("dp", "class"),
            P("dp", "class"),
            P(None, "class"),
            P("dp", None),
            P("dp", None),
            P("dp", None),
            P("dp"),
        ),
        out_specs=(P("dp", "class"), P(None, "class")),
        check_vma=False,
    )
```

```python
import math

import jax
import jax.numpy as jnp
from jax import lax
from jax.experimental import pallas as pl
from jax.experimental.pallas import tpu as pltpu
from jax.sharding import PartitionSpec as P
import functools

D = 1024
C = 4096
BLOCK = 128

MESH = pl.DeviceIdType.MESH

def _grad_kernel(nk, nx, nz, nch, ncls, scale, limit, zt_ref, qt_ref, embt_ref,
                 out_ref, part_ref, sbuf, recv1, acc1, recv2, acc2, recv3, gath, nrm_dp, nrm_cls,
                 ss, rs, s1, r1, s2, r2, s3, r3, sb, rb, sc, rc, g3s, g3r, g2s, g2r, g1s, g1r):
    n = nk * nx * nz
    me = lax.axis_index("dp")
    cj = lax.axis_index("class")
    kc = lax.rem(me, nk)
    xc = lax.rem(me // nk, nx)
    zc = me // (nk * nx)
    total = part_ref.shape[0]
    half = total // nk
    quarter = half // nx
    piece = quarter // nz

    def dev(z, x, k):
        return ((z * nx + x) * nk + k, cj)

    def rows(start, size):
        return pl.ds(pl.multiple_of(start, size), size)

    barrier = pltpu.get_barrier_semaphore()

    def greet(d, c):
        pl.semaphore_signal(barrier, 1, device_id=(lax.rem(me + d, n), cj), device_id_type=MESH)
        return c
    lax.fori_loop(1, n, greet, 0)
    for e in range(1, ncls):
        pl.semaphore_signal(barrier, 1, device_id=(me, lax.rem(cj + e, ncls)), device_id_type=MESH)
    pl.semaphore_wait(barrier, n - 1 + ncls - 1)

    c_peers = [lax.rem(cj + e, ncls) for e in range(1, ncls)]

    z_t = zt_ref[...]
    z_max = jnp.max(z_t, axis=0, keepdims=True)
    sbuf[cj, 0:1, :] = z_max
    sbuf[cj, 1:2, :] = jnp.sum(jnp.exp(z_t - z_max), axis=0, keepdims=True)

    def st_desc(t, s):
        return pltpu.make_async_remote_copy(
            src_ref=sbuf.at[s], dst_ref=sbuf.at[s], send_sem=ss.at[t], recv_sem=rs.at[s],
            device_id=(me, t), device_id_type=MESH)
    for t in c_peers:
        st_desc(t, cj).start()
    for t in c_peers:
        st_desc(t, cj).wait_send()
        st_desc(cj, t).wait_recv()
    top = sbuf[0, 0:1, :]
    for e in range(1, ncls):
        top = jnp.maximum(top, sbuf[e, 0:1, :])
    tot_exp = sbuf[0, 1:2, :] * jnp.exp(sbuf[0, 0:1, :] - top)
    for e in range(1, ncls):
        tot_exp = tot_exp + sbuf[e, 1:2, :] * jnp.exp(sbuf[e, 0:1, :] - top)
    prob_t = jnp.exp(zt_ref[...] - top) / tot_exp
    diff_t = (qt_ref.shape[0] * ncls * (qt_ref[...] - prob_t)).astype(jnp.bfloat16)
    part_ref[...] = lax.dot_general(
        embt_ref[...], diff_t, (((1,), (1,)), ((), ())), preferred_element_type=jnp.float32)

    def exchange(peers, make):
        for p in peers:
            make(p, True).start()
        for p in peers:
            make(p, True).wait_send()
            make(p, False).wait_recv()

    k_peers = [lax.rem(kc + e, nk) for e in range(1, nk)]

    chunk = half // nch

    def m1(p, mine, c):
        part = rows(c * chunk, chunk)
        if mine:
            return pltpu.make_async_remote_copy(
                src_ref=part_ref.at[rows(p * half + c * chunk, chunk)], dst_ref=recv1.at[kc, part],
                send_sem=s1.at[p * nch + c], recv_sem=r1.at[kc * nch + c],
                device_id=dev(zc, xc, p), device_id_type=MESH)
        return pltpu.make_async_remote_copy(
            src_ref=part_ref.at[rows(kc * half + c * chunk, chunk)], dst_ref=recv1.at[p, part],
            send_sem=s1.at[kc * nch + c], recv_sem=r1.at[p * nch + c],
            device_id=dev(zc, xc, p), device_id_type=MESH)
    for p in k_peers:
        for c in range(nch):
            m1(p, True, c).start()
    for p in k_peers:
        for c in range(nch):
            m1(p, True, c).wait_send()
            m1(p, False, c).wait_recv()
    a1 = part_ref[rows(kc * half, half), :]
    for p in k_peers:
        a1 = a1 + recv1[p]
    acc1[...] = a1

    x_peers = [lax.rem(xc + e, nx) for e in range(1, nx)]

    def m2(p, mine):
        if mine:
            return pltpu.make_async_remote_copy(
                src_ref=acc1.at[rows(p * quarter, quarter)], dst_ref=recv2.at[xc],
                send_sem=s2.at[p], recv_sem=r2.at[xc], device_id=dev(zc, p, kc), device_id_type=MESH)
        return pltpu.make_async_remote_copy(
            src_ref=acc1.at[rows(xc * quarter, quarter)], dst_ref=recv2.at[p],
            send_sem=s2.at[xc], recv_sem=r2.at[p], device_id=dev(zc, p, kc), device_id_type=MESH)
    exchange(x_peers, m2)
    a2 = acc1[rows(xc * quarter, quarter), :]
    for p in x_peers:
        a2 = a2 + recv2[p]
    acc2[...] = a2

    z_peers = [lax.rem(zc + e, nz) for e in range(1, nz)]

    def m3(p, mine):
        if mine:
            return pltpu.make_async_remote_copy(
                src_ref=acc2.at[rows(p * piece, piece)], dst_ref=recv3.at[zc],
                send_sem=s3.at[p], recv_sem=r3.at[zc], device_id=dev(p, xc, kc), device_id_type=MESH)
        return pltpu.make_async_remote_copy(
            src_ref=acc2.at[rows(zc * piece, piece)], dst_ref=recv3.at[p],
            send_sem=s3.at[zc], recv_sem=r3.at[p], device_id=dev(p, xc, kc), device_id_type=MESH)
    exchange(z_peers, m3)
    a3 = acc2[rows(zc * piece, piece), :]
    for p in z_peers:
        a3 = a3 + recv3[p]
    summed = a3 * scale
    own = kc * half + xc * quarter + zc * piece
    gath[rows(own, piece), :] = summed.astype(gath.dtype)

    sq = jnp.sum(summed * summed, axis=(0, 1), keepdims=True)
    nrm_dp[me] = jnp.broadcast_to(sq, nrm_dp.shape[1:])

    def b_desc(t, s):
        return pltpu.make_async_remote_copy(
            src_ref=nrm_dp.at[s], dst_ref=nrm_dp.at[s],
            send_sem=sb.at[t], recv_sem=rb.at[s],
            device_id=(t, cj), device_id_type=MESH)

    def b_start(d, c):
        b_desc(lax.rem(me + d, n), me).start()
        return c
    lax.fori_loop(1, n, b_start, 0)

    def g3(p, mine):
        src = own if mine else kc * half + xc * quarter + p * piece
        return pltpu.make_async_remote_copy(
            src_ref=gath.at[rows(src, piece)], dst_ref=gath.at[rows(src, piece)],
            send_sem=g3s.at[p], recv_sem=g3r.at[zc if mine else p],
            device_id=dev(p, xc, kc), device_id_type=MESH)
    exchange(z_peers, g3)

    def g2(p, mine):
        src = kc * half + (xc if mine else p) * quarter
        return pltpu.make_async_remote_copy(
            src_ref=gath.at[rows(src, quarter)], dst_ref=gath.at[rows(src, quarter)],
            send_sem=g2s.at[p], recv_sem=g2r.at[xc if mine else p],
            device_id=dev(zc, p, kc), device_id_type=MESH)
    for p in x_peers:
        g2(p, True).start()

    def b_wait(d, c):
        b_desc(lax.rem(me + d, n), me).wait_send()
        b_desc(me, lax.rem(me + d, n)).wait_recv()
        return c
    lax.fori_loop(1, n, b_wait, 0)

    def b_add(d, acc):
        return acc + nrm_dp[lax.rem(me + d, n)]
    col = lax.fori_loop(1, n, b_add, nrm_dp[me])
    nrm_cls[cj] = col

    def c_desc(t, s):
        return pltpu.make_async_remote_copy(
            src_ref=nrm_cls.at[s], dst_ref=nrm_cls.at[s],
            send_sem=sc.at[t], recv_sem=rc.at[s],
            device_id=(me, t), device_id_type=MESH)

    for t in c_peers:
        c_desc(t, cj).start()
    for p in x_peers:
        g2(p, True).wait_send()
        g2(p, False).wait_recv()

    def g1(p, mine, c):
        src = (kc if mine else p) * half + c * chunk
        return pltpu.make_async_remote_copy(
            src_ref=gath.at[rows(src, chunk)], dst_ref=gath.at[rows(src, chunk)],
            send_sem=g1s.at[p * nch + c], recv_sem=g1r.at[(kc if mine else p) * nch + c],
            device_id=dev(zc, xc, p), device_id_type=MESH)
    for p in k_peers:
        for c in range(nch):
            g1(p, True, c).start()
    for t in c_peers:
        c_desc(t, cj).wait_send()
        c_desc(cj, t).wait_recv()
    tot = col
    for t in c_peers:
        tot = tot + nrm_cls[t]
    factor = jnp.minimum(1.0, limit / jnp.sqrt(tot))
    for p in k_peers:
        for c in range(nch):
            g1(p, True, c).wait_send()
            g1(p, False, c).wait_recv()
    fac = jnp.broadcast_to(factor[0:1, 0:1], out_ref.shape)
    out_ref[...] = (gath[...].astype(jnp.float32) * fac).astype(out_ref.dtype)


def grad_reduce(z_t, q_t, emb_t, n, ncls, scale, limit, nk=2, nx=4, nch=4):
    nz = n // (nk * nx)
    width = z_t.shape[0]
    total = emb_t.shape[0]
    half = total // nk
    quarter = half // nx
    piece = quarter // nz
    dma = pltpu.SemaphoreType.DMA
    vmem = pl.BlockSpec(memory_space=pltpu.VMEM)
    return pl.pallas_call(
        functools.partial(_grad_kernel, nk, nx, nz, nch, ncls, scale, limit),
        out_shape=jax.ShapeDtypeStruct((total, width), jnp.bfloat16),
        in_specs=[vmem] * 3,
        out_specs=vmem,
        scratch_shapes=[
            pltpu.VMEM((total, width), jnp.float32),
            pltpu.VMEM((ncls, 2, z_t.shape[1]), jnp.float32),
            pltpu.VMEM((nk, half, width), jnp.float32),
            pltpu.VMEM((half, width), jnp.float32),
            pltpu.VMEM((nx, quarter, width), jnp.float32),
            pltpu.VMEM((quarter, width), jnp.float32),
            pltpu.VMEM((nz, piece, width), jnp.float32),
            pltpu.VMEM((total, width), jnp.bfloat16),
            pltpu.VMEM((n, 8, 128), jnp.float32),
            pltpu.VMEM((ncls, 8, 128), jnp.float32),
            dma((ncls,)), dma((ncls,)),
            dma((nk * nch,)), dma((nk * nch,)), dma((nx,)), dma((nx,)), dma((nz,)), dma((nz,)),
            dma((n,)), dma((n,)), dma((ncls,)), dma((ncls,)),
            dma((nz,)), dma((nz,)), dma((nx,)), dma((nx,)), dma((nk * nch,)), dma((nk * nch,)),
        ],
        compiler_params=pltpu.CompilerParams(collective_id=0, has_side_effects=True),
    )(z_t, q_t, emb_t)


def _class_gather_kernel(ncls, x_ref, out_ref, buf, ssem, rsem):
    me = lax.axis_index("dp")
    cj = lax.axis_index("class")
    peers = [lax.rem(cj + e, ncls) for e in range(1, ncls)]
    barrier = pltpu.get_barrier_semaphore()
    for t in peers:
        pl.semaphore_signal(barrier, 1, device_id=(me, t), device_id_type=MESH)
    pl.semaphore_wait(barrier, ncls - 1)

    def desc(t, s):
        return pltpu.make_async_remote_copy(
            src_ref=x_ref, dst_ref=buf.at[s], send_sem=ssem.at[t], recv_sem=rsem.at[s],
            device_id=(me, t), device_id_type=MESH)
    for t in peers:
        desc(t, cj).start()
    buf[cj] = x_ref[...]
    for t in peers:
        desc(t, cj).wait_send()
        desc(cj, t).wait_recv()
    out_ref[...] = buf[...]


def class_gather(x, ncls, cid):
    dma = pltpu.SemaphoreType.DMA
    return pl.pallas_call(
        functools.partial(_class_gather_kernel, ncls),
        out_shape=jax.ShapeDtypeStruct((ncls,) + x.shape, x.dtype),
        in_specs=[pl.BlockSpec(memory_space=pltpu.VMEM)],
        out_specs=pl.BlockSpec(memory_space=pltpu.VMEM),
        scratch_shapes=[pltpu.VMEM((ncls,) + x.shape, x.dtype), dma((ncls,)), dma((ncls,))],
        compiler_params=pltpu.CompilerParams(collective_id=cid, has_side_effects=True),
    )(x)


def _combine_stats(local_max, local_sum, cid):
    both = class_gather(jnp.stack([local_max, local_sum], axis=0), lax.axis_size("class"), cid)
    maxes, sums = both[:, 0], both[:, 1]
    top = jnp.max(maxes, axis=0)
    total = jnp.sum(sums * jnp.exp(maxes - top[None, :]), axis=0)
    return top, total


def on_device(embeddings, labels, head_weight, send_blocks, nbr_source, nbr_offset, counts):
    rows = embeddings.shape[0]
    width_part = embeddings.shape[1]
    class_part = labels.shape[1]
    dp_count = lax.axis_size("dp")
    nbrs = nbr_source.shape[1]
    picks = send_blocks[0]
    out_emb = embeddings.reshape(rows // BLOCK, BLOCK, width_part)[picks]
    out_lab = labels.reshape(rows // BLOCK, BLOCK, class_part)[picks]
    pool_emb = lax.all_to_all(out_emb, "dp", split_axis=0, concat_axis=0, tiled=True)
    pool_lab = lax.all_to_all(out_lab, "dp", split_axis=0, concat_axis=0, tiled=True)
    pool_rows = dp_count * BLOCK
    pool_emb = pool_emb.reshape(pool_rows, width_part)
    pool_lab = pool_lab.reshape(pool_rows, class_part)
    located = nbr_source * BLOCK + nbr_offset

    full_emb = lax.all_gather(embeddings, "class", axis=1, tiled=True)
    head = jnp.dot(full_emb, head_weight, preferred_element_type=jnp.float32)
    h_top, h_total = _combine_stats(
        jnp.max(head, axis=1),
        jnp.sum(jnp.exp(head - jnp.max(head, axis=1, keepdims=True)), axis=1),
        1,
    )
    prob_head = jnp.exp(head - h_top[:, None]) / h_total[:, None]

    near = pool_emb[located]
    partial_value = jnp.einsum(
        "rd,rkd->rk", embeddings, near, preferred_element_type=jnp.float32
    )
    scores = lax.psum(partial_value, "class")
    valid = lax.broadcasted_iota(jnp.int32, (rows, nbrs), 1) < counts[:, None]
    logits = jnp.where(valid, scores / math.sqrt(D), -1e30)
    top = jnp.max(logits, axis=1, keepdims=True)
    expd = jnp.where(valid, jnp.exp(logits - top), 0.0)
    weights = (expd / jnp.sum(expd, axis=1, keepdims=True)).astype(jnp.bfloat16)

    row_ids = lax.broadcasted_iota(jnp.int32, (rows, nbrs), 0)
    dense = jnp.zeros((rows, pool_rows), jnp.float32).at[row_ids, located].add(
        weights.astype(jnp.float32)
    )
    dense_hi = dense.astype(jnp.bfloat16)
    dense_lo = (dense - dense_hi.astype(jnp.float32)).astype(jnp.bfloat16)
    stacked = lax.optimization_barrier(jnp.concatenate([dense_hi, dense_lo], axis=0))
    both = jnp.dot(stacked, pool_lab, preferred_element_type=jnp.float32)
    spread = both[:rows] + both[rows:]
    target = 4.0 * spread + labels.astype(jnp.float32)
    scale = 1.0 / math.sqrt(rows * dp_count)
    limit = 0.5 * math.sqrt(D * C)
    head_grad = grad_reduce(
        target.T, prob_head.T, full_emb.T,
        dp_count, lax.axis_size("class"), scale, limit,
    )
    return (target.astype(jnp.bfloat16), head_grad)


def solution(mesh):
    return jax.shard_map(
        on_device,
        mesh=mesh,
        in_specs=(
            P("dp", "class"),
            P("dp", "class"),
            P(None, "class"),
            P("dp", None),
            P("dp", None),
            P("dp", None),
            P("dp"),
        ),
        out_specs=(P("dp", "class"), P(None, "class")),
        check_vma=False,
    )
```

```python
import math

import jax
import jax.numpy as jnp
from jax import lax
from jax.experimental import pallas as pl
from jax.experimental.pallas import tpu as pltpu
from jax.sharding import PartitionSpec as P
import functools

D = 1024
C = 4096
BLOCK = 128

MESH = pl.DeviceIdType.MESH

def _grad_kernel(nk, nx, nz, nch, ncls, scale, limit, stats_ref, zt_ref, qt_ref, embt_ref,
                 out_ref, part_ref, sbuf, recv1, acc1, recv2, acc2, recv3, gath, nrm_dp, nrm_cls,
                 ss, rs, s1, r1, s2, r2, s3, r3, sb, rb, sc, rc, g3s, g3r, g2s, g2r, g1s, g1r):
    n = nk * nx * nz
    me = lax.axis_index("dp")
    cj = lax.axis_index("class")
    kc = lax.rem(me, nk)
    xc = lax.rem(me // nk, nx)
    zc = me // (nk * nx)
    total = part_ref.shape[0]
    half = total // nk
    quarter = half // nx
    piece = quarter // nz

    def dev(z, x, k):
        return ((z * nx + x) * nk + k, cj)

    def rows(start, size):
        return pl.ds(pl.multiple_of(start, size), size)

    barrier = pltpu.get_barrier_semaphore()

    def greet(d, c):
        pl.semaphore_signal(barrier, 1, device_id=(lax.rem(me + d, n), cj), device_id_type=MESH)
        return c
    lax.fori_loop(1, n, greet, 0)
    for e in range(1, ncls):
        pl.semaphore_signal(barrier, 1, device_id=(me, lax.rem(cj + e, ncls)), device_id_type=MESH)
    pl.semaphore_wait(barrier, n - 1 + ncls - 1)

    c_peers = [lax.rem(cj + e, ncls) for e in range(1, ncls)]

    def st_desc(t, s):
        return pltpu.make_async_remote_copy(
            src_ref=stats_ref, dst_ref=sbuf.at[s], send_sem=ss.at[t], recv_sem=rs.at[s],
            device_id=(me, t), device_id_type=MESH)
    for t in c_peers:
        st_desc(t, cj).start()
    sbuf[cj] = stats_ref[...]
    for t in c_peers:
        st_desc(t, cj).wait_send()
        st_desc(cj, t).wait_recv()
    top = sbuf[0, 0:1, :]
    for e in range(1, ncls):
        top = jnp.maximum(top, sbuf[e, 0:1, :])
    tot_exp = sbuf[0, 1:2, :] * jnp.exp(sbuf[0, 0:1, :] - top)
    for e in range(1, ncls):
        tot_exp = tot_exp + sbuf[e, 1:2, :] * jnp.exp(sbuf[e, 0:1, :] - top)
    prob_t = jnp.exp(zt_ref[...] - top) / tot_exp
    diff_t = (qt_ref.shape[0] * ncls * (qt_ref[...] - prob_t)).astype(jnp.bfloat16)
    part_ref[...] = lax.dot_general(
        embt_ref[...], diff_t, (((1,), (1,)), ((), ())), preferred_element_type=jnp.float32)

    def exchange(peers, make):
        for p in peers:
            make(p, True).start()
        for p in peers:
            make(p, True).wait_send()
            make(p, False).wait_recv()

    k_peers = [lax.rem(kc + e, nk) for e in range(1, nk)]

    chunk = half // nch

    def m1(p, mine, c):
        part = rows(c * chunk, chunk)
        if mine:
            return pltpu.make_async_remote_copy(
                src_ref=part_ref.at[rows(p * half + c * chunk, chunk)], dst_ref=recv1.at[kc, part],
                send_sem=s1.at[p * nch + c], recv_sem=r1.at[kc * nch + c],
                device_id=dev(zc, xc, p), device_id_type=MESH)
        return pltpu.make_async_remote_copy(
            src_ref=part_ref.at[rows(kc * half + c * chunk, chunk)], dst_ref=recv1.at[p, part],
            send_sem=s1.at[kc * nch + c], recv_sem=r1.at[p * nch + c],
            device_id=dev(zc, xc, p), device_id_type=MESH)
    for p in k_peers:
        for c in range(nch):
            m1(p, True, c).start()
    for p in k_peers:
        for c in range(nch):
            m1(p, True, c).wait_send()
            m1(p, False, c).wait_recv()
    a1 = part_ref[rows(kc * half, half), :]
    for p in k_peers:
        a1 = a1 + recv1[p]
    acc1[...] = a1

    x_peers = [lax.rem(xc + e, nx) for e in sorted(range(1, nx), key=lambda e: -min(e, nx - e))]

    def m2(p, mine):
        if mine:
            return pltpu.make_async_remote_copy(
                src_ref=acc1.at[rows(p * quarter, quarter)], dst_ref=recv2.at[xc],
                send_sem=s2.at[p], recv_sem=r2.at[xc], device_id=dev(zc, p, kc), device_id_type=MESH)
        return pltpu.make_async_remote_copy(
            src_ref=acc1.at[rows(xc * quarter, quarter)], dst_ref=recv2.at[p],
            send_sem=s2.at[xc], recv_sem=r2.at[p], device_id=dev(zc, p, kc), device_id_type=MESH)
    exchange(x_peers, m2)
    a2 = acc1[rows(xc * quarter, quarter), :]
    for p in x_peers:
        a2 = a2 + recv2[p]
    acc2[...] = a2

    z_peers = [lax.rem(zc + e, nz) for e in sorted(range(1, nz), key=lambda e: -min(e, nz - e))]

    def m3(p, mine):
        if mine:
            return pltpu.make_async_remote_copy(
                src_ref=acc2.at[rows(p * piece, piece)], dst_ref=recv3.at[zc],
                send_sem=s3.at[p], recv_sem=r3.at[zc], device_id=dev(p, xc, kc), device_id_type=MESH)
        return pltpu.make_async_remote_copy(
            src_ref=acc2.at[rows(zc * piece, piece)], dst_ref=recv3.at[p],
            send_sem=s3.at[zc], recv_sem=r3.at[p], device_id=dev(p, xc, kc), device_id_type=MESH)
    exchange(z_peers, m3)
    a3 = acc2[rows(zc * piece, piece), :]
    for p in z_peers:
        a3 = a3 + recv3[p]
    summed = a3 * scale
    own = kc * half + xc * quarter + zc * piece
    gath[rows(own, piece), :] = summed.astype(gath.dtype)

    sq = jnp.sum(summed * summed, axis=(0, 1), keepdims=True)
    nrm_dp[me] = jnp.broadcast_to(sq, nrm_dp.shape[1:])

    def b_desc(t, s):
        return pltpu.make_async_remote_copy(
            src_ref=nrm_dp.at[s], dst_ref=nrm_dp.at[s],
            send_sem=sb.at[t], recv_sem=rb.at[s],
            device_id=(t, cj), device_id_type=MESH)

    def b_start(d, c):
        b_desc(lax.rem(me + d, n), me).start()
        return c
    lax.fori_loop(1, n, b_start, 0)

    def g3(p, mine):
        src = own if mine else kc * half + xc * quarter + p * piece
        return pltpu.make_async_remote_copy(
            src_ref=gath.at[rows(src, piece)], dst_ref=gath.at[rows(src, piece)],
            send_sem=g3s.at[p], recv_sem=g3r.at[zc if mine else p],
            device_id=dev(p, xc, kc), device_id_type=MESH)
    exchange(z_peers, g3)

    def g2(p, mine):
        src = kc * half + (xc if mine else p) * quarter
        return pltpu.make_async_remote_copy(
            src_ref=gath.at[rows(src, quarter)], dst_ref=gath.at[rows(src, quarter)],
            send_sem=g2s.at[p], recv_sem=g2r.at[xc if mine else p],
            device_id=dev(zc, p, kc), device_id_type=MESH)
    for p in x_peers:
        g2(p, True).start()

    def b_wait(d, c):
        b_desc(lax.rem(me + d, n), me).wait_send()
        b_desc(me, lax.rem(me + d, n)).wait_recv()
        return c
    lax.fori_loop(1, n, b_wait, 0)

    def b_add(d, acc):
        return acc + nrm_dp[lax.rem(me + d, n)]
    col = lax.fori_loop(1, n, b_add, nrm_dp[me])
    nrm_cls[cj] = col

    def c_desc(t, s):
        return pltpu.make_async_remote_copy(
            src_ref=nrm_cls.at[s], dst_ref=nrm_cls.at[s],
            send_sem=sc.at[t], recv_sem=rc.at[s],
            device_id=(me, t), device_id_type=MESH)

    for t in c_peers:
        c_desc(t, cj).start()
    for p in x_peers:
        g2(p, True).wait_send()
        g2(p, False).wait_recv()

    def g1(p, mine, c):
        src = (kc if mine else p) * half + c * chunk
        return pltpu.make_async_remote_copy(
            src_ref=gath.at[rows(src, chunk)], dst_ref=gath.at[rows(src, chunk)],
            send_sem=g1s.at[p * nch + c], recv_sem=g1r.at[(kc if mine else p) * nch + c],
            device_id=dev(zc, xc, p), device_id_type=MESH)
    for p in k_peers:
        for c in range(nch):
            g1(p, True, c).start()
    for t in c_peers:
        c_desc(t, cj).wait_send()
        c_desc(cj, t).wait_recv()
    tot = col
    for t in c_peers:
        tot = tot + nrm_cls[t]
    factor = jnp.minimum(1.0, limit / jnp.sqrt(tot))
    for p in k_peers:
        for c in range(nch):
            g1(p, True, c).wait_send()
            g1(p, False, c).wait_recv()
    fac = jnp.broadcast_to(factor[0:1, 0:1], out_ref.shape)
    out_ref[...] = (gath[...].astype(jnp.float32) * fac).astype(out_ref.dtype)


def grad_reduce(stats, z_t, q_t, emb_t, n, ncls, scale, limit, nk=2, nx=4, nch=4):
    nz = n // (nk * nx)
    width = z_t.shape[0]
    total = emb_t.shape[0]
    half = total // nk
    quarter = half // nx
    piece = quarter // nz
    dma = pltpu.SemaphoreType.DMA
    vmem = pl.BlockSpec(memory_space=pltpu.VMEM)
    return pl.pallas_call(
        functools.partial(_grad_kernel, nk, nx, nz, nch, ncls, scale, limit),
        out_shape=jax.ShapeDtypeStruct((total, width), jnp.bfloat16),
        in_specs=[vmem] * 4,
        out_specs=vmem,
        scratch_shapes=[
            pltpu.VMEM((total, width), jnp.float32),
            pltpu.VMEM((ncls,) + stats.shape, jnp.float32),
            pltpu.VMEM((nk, half, width), jnp.float32),
            pltpu.VMEM((half, width), jnp.float32),
            pltpu.VMEM((nx, quarter, width), jnp.float32),
            pltpu.VMEM((quarter, width), jnp.float32),
            pltpu.VMEM((nz, piece, width), jnp.float32),
            pltpu.VMEM((total, width), jnp.bfloat16),
            pltpu.VMEM((n, 8, 128), jnp.float32),
            pltpu.VMEM((ncls, 8, 128), jnp.float32),
            dma((ncls,)), dma((ncls,)),
            dma((nk * nch,)), dma((nk * nch,)), dma((nx,)), dma((nx,)), dma((nz,)), dma((nz,)),
            dma((n,)), dma((n,)), dma((ncls,)), dma((ncls,)),
            dma((nz,)), dma((nz,)), dma((nx,)), dma((nx,)), dma((nk * nch,)), dma((nk * nch,)),
        ],
        compiler_params=pltpu.CompilerParams(collective_id=0, has_side_effects=True),
    )(stats, z_t, q_t, emb_t)


def _class_gather_kernel(ncls, x_ref, out_ref, buf, ssem, rsem):
    me = lax.axis_index("dp")
    cj = lax.axis_index("class")
    peers = [lax.rem(cj + e, ncls) for e in range(1, ncls)]
    barrier = pltpu.get_barrier_semaphore()
    for t in peers:
        pl.semaphore_signal(barrier, 1, device_id=(me, t), device_id_type=MESH)
    pl.semaphore_wait(barrier, ncls - 1)

    def desc(t, s):
        return pltpu.make_async_remote_copy(
            src_ref=x_ref, dst_ref=buf.at[s], send_sem=ssem.at[t], recv_sem=rsem.at[s],
            device_id=(me, t), device_id_type=MESH)
    for t in peers:
        desc(t, cj).start()
    buf[cj] = x_ref[...]
    for t in peers:
        desc(t, cj).wait_send()
        desc(cj, t).wait_recv()
    out_ref[...] = buf[...]


def class_gather(x, ncls, cid):
    dma = pltpu.SemaphoreType.DMA
    return pl.pallas_call(
        functools.partial(_class_gather_kernel, ncls),
        out_shape=jax.ShapeDtypeStruct((ncls,) + x.shape, x.dtype),
        in_specs=[pl.BlockSpec(memory_space=pltpu.VMEM)],
        out_specs=pl.BlockSpec(memory_space=pltpu.VMEM),
        scratch_shapes=[pltpu.VMEM((ncls,) + x.shape, x.dtype), dma((ncls,)), dma((ncls,))],
        compiler_params=pltpu.CompilerParams(collective_id=cid, has_side_effects=True),
    )(x)


def _combine_stats(local_max, local_sum, cid):
    both = class_gather(jnp.stack([local_max, local_sum], axis=0), lax.axis_size("class"), cid)
    maxes, sums = both[:, 0], both[:, 1]
    top = jnp.max(maxes, axis=0)
    total = jnp.sum(sums * jnp.exp(maxes - top[None, :]), axis=0)
    return top, total


def on_device(embeddings, labels, head_weight, send_blocks, nbr_source, nbr_offset, counts):
    rows = embeddings.shape[0]
    width_part = embeddings.shape[1]
    class_part = labels.shape[1]
    dp_count = lax.axis_size("dp")
    nbrs = nbr_source.shape[1]
    picks = send_blocks[0]
    out_emb = embeddings.reshape(rows // BLOCK, BLOCK, width_part)[picks]
    out_lab = labels.reshape(rows // BLOCK, BLOCK, class_part)[picks]
    pool_emb = lax.all_to_all(out_emb, "dp", split_axis=0, concat_axis=0, tiled=True)
    pool_lab = lax.all_to_all(out_lab, "dp", split_axis=0, concat_axis=0, tiled=True)
    pool_rows = dp_count * BLOCK
    pool_emb = pool_emb.reshape(pool_rows, width_part)
    pool_lab = pool_lab.reshape(pool_rows, class_part)
    located = nbr_source * BLOCK + nbr_offset

    full_emb = lax.all_gather(embeddings, "class", axis=1, tiled=True)
    head = jnp.dot(full_emb, head_weight, preferred_element_type=jnp.float32)
    h_top, h_total = _combine_stats(
        jnp.max(head, axis=1),
        jnp.sum(jnp.exp(head - jnp.max(head, axis=1, keepdims=True)), axis=1),
        1,
    )
    prob_head = jnp.exp(head - h_top[:, None]) / h_total[:, None]

    near = pool_emb[located]
    partial_value = jnp.einsum(
        "rd,rkd->rk", embeddings, near, preferred_element_type=jnp.float32
    )
    scores = lax.psum(partial_value, "class")
    valid = lax.broadcasted_iota(jnp.int32, (rows, nbrs), 1) < counts[:, None]
    logits = jnp.where(valid, scores / math.sqrt(D), -1e30)
    top = jnp.max(logits, axis=1, keepdims=True)
    expd = jnp.where(valid, jnp.exp(logits - top), 0.0)
    weights = (expd / jnp.sum(expd, axis=1, keepdims=True)).astype(jnp.bfloat16)

    row_ids = lax.broadcasted_iota(jnp.int32, (rows, nbrs), 0)
    dense = jnp.zeros((rows, pool_rows), jnp.float32).at[row_ids, located].add(
        weights.astype(jnp.float32)
    )
    dense_hi = dense.astype(jnp.bfloat16)
    dense_lo = (dense - dense_hi.astype(jnp.float32)).astype(jnp.bfloat16)
    stacked = lax.optimization_barrier(jnp.concatenate([dense_hi, dense_lo], axis=0))
    both = jnp.dot(stacked, pool_lab, preferred_element_type=jnp.float32)
    spread = both[:rows] + both[rows:]
    target = 4.0 * spread + labels.astype(jnp.float32)
    z_local = jnp.max(target, axis=1)
    z_sum = jnp.sum(jnp.exp(target - z_local[:, None]), axis=1)
    scale = 1.0 / math.sqrt(rows * dp_count)
    limit = 0.5 * math.sqrt(D * C)
    head_grad = grad_reduce(
        jnp.stack([z_local, z_sum], axis=0), target.T, prob_head.T, full_emb.T,
        dp_count, lax.axis_size("class"), scale, limit,
    )
    return (target.astype(jnp.bfloat16), head_grad)


def solution(mesh):
    return jax.shard_map(
        on_device,
        mesh=mesh,
        in_specs=(
            P("dp", "class"),
            P("dp", "class"),
            P(None, "class"),
            P("dp", None),
            P("dp", None),
            P("dp", None),
            P("dp"),
        ),
        out_specs=(P("dp", "class"), P(None, "class")),
        check_vma=False,
    )
```
